256 devices in a mesh: grp: 8 (over y, core), dev: 32 (over x, z).
Axes of the slice: x: 4, y: 4, z: 8, core: 2. Of those that a mesh axis runs over, the one named last changes fastest.
Arguments:
- particle_pos: float32 [2, 4194304], P(None, ('grp', 'dev')), may hold values from -1 to 1
- particle_mass: float32 [4194304], P(('grp', 'dev')), may hold values from 0.02 to 0.2
- leaf_counts: int32 [65536], P(('grp', 'dev')), may hold values from 1 to 64, 3145728 in all
Outputs:
- lens_field: float32 [4, 4194304], P(None, ('grp', 'dev'))
The draws below stay inside these ranges and needn't reach their ends.
Inputs may be any that keep to these rules, and one draw needn't show every extreme that they name: `leaf_counts`: every leaf holds 1 to 64 live particles and some leaf exactly 64; the counts sum to 3145728.
All inputs are finite; a program needn't handle non-finite values. No bound on the sum of `leaf_counts` on one device may be relied on, other than what follows from the above.
Results may differ from the reference program's by a relative error of at most 0.0001.
Values sent between devices are 32-bit elements; how exact they have to be, the bound alone decides.
A program may use at most 192 MiB of HBM per device.

```python
import math
import jax
import jax.numpy as jnp
import numpy as np
from jax import lax

NODES = 6
PPL = 64
NLEAF = 65536
NPART = 4194304


def levels(key, extent, split, smallest, top_value):
    level, own = 1.0, jax.random.fold_in(key, 6)
    for axis_at, shards_of in split:
        draws = jnp.exp(jax.random.uniform(jax.random.fold_in(own, axis_at), (shards_of,), jnp.float32, smallest / len(split), top_value / len(split)))
        level = level * jnp.repeat(draws, extent[axis_at] // shards_of).reshape([-1 if axis == axis_at else 1 for axis in range(len(extent))])
    return level


def profile(number_of, total, limit, slope):
    loads = [(1 << 20) // math.isqrt(grade ** slope) + 1 for grade in range(2, number_of + 1)]
    spare, counts = total - limit - (number_of - 1), [1] * (number_of - 1)
    while spare > 0:
        candidates = [i for i in range(number_of - 1) if counts[i] < limit]
        whole, remaining = sum([loads[i] for i in candidates]), spare
        for i in candidates:
            addition = min(limit - counts[i], max(1, remaining * loads[i] // whole), spare)
            counts[i] = counts[i] + addition
            spare = spare - addition
    return np.array([limit] + counts)


def uneven(stream_key, number_of, total, limit, slope):
    if number_of == 2:
        one = jax.random.randint(stream_key, (), max(1, total - limit), min(limit, total - 1) + 1)
        return jnp.stack([one, total - one])
    lengths = jnp.asarray(profile(number_of, total, limit, slope), jnp.int32)
    couples = (number_of - 1) // 2
    donor, receiver = lengths[1:1 + 2 * couples:2], lengths[2:2 + 2 * couples:2]
    room = jnp.minimum(donor - 1, limit - receiver)
    moved = jax.random.randint(jax.random.fold_in(stream_key, 1), (couples,), 0, 1 << 20) % (room + 1)
    lengths = lengths.at[1:1 + 2 * couples:2].set(donor - moved).at[2:2 + 2 * couples:2].set(receiver + moved)
    return lengths[jax.random.permutation(jax.random.fold_in(stream_key, 2), number_of)]


def setup_inputs(seed: int = 0) -> dict:
    arg_keys = jax.random.split(jax.random.key(seed), 4)
    particle_pos = jnp.clip(jax.random.uniform(arg_keys[0], (2, NPART), jnp.float32, -1.0, 1.0) * levels(arg_keys[0], (2, NPART), ((1, 256),), -0.4, 0.0), -1.0, 1.0)
    particle_mass = jnp.clip(jnp.exp(math.log(0.2) - 2.3025851 * jax.random.uniform(arg_keys[1], (NPART,), jnp.float32) ** levels(arg_keys[1], (NPART,), ((0, 256),), -0.2, 0.2)), 0.02, 0.2)
    leaf_counts = uneven(arg_keys[2], NLEAF, 3 * PPL * NLEAF // 4, PPL, 0).astype(jnp.int32)
    return {"particle_pos": particle_pos, "particle_mass": particle_mass, "leaf_counts": leaf_counts}


SOFTEN = 0.01
PRECISE = lax.Precision.HIGHEST


def node_angles():
    return (2.0 * jnp.arange(NODES, dtype=jnp.float32) + 1.0) * (jnp.pi / (2.0 * NODES))


def cheb_points():
    return jnp.cos(node_angles())


def interp_basis(coords):
    angles = node_angles()
    expand = (slice(None),) + (None,) * coords.ndim
    result = jnp.zeros((NODES,) + coords.shape, jnp.float32) + 1.0 / NODES
    lower_poly = jnp.ones_like(coords)
    upper_poly = coords
    for degree in range(1, NODES):
        at_nodes = jnp.cos(degree * angles)
        result = result + (2.0 / NODES) * at_nodes[expand] * upper_poly[None]
        lower_poly, upper_poly = upper_poly, 2.0 * coords * upper_poly - lower_poly
    return result


def kernel_vals(delta_x, delta_y):
    inv_r2 = 1.0 / (delta_x * delta_x + delta_y * delta_y + SOFTEN)
    inv_sq = inv_r2 * inv_r2
    return (delta_x * inv_r2, delta_y * inv_r2, (delta_y * delta_y - delta_x * delta_x) * inv_sq, -2.0 * delta_x * delta_y * inv_sq)


def far_offsets():
    return [(off_x, off_y) for off_x in range(-3, 4) for off_y in range(-3, 4) if max(abs(off_x), abs(off_y)) >= 2]


def transfer_table(half_width, off_x, off_y):
    points = cheb_points()
    node_diff = points[:, None] - points[None, :]
    delta_x = half_width * node_diff[:, None, :, None] - 2.0 * half_width * off_x
    delta_y = half_width * node_diff[None, :, None, :] - 2.0 * half_width * off_y
    kernel_set = kernel_vals(delta_x, delta_y)
    stacked = jnp.stack([jnp.broadcast_to(term_val, (NODES, NODES, NODES, NODES)) for term_val in kernel_set])
    return stacked.reshape(4 * NODES * NODES, NODES * NODES)


def pair_mask(size_x, size_y, off_x, off_y):
    cells_x = jnp.arange(size_x, dtype=jnp.int32)
    cells_y = jnp.arange(size_y, dtype=jnp.int32)
    keep_x = jnp.abs((cells_x + off_x) // 2 - cells_x // 2) <= 1
    keep_y = jnp.abs((cells_y + off_y) // 2 - cells_y // 2) <= 1
    return (keep_x[:, None] & keep_y[None, :]).astype(jnp.float32)


def far_field(padded, size_x, size_y, half_width):
    result = jnp.zeros((4 * NODES * NODES, size_x * size_y), jnp.float32)
    for off_x, off_y in far_offsets():
        shifted = padded[:, 3 + off_x:3 + off_x + size_x, 3 + off_y:3 + off_y + size_y] * pair_mask(size_x, size_y, off_x, off_y)[None]
        result = result + jnp.dot(transfer_table(half_width, off_x, off_y), shifted.reshape(NODES * NODES, size_x * size_y), precision=PRECISE, preferred_element_type=jnp.float32)
    return result.reshape(4, NODES * NODES, size_x, size_y)


def child_table():
    points = cheb_points()
    sides = jnp.arange(2, dtype=jnp.float32)
    coords = -0.5 + sides[:, None] + 0.5 * points[None, :]
    per_side = jnp.transpose(interp_basis(coords), (1, 2, 0))
    product_table = per_side[:, None, :, None, :, None] * per_side[None, :, None, :, None, :]
    return product_table.reshape(2, 2, NODES * NODES, NODES * NODES)


def upward(leaf_grid):
    node_table = child_table()
    size_x = leaf_grid.shape[1] // 2
    size_y = leaf_grid.shape[2] // 2
    result = jnp.zeros((NODES * NODES, size_x * size_y), jnp.float32)
    for side_x in (0, 1):
        for side_y in (0, 1):
            child_part = leaf_grid[:, side_x::2, side_y::2].reshape(NODES * NODES, size_x * size_y)
            result = result + jnp.dot(node_table[side_x, side_y].T, child_part, precision=PRECISE, preferred_element_type=jnp.float32)
    return result.reshape(NODES * NODES, size_x, size_y)


def downward(parent_local):
    node_table = child_table()
    size_x = parent_local.shape[2]
    size_y = parent_local.shape[3]
    flat_local = jnp.transpose(parent_local, (1, 0, 2, 3)).reshape(NODES * NODES, 4 * size_x * size_y)
    row_list = []
    for side_x in (0, 1):
        col_list = []
        for side_y in (0, 1):
            child_part = jnp.dot(node_table[side_x, side_y], flat_local, precision=PRECISE, preferred_element_type=jnp.float32)
            col_list.append(child_part.reshape(NODES * NODES, 4, size_x, size_y))
        row_list.append(jnp.stack(col_list, axis=-1))
    stacked = jnp.stack(row_list, axis=3).reshape(NODES * NODES, 4, 2 * size_x, 2 * size_y)
    return jnp.transpose(stacked, (1, 0, 2, 3))


def moments(grid_u, grid_v, grid_w):
    basis_u = interp_basis(grid_u) * grid_w[None]
    basis_v = interp_basis(grid_v)
    result = jnp.einsum('axyp,bxyp->abxy', basis_u, basis_v, precision=PRECISE)
    return result.reshape(NODES * NODES, grid_u.shape[0], grid_u.shape[1])


def near_row(target_u, target_v, near_rows):
    size_y = target_u.shape[0]
    blocks = []
    shift_x = []
    shift_y = []
    for off_x in (-1, 0, 1):
        for off_y in (-1, 0, 1):
            blocks.append(near_rows[:, off_x + 1, off_y + 1:off_y + 1 + size_y, :])
            shift_x.append(jnp.full((PPL,), -off_x, jnp.float32))
            shift_y.append(jnp.full((PPL,), -off_y, jnp.float32))
    sources = jnp.concatenate(blocks, axis=2)
    delta_x = jnp.concatenate(shift_x)[None, None, :] + 0.5 * (target_u[:, :, None] - sources[0][:, None, :])
    delta_y = jnp.concatenate(shift_y)[None, None, :] + 0.5 * (target_v[:, :, None] - sources[1][:, None, :])
    weight = sources[2][:, None, :]
    return jnp.stack([jnp.sum(weight * term_val, axis=2) for term_val in kernel_vals(delta_x, delta_y)])


def evaluate_row(target_u, target_v, local_row, near_rows):
    basis_u = interp_basis(target_u)
    basis_v = interp_basis(target_v)
    coeffs = local_row.reshape(4, NODES, NODES, target_u.shape[0])
    half_sum = jnp.einsum('cabq,bqp->caqp', coeffs, basis_v, precision=PRECISE)
    far_part = jnp.sum(half_sum * basis_u[None], axis=1)
    return far_part + near_row(target_u, target_v, near_rows)


def leaves_to_grid(values, axis_pos, bit_count):
    x_bits = (bit_count + 1) // 2
    y_bits = bit_count // 2
    old_shape = values.shape
    split_vals = values.reshape(old_shape[:axis_pos] + (2,) * bit_count + old_shape[axis_pos + 1:])
    x_dims = [axis_pos + bit_count - 1 - 2 * bit_level for bit_level in range(x_bits - 1, -1, -1)]
    y_dims = [axis_pos + bit_count - 2 - 2 * bit_level for bit_level in range(y_bits - 1, -1, -1)]
    lead_dims = list(range(axis_pos))
    tail_dims = list(range(axis_pos + bit_count, split_vals.ndim))
    permuted = jnp.transpose(split_vals, lead_dims + x_dims + y_dims + tail_dims)
    return permuted.reshape(old_shape[:axis_pos] + (2 ** x_bits, 2 ** y_bits) + old_shape[axis_pos + 1:])


def grid_to_leaves(values, axis_pos, bit_count):
    x_bits = (bit_count + 1) // 2
    y_bits = bit_count // 2
    old_shape = values.shape
    split_vals = values.reshape(old_shape[:axis_pos] + (2,) * bit_count + old_shape[axis_pos + 2:])
    order_dims = []
    for bit_level in range(bit_count - 1, -1, -1):
        if bit_level % 2 == 0:
            order_dims.append(axis_pos + x_bits - 1 - bit_level // 2)
        else:
            order_dims.append(axis_pos + x_bits + y_bits - 1 - (bit_level - 1) // 2)
    lead_dims = list(range(axis_pos))
    tail_dims = list(range(axis_pos + bit_count, split_vals.ndim))
    permuted = jnp.transpose(split_vals, lead_dims + order_dims + tail_dims)
    return permuted.reshape(old_shape[:axis_pos] + (2 ** bit_count,) + old_shape[axis_pos + 2:])


def reference(particle_pos, particle_mass, leaf_counts):
    leaf_bits = NLEAF.bit_length() - 1
    live_mask = (jnp.arange(PPL, dtype=jnp.int32)[None, :] < leaf_counts[:, None]).astype(jnp.float32)
    mass_rows = particle_mass.reshape(NLEAF, PPL)
    mean_mass = jnp.sum(mass_rows * live_mask) / jnp.sum(live_mask)
    weights = (mass_rows - mean_mass) * live_mask
    positions = particle_pos.reshape(2, NLEAF, PPL)
    grid_u = leaves_to_grid(positions[0], 0, leaf_bits)
    grid_v = leaves_to_grid(positions[1], 0, leaf_bits)
    grid_w = leaves_to_grid(weights, 0, leaf_bits)
    size_x = grid_u.shape[0]
    size_y = grid_u.shape[1]
    leaf_moments = moments(grid_u, grid_v, grid_w)
    parent_moments = upward(leaf_moments)
    edge_pad = ((0, 0), (3, 3), (3, 3))
    parent_local = far_field(jnp.pad(parent_moments, edge_pad), size_x // 2, size_y // 2, 1.0)
    leaf_local = far_field(jnp.pad(leaf_moments, edge_pad), size_x, size_y, 0.5) + downward(parent_local)
    particles = jnp.pad(jnp.stack([grid_u, grid_v, grid_w]), ((0, 0), (1, 1), (1, 1), (0, 0)))

    def one_row(row_idx):
        near_rows = lax.dynamic_slice_in_dim(particles, row_idx, 3, 1)
        target_u = lax.dynamic_index_in_dim(grid_u, row_idx, 0, keepdims=False)
        target_v = lax.dynamic_index_in_dim(grid_v, row_idx, 0, keepdims=False)
        local_row = lax.dynamic_index_in_dim(leaf_local, row_idx, 2, keepdims=False)
        return evaluate_row(target_u, target_v, local_row, near_rows)

    fields = lax.map(one_row, jnp.arange(size_x, dtype=jnp.int32))
    fields = jnp.transpose(fields, (1, 0, 2, 3))
    return grid_to_leaves(fields, 1, leaf_bits).reshape(4, NPART)
```

```python
import functools

import jax
import jax.numpy as jnp
import numpy as np
from jax import lax
from jax.experimental import pallas as pl
from jax.experimental.pallas import tpu as pltpu
from jax.sharding import PartitionSpec as P

NODES = 6
PPL = 64
LSIDE = 16
SOFTEN = 0.01
NM = 40
HIGHEST = lax.Precision.HIGHEST
F32 = jnp.float32
BF16 = jnp.bfloat16

DIRS = ((-1, 0), (1, 0), (0, -1), (0, 1), (-1, -1), (1, -1), (-1, 1), (1, 1))
ROW_OF = (0, 16, 32, 48, 64, 72, 80, 88)
ROWS_IN = (16, 16, 16, 16, 8, 8, 8, 8)
HROWS = 128
LANES_OUT = 512
OFFS = tuple((ox, oy) for ox in (-1, 0, 1) for oy in (-1, 0, 1))


def gp_col(gx, gy):
    return (gx & 1) + 2 * (gy & 1) + 4 * (gx >> 1) + 8 * (gy >> 1)


def par_col(px, py):
    return (px & 1) * 32 + (py & 1) * 16 + gp_col(px >> 1, py >> 1)


def leaf_col(x, y):
    return (x & 1) * 128 + (y & 1) * 64 + par_col(x >> 1, y >> 1)


def halo_cells(side):
    cells = []
    for dx, dy in DIRS:
        ex = -1 if dx < 0 else side
        ey = -1 if dy < 0 else side
        if dy == 0:
            cells.append([(ex, j) for j in range(side)])
        elif dx == 0:
            cells.append([(j, ey) for j in range(side)])
        else:
            cells.append([(ex, ey)])
    return cells


def pick_rows(side, col, base, lanes):
    out = np.zeros((HROWS, lanes), np.float32)
    for d, cells in enumerate(halo_cells(side)):
        for j, (cx, cy) in enumerate(cells):
            out[ROW_OF[d] + base[d] + j, col(cx % side, cy % side)] = 1.0
    return out


PAR_BASE = (0,) * 8
GP_BASE = (8,) * 4 + (1,) * 4


def shift_index(side, col, base, own_at, halo_at):
    where = {}
    for x in range(side):
        for y in range(side):
            where[x, y] = own_at + col(x, y)
    for d, cells in enumerate(halo_cells(side)):
        for j, cell in enumerate(cells):
            where[cell] = halo_at + ROW_OF[d] + base[d] + j
    out = np.zeros((9, side * side), np.int32)
    for o, (ox, oy) in enumerate(OFFS):
        for x in range(side):
            for y in range(side):
                out[o, col(x, y)] = where[x + ox, y + oy]
    return out


def cheb(u):
    terms = [u * 0 + 1.0, u]
    for _ in range(NODES - 2):
        terms.append(2.0 * u * terms[-1] - terms[-2])
    return terms


ANGLES = (2.0 * np.arange(NODES) + 1.0) * np.pi / (2.0 * NODES)
POINTS = np.cos(ANGLES)
S_COEF = 2.0 / NODES * np.cos(np.arange(NODES)[:, None] * ANGLES[None, :])
S_COEF[0] = 1.0 / NODES


def basis(u):
    terms = cheb(u)
    out = []
    for k in range(NODES):
        total = S_COEF[0, k] + float(S_COEF[1, k]) * terms[1]
        for n in range(2, NODES):
            total = total + float(S_COEF[n, k]) * terms[n]
        out.append(total)
    return out


def child_table():
    side = []
    for s in (0, 1):
        side.append(np.stack(basis(s - 0.5 + POINTS / 2), axis=1))
    out = np.zeros((4, NM, NM), np.float32)
    for sx in (0, 1):
        for sy in (0, 1):
            prod = side[sx][:, None, :, None] * side[sy][None, :, None, :]
            out[2 * sx + sy, :36, :36] = prod.reshape(36, 36)
    return out


def cell_vectors():
    coord = np.zeros((2, 4, NM), np.float32)
    cell = np.zeros((2, 4, NM), np.float32)
    for sx in (0, 1):
        for sy in (0, 1):
            ch = 2 * sx + sy
            node = np.arange(36)
            coord[0, ch] = sx - 0.5
            coord[1, ch] = sy - 0.5
            coord[0, ch, :36] += 0.5 * POINTS[node // 6]
            coord[1, ch, :36] += 0.5 * POINTS[node % 6]
            cell[0, ch] = sx
            cell[1, ch] = sy
    return coord.reshape(2, 4 * NM), cell.reshape(2, 4 * NM)


def constants():
    c = {}
    c["sel_leaf"] = pick_rows(LSIDE, leaf_col, PAR_BASE, 256).astype(BF16)
    sel_par = pick_rows(LSIDE // 2, par_col, PAR_BASE, 64)
    sel_gp = pick_rows(LSIDE // 4, gp_col, GP_BASE, 64)
    c["sel_mom"] = np.concatenate([sel_par, sel_gp], axis=1).astype(BF16)
    table = child_table()
    c["up"] = np.transpose(table, (2, 0, 1)).reshape(NM, 4 * NM)
    c["down"] = table.reshape(4 * NM, NM)
    src = np.zeros((16, 256), np.int32)
    src[:9] = shift_index(LSIDE, leaf_col, PAR_BASE, 0, 256)
    c["src_leaf"] = src
    msrc = np.full((16, 128), -1, np.int32)
    msrc[:9, :64] = shift_index(LSIDE // 2, par_col, PAR_BASE, 0, 128)
    msrc[:9, 64:80] = shift_index(LSIDE // 4, gp_col, GP_BASE, 64, 128)
    c["src_mom"] = msrc
    coord, cell = cell_vectors()
    rows = np.zeros((160, 128), np.float32)
    rows[:, 0:2] = coord.T
    rows[:, 2:4] = cell.T
    c["t_rows"] = rows
    cols = np.zeros((8, 9, 160), np.float32)
    for o, (ox, oy) in enumerate(OFFS):
        cols[0, o] = coord[0] + 2 * ox
        cols[1, o] = coord[1] + 2 * oy
        cols[2, o] = cell[0] + 2 * ox
        cols[3, o] = cell[1] + 2 * oy
    c["t_cols"] = cols.reshape(8, 1440)
    sides = np.zeros((8, HROWS), np.float32)
    for d, (dx, dy) in enumerate(DIRS):
        sides[0, ROW_OF[d] : ROW_OF[d] + ROWS_IN[d]] = dx
        sides[1, ROW_OF[d] : ROW_OF[d] + ROWS_IN[d]] = dy
    c["sides"] = sides
    return c


CONST = constants()


def split2(x):
    hi = x.astype(BF16)
    return hi, (x - hi.astype(F32)).astype(BF16)


def split3(x):
    hi = x.astype(BF16)
    rest = x - hi.astype(F32)
    mid = rest.astype(BF16)
    return hi, mid, (rest - mid.astype(F32)).astype(BF16)


def nt_dot(a, b):
    return lax.dot_general(a, b, (((1,), (1,)), ((), ())), preferred_element_type=F32)


def tn_none(a, b):
    return lax.dot_general(a, b, (((1,), (0,)), ((), ())), preferred_element_type=F32)


def prep_kernel(pos, mass, count, sel_leaf, sel_mom, up, own, mom, send, part, leaf_mom):
    starts = [qx * 2 + qy * 4 + sy for sy in (0, 1) for qx in (0, 1) for qy in (0, 1)]

    def rows_of(ref, lead, step):
        return jnp.concatenate(
            [ref[pl.ds(lead + step * s, 16, stride=8 * step), :] for s in starts], axis=0
        )

    u_rows = rows_of(pos, 0, 2)
    v_rows = rows_of(pos, 1, 2)
    m_rows = rows_of(mass, 0, 1)
    counts = rows_of(count, 0, 1)
    lane = lax.broadcasted_iota(jnp.int32, (128, 128), 1)
    live = (lane % PPL).astype(F32) < counts
    m_rows = jnp.where(live, m_rows, 0.0)
    l_rows = jnp.where(live, 1.0, 0.0)
    row = lax.broadcasted_iota(jnp.int32, (8, 128), 0)
    part[...] = jnp.where(
        row == 0,
        jnp.sum(m_rows, axis=0, keepdims=True),
        jnp.where(row == 1, jnp.sum(l_rows, axis=0, keepdims=True), 0.0),
    )
    for k, vals in enumerate((u_rows, v_rows, m_rows)):
        turned = vals.T
        own[k * PPL : (k + 1) * PPL, 0:128] = turned[:PPL]
        own[k * PPL : (k + 1) * PPL, 128:256] = turned[PPL:]
    leaf_mom[...] = jnp.zeros_like(leaf_mom)
    for tile in (0, 1):
        lanes = slice(tile * 128, tile * 128 + 128)
        bu = basis(own[0:64, lanes])
        bv = basis(own[64:128, lanes])
        m_t = own[128:192, lanes]
        live_t = jnp.where(m_t > 0.0, 1.0, 0.0)
        for kind, weight in enumerate((m_t, live_t)):
            for a in range(NODES):
                wa = bu[a] * weight
                for b in range(NODES):
                    leaf_mom[pl.ds(kind * NM + a * 6 + b, 1), lanes] = jnp.sum(
                        wa * bv[b], axis=0, keepdims=True
                    )
    mom[...] = jnp.zeros_like(mom)
    stacked = []
    for kind in (0, 1):
        block = jnp.concatenate(
            [
                leaf_mom[kind * NM : (kind + 1) * NM, ch * 64 : ch * 64 + 64]
                for ch in range(4)
            ],
            axis=0,
        )
        mom[kind * 160 : kind * 160 + 160, 0:64] = block
        stacked.append(block)
    par = jnp.dot(
        up[...], jnp.concatenate(stacked, axis=1), precision=HIGHEST, preferred_element_type=F32
    )
    for kind in (0, 1):
        for q in range(4):
            at = kind * 64 + q * 16
            mom[pl.ds(kind * 160 + q * NM, NM), 64:80] = par[:, at : at + 16]
    send[:, 0:192] = nt_dot(
        jnp.concatenate([sel_leaf[...]] * 3, axis=1),
        jnp.concatenate(split3(own[...]), axis=1),
    )
    send[:, 192:512] = nt_dot(
        jnp.concatenate([sel_mom[...]] * 3, axis=1),
        jnp.concatenate(split3(mom[...]), axis=1),
    )


def morton_split(code, bits):
    cx, cy = 0, 0
    for level in range((bits + 1) // 2):
        cx = cx + code // 4**level % 2 * 2**level
        cy = cy + code // (2 * 4**level) % 2 * 2**level
    return cx, cy


def morton_join(cx, cy, bits):
    code = 0
    for level in range((bits + 1) // 2):
        code = code + cx // 2**level % 2 * 4**level
        code = code + cy // 2**level % 2 * 2 * 4**level
    return code


def comm_kernel(dev_count, bits, send, part, recv, total, first, second, mid, sems_s, sems_r,
                sum_s1, sum_r1, sum_s2, sum_r2):
    code = lax.axis_index("grp") * dev_count + lax.axis_index("dev")
    bx, by = morton_split(code, bits)
    nx, ny = 2 ** ((bits + 1) // 2), 2 ** (bits // 2)
    low_n = 2 ** (bits // 2)
    high_n = 2**bits // low_n
    low, high = code % low_n, code // low_n

    def device(c):
        return {"grp": c // dev_count, "dev": c % dev_count}

    def beside(dx, dy):
        return device(morton_join((bx + dx + nx) % nx, (by + dy + ny) % ny, bits))

    barrier = pltpu.get_barrier_semaphore()
    for dx, dy in DIRS:
        pl.semaphore_signal(
            barrier, inc=1, device_id=beside(dx, dy), device_id_type=pl.DeviceIdType.MESH
        )

    def in_low(k):
        return device(high * low_n + (low + k) % low_n)

    def in_high(k):
        return device((high + k) % high_n * low_n + low)

    def greet_low(k, carry):
        pl.semaphore_signal(
            barrier, inc=1, device_id=in_low(k), device_id_type=pl.DeviceIdType.MESH
        )
        return carry

    def greet_high(k, carry):
        pl.semaphore_signal(
            barrier, inc=1, device_id=in_high(k), device_id_type=pl.DeviceIdType.MESH
        )
        return carry

    lax.fori_loop(1, low_n, greet_low, 0)
    lax.fori_loop(1, high_n, greet_high, 0)
    pl.semaphore_wait(barrier, 8 + low_n - 1 + high_n - 1)

    def low_copy(k):
        return pltpu.make_async_remote_copy(
            src_ref=part, dst_ref=first.at[k], send_sem=sum_s1.at[k], recv_sem=sum_r1.at[k],
            device_id=in_low(k), device_id_type=pl.DeviceIdType.MESH,
        )

    def high_copy(k):
        return pltpu.make_async_remote_copy(
            src_ref=mid, dst_ref=second.at[k], send_sem=sum_s2.at[k], recv_sem=sum_r2.at[k],
            device_id=in_high(k), device_id_type=pl.DeviceIdType.MESH,
        )

    def start_low(k, carry):
        low_copy(k).start()
        return carry

    def start_high(k, carry):
        high_copy(k).start()
        return carry

    lax.fori_loop(1, low_n, start_low, 0)
    edges = []
    for d, (dx, dy) in enumerate(DIRS):
        rows = pl.ds(ROW_OF[d], ROWS_IN[d])
        copy = pltpu.make_async_remote_copy(
            src_ref=send.at[rows], dst_ref=recv.at[rows], send_sem=sems_s.at[d],
            recv_sem=sems_r.at[d], device_id=beside(-dx, -dy),
            device_id_type=pl.DeviceIdType.MESH,
        )
        copy.start()
        edges.append(copy)

    def add_low(k, acc):
        low_copy(k).wait()
        return acc + first[k]

    def add_high(k, acc):
        high_copy(k).wait()
        return acc + second[k]

    mid[...] = lax.fori_loop(1, low_n, add_low, part[...])
    lax.fori_loop(1, high_n, start_high, 0)
    recv[96:HROWS, :] = jnp.zeros((HROWS - 96, LANES_OUT), F32)
    total[...] = lax.fori_loop(1, high_n, add_high, mid[...])
    for copy in edges:
        copy.wait()


def main_kernel(dev_count, bits, own, mom, recv, total, sides, src_leaf, src_mom, down, t_rows,
                t_cols, out, su, sv, sw, xs, table_hi, table_lo, leaf_local, result):
    code = lax.axis_index("grp") * dev_count + lax.axis_index("dev")
    bx, by = morton_split(code, bits)
    nx, ny = 2 ** ((bits + 1) // 2), 2 ** (bits // 2)
    sums = total[...]
    mass_sum = jnp.sum(sums[0:1], axis=1, keepdims=True)
    live_sum = jnp.sum(sums[1:2], axis=1, keepdims=True)
    mean = mass_sum / live_sum
    side_x = sides[0:1]
    side_y = sides[1:2]
    cell_x = side_x + jnp.full((1, 128), bx, jnp.int32).astype(F32)
    cell_y = side_y + jnp.full((1, 128), by, jnp.int32).astype(F32)
    inside = jnp.where(
        (cell_x >= 0.0) & (cell_x < float(nx)) & (cell_y >= 0.0) & (cell_y < float(ny)), 1.0, 0.0
    )
    halo = recv[...].T * inside

    both = jnp.concatenate([own[...], halo[0:192]], axis=1)
    m_all = both[128:192]
    weight = jnp.where(m_all > 0.0, m_all - mean, 0.0)
    sources = jnp.concatenate([both[0:128] * 0.5, weight], axis=0)
    cut = jnp.concatenate(split3(sources), axis=0)
    row384 = lax.broadcasted_iota(jnp.int32, (384, 256), 0)

    def shift_sources(o, carry):
        pick = jnp.where(row384 == src_leaf[pl.ds(o, 1), :], 1.0, 0.0).astype(BF16)
        moved = tn_none(cut, pick)
        moved = moved[0:192] + moved[192:384] + moved[384:576]
        off_x = (o // 3 - 1).astype(F32)
        off_y = (o % 3 - 1).astype(F32)
        at = pl.ds(pl.multiple_of(o * PPL, PPL), PPL)
        for tile in (0, 1):
            lanes = slice(tile * 128, tile * 128 + 128)
            su[tile, at, :] = moved[0:64, lanes] + off_x
            sv[tile, at, :] = moved[64:128, lanes] + off_y
            sw[tile, at, :] = moved[128:192, lanes]
        return carry

    lax.fori_loop(0, 9, shift_sources, 0)

    all_mom = jnp.concatenate([mom[...], halo[192:512]], axis=1)
    all_mom = all_mom[0:160] - mean * all_mom[160:320]
    cut_mom = jnp.concatenate(split2(all_mom), axis=0)
    row256 = lax.broadcasted_iota(jnp.int32, (256, 128), 0)

    def shift_moments(o, carry):
        pick = jnp.where(row256 == src_mom[pl.ds(o, 1), :], 1.0, 0.0).astype(BF16)
        moved = tn_none(cut_mom, pick).astype(BF16)
        at = pl.ds(pl.multiple_of(o * 160, 32), 160)
        xs[at, 0:128] = moved[0:160]
        xs[at, 128:256] = moved[160:320]
        return carry

    lax.fori_loop(0, 9, shift_moments, 0)

    def far(scale):
        def fill(i, carry):
            at = pl.multiple_of(i * 16, 16)
            rows = t_rows[pl.ds(at, 16), :]
            dx = (rows[:, 0:1] - t_cols[0:1, :]) * scale
            dy = (rows[:, 1:2] - t_cols[1:2, :]) * scale
            gap = jnp.maximum(
                jnp.abs(rows[:, 2:3] - t_cols[2:3, :]), jnp.abs(rows[:, 3:4] - t_cols[3:4, :])
            )
            x2 = dx * dx
            y2 = dy * dy
            inv = jnp.where(gap > 1.5, 1.0 / (x2 + y2 + SOFTEN), 0.0)
            inv_sq = inv * inv
            for c, val in enumerate(
                (dx * inv, dy * inv, (y2 - x2) * inv_sq, -2.0 * dx * dy * inv_sq)
            ):
                hi, lo = split2(val)
                table_hi[pl.ds(c * 160 + at, 16), :] = hi
                table_lo[pl.ds(c * 160 + at, 16), :] = lo
            return carry

        lax.fori_loop(0, 10, fill, 0)
        wide = tn_none(table_hi[...], xs[...])
        return wide[:, 0:128] + wide[:, 128:256] + tn_none(table_lo[...], xs[:, 0:128])

    par = far(2.0)
    par_cols = jnp.concatenate(
        [
            jnp.concatenate(
                [par[c * 160 + q * NM : c * 160 + q * NM + NM, 64:80] for q in range(4)], axis=1
            )
            for c in range(4)
        ],
        axis=1,
    )
    from_par = jnp.dot(
        down[...], par_cols, precision=HIGHEST, preferred_element_type=F32
    )
    leaf = far(1.0)
    for c in range(4):
        leaf_local[c] = jnp.concatenate(
            [
                leaf[c * 160 + ch * NM : c * 160 + ch * NM + NM, 0:64]
                + from_par[ch * NM : ch * NM + NM, c * 64 : c * 64 + 64]
                for ch in range(4)
            ],
            axis=1,
        )

    for tile in (0, 1):
        lanes = slice(tile * 128, tile * 128 + 128)
        bu = basis(own[0:64, lanes])
        bv = basis(own[64:128, lanes])
        for c in range(4):
            acc = None
            for a in range(NODES):
                half = leaf_local[c, pl.ds(a * 6, 1), lanes] * bv[0]
                for b in range(1, NODES):
                    half = half + leaf_local[c, pl.ds(a * 6 + b, 1), lanes] * bv[b]
                acc = half * bu[a] if acc is None else acc + half * bu[a]
            result[c, tile * PPL : tile * PPL + PPL, :] = acc

    width, unroll = 4, 4
    for tile in (0, 1):
        lanes = slice(tile * 128, tile * 128 + 128)
        for part in range(PPL // (8 * width)):
            base = part * 8 * width
            tx = [own[base + 8 * i : base + 8 * i + 8, lanes] * 0.5 for i in range(width)]
            ty = [own[64 + base + 8 * i : 72 + base + 8 * i, lanes] * 0.5 for i in range(width)]

            def pairs(step, acc):
                acc = list(acc)
                for i in range(unroll):
                    at = pl.ds(step * unroll + i, 8, stride=0)
                    sx, sy, w = su[tile, at, :], sv[tile, at, :], sw[tile, at, :]
                    for t in range(width):
                        dx = tx[t] - sx
                        dy = ty[t] - sy
                        x2 = dx * dx
                        y2 = dy * dy
                        inv = 1.0 / (x2 + y2 + SOFTEN)
                        w1 = w * inv
                        w2 = w1 * inv
                        acc[4 * t] = acc[4 * t] + w1 * dx
                        acc[4 * t + 1] = acc[4 * t + 1] + w1 * dy
                        acc[4 * t + 2] = acc[4 * t + 2] + w2 * (y2 - x2)
                        acc[4 * t + 3] = acc[4 * t + 3] + w2 * (dx * dy)
                return tuple(acc)

            zero = jnp.zeros((8, 128), F32)
            acc = lax.fori_loop(0, 9 * PPL // unroll, pairs, (zero,) * (4 * width))
            for t in range(width):
                rows = slice(tile * PPL + base + 8 * t, tile * PPL + base + 8 * t + 8)
                for c in range(4):
                    near = acc[4 * t + c]
                    if c == 3:
                        near = near * -2.0
                    result[c, rows, :] = result[c, rows, :] + near

    starts = [qx * 2 + qy * 4 + sy for sy in (0, 1) for qx in (0, 1) for qy in (0, 1)]
    for c in range(4):
        turned = result[c].T
        for i, s in enumerate(starts):
            out[pl.ds(s * 4 + c, 16, stride=32), :] = turned[16 * i : 16 * i + 16]


def vmem():
    return pl.BlockSpec(memory_space=pltpu.VMEM)


def on_device(particle_pos, particle_mass, leaf_counts):
    dev_count = lax.axis_size("dev")
    bits = (lax.axis_size("grp") * dev_count).bit_length() - 1
    low_n = 2 ** (bits // 2)
    high_n = 2**bits // low_n
    pos = particle_pos.reshape(2, 128, 128).transpose(1, 0, 2).reshape(256, 128)
    mass = particle_mass.reshape(128, 128)
    count = jnp.broadcast_to(
        leaf_counts.astype(F32).reshape(128, 2, 1), (128, 2, PPL)
    ).reshape(128, 128)
    c = {k: jnp.asarray(v) for k, v in CONST.items()}
    f32 = functools.partial(jax.ShapeDtypeStruct, dtype=F32)
    own, mom, send, part = pl.pallas_call(
        prep_kernel,
        out_shape=(f32((192, 256)), f32((320, 128)), f32((HROWS, LANES_OUT)), f32((8, 128))),
        in_specs=[vmem()] * 6,
        out_specs=(vmem(),) * 4,
        scratch_shapes=[pltpu.VMEM((2 * NM, 256), F32)],
        name="prep",
    )(pos, mass, count, c["sel_leaf"], c["sel_mom"], c["up"])
    recv, total = pl.pallas_call(
        functools.partial(comm_kernel, dev_count, bits),
        out_shape=(f32((HROWS, LANES_OUT)), f32((8, 128))),
        in_specs=[vmem()] * 2,
        out_specs=(vmem(),) * 2,
        scratch_shapes=[
            pltpu.VMEM((low_n, 8, 128), F32),
            pltpu.VMEM((high_n, 8, 128), F32),
            pltpu.VMEM((8, 128), F32),
            pltpu.SemaphoreType.DMA((8,)),
            pltpu.SemaphoreType.DMA((8,)),
            pltpu.SemaphoreType.DMA((low_n,)),
            pltpu.SemaphoreType.DMA((low_n,)),
            pltpu.SemaphoreType.DMA((high_n,)),
            pltpu.SemaphoreType.DMA((high_n,)),
        ],
        compiler_params=pltpu.CompilerParams(collective_id=0, has_side_effects=True),
        name="comm",
    )(send, part)
    out = pl.pallas_call(
        functools.partial(main_kernel, dev_count, bits),
        out_shape=f32((512, 128)),
        in_specs=[vmem()] * 10,
        out_specs=vmem(),
        scratch_shapes=[
            pltpu.VMEM((2, 9 * PPL, 128), F32),
            pltpu.VMEM((2, 9 * PPL, 128), F32),
            pltpu.VMEM((2, 9 * PPL, 128), F32),
            pltpu.VMEM((1440, 256), BF16),
            pltpu.VMEM((640, 1440), BF16),
            pltpu.VMEM((640, 1440), BF16),
            pltpu.VMEM((4, NM, 256), F32),
            pltpu.VMEM((4, 128, 128), F32),
        ],
        compiler_params=pltpu.CompilerParams(vmem_limit_bytes=48 * 2**20),
        name="fields",
    )(own, mom, recv, total, c["sides"], c["src_leaf"], c["src_mom"], c["down"], c["t_rows"],
      c["t_cols"])
    return out.reshape(128, 4, 128).transpose(1, 0, 2).reshape(4, LSIDE * LSIDE * PPL)


def solution(mesh):
    in_specs = (P(None, ("grp", "dev")), P(("grp", "dev")), P(("grp", "dev")))
    out_specs = P(None, ("grp", "dev"))
    return jax.shard_map(
        on_device, mesh=mesh, in_specs=in_specs, out_specs=out_specs, check_vma=False
    )
```

```python
import functools

import jax
import jax.numpy as jnp
import numpy as np
from jax import lax
from jax.experimental import pallas as pl
from jax.experimental.pallas import tpu as pltpu
from jax.sharding import PartitionSpec as P

NODES = 6
PPL = 64
LSIDE = 16
SOFTEN = 0.01
NM = 40
HIGHEST = lax.Precision.HIGHEST
F32 = jnp.float32
BF16 = jnp.bfloat16

DIRS = ((-1, 0), (1, 0), (0, -1), (0, 1), (-1, -1), (1, -1), (-1, 1), (1, 1))
ROW_OF = (0, 16, 32, 48, 64, 72, 80, 88)
ROWS_IN = (16, 16, 16, 16, 8, 8, 8, 8)
HROWS = 128
LANES_OUT = 512
OFFS = tuple((ox, oy) for ox in (-1, 0, 1) for oy in (-1, 0, 1) if (ox, oy) != (0, 0)) + ((0, 0),)
NEIGHBOURS = 8


def gp_col(gx, gy):
    return (gx & 1) + 2 * (gy & 1) + 4 * (gx >> 1) + 8 * (gy >> 1)


def par_col(px, py):
    return (px & 1) * 32 + (py & 1) * 16 + gp_col(px >> 1, py >> 1)


def leaf_col(x, y):
    return (x & 1) * 128 + (y & 1) * 64 + par_col(x >> 1, y >> 1)


def halo_cells(side):
    cells = []
    for dx, dy in DIRS:
        ex = -1 if dx < 0 else side
        ey = -1 if dy < 0 else side
        if dy == 0:
            cells.append([(ex, j) for j in range(side)])
        elif dx == 0:
            cells.append([(j, ey) for j in range(side)])
        else:
            cells.append([(ex, ey)])
    return cells


def pick_rows(side, col, base, lanes):
    out = np.zeros((HROWS, lanes), np.float32)
    for d, cells in enumerate(halo_cells(side)):
        for j, (cx, cy) in enumerate(cells):
            out[ROW_OF[d] + base[d] + j, col(cx % side, cy % side)] = 1.0
    return out


PAR_BASE = (0,) * 8
GP_BASE = (8,) * 4 + (1,) * 4


def shift_index(side, col, base, own_at, halo_at):
    where = {}
    for x in range(side):
        for y in range(side):
            where[x, y] = own_at + col(x, y)
    for d, cells in enumerate(halo_cells(side)):
        for j, cell in enumerate(cells):
            where[cell] = halo_at + ROW_OF[d] + base[d] + j
    out = np.zeros((9, side * side), np.int32)
    for o, (ox, oy) in enumerate(OFFS):
        for x in range(side):
            for y in range(side):
                out[o, col(x, y)] = where[x + ox, y + oy]
    return out


def cheb(u):
    terms = [u * 0 + 1.0, u]
    for _ in range(NODES - 2):
        terms.append(2.0 * u * terms[-1] - terms[-2])
    return terms


ANGLES = (2.0 * np.arange(NODES) + 1.0) * np.pi / (2.0 * NODES)
POINTS = np.cos(ANGLES)
S_COEF = 2.0 / NODES * np.cos(np.arange(NODES)[:, None] * ANGLES[None, :])
S_COEF[0] = 1.0 / NODES


def basis(u):
    terms = cheb(u)
    out = []
    for k in range(NODES):
        total = S_COEF[0, k] + float(S_COEF[1, k]) * terms[1]
        for n in range(2, NODES):
            total = total + float(S_COEF[n, k]) * terms[n]
        out.append(total)
    return out


def child_table():
    side = []
    for s in (0, 1):
        side.append(np.stack(basis(s - 0.5 + POINTS / 2), axis=1))
    out = np.zeros((4, NM, NM), np.float32)
    for sx in (0, 1):
        for sy in (0, 1):
            prod = side[sx][:, None, :, None] * side[sy][None, :, None, :]
            out[2 * sx + sy, :36, :36] = prod.reshape(36, 36)
    return out


def cell_vectors():
    coord = np.zeros((2, 4, NM), np.float32)
    cell = np.zeros((2, 4, NM), np.float32)
    for sx in (0, 1):
        for sy in (0, 1):
            ch = 2 * sx + sy
            node = np.arange(36)
            coord[0, ch] = sx - 0.5
            coord[1, ch] = sy - 0.5
            coord[0, ch, :36] += 0.5 * POINTS[node // 6]
            coord[1, ch, :36] += 0.5 * POINTS[node % 6]
            cell[0, ch] = sx
            cell[1, ch] = sy
    return coord.reshape(2, 4 * NM), cell.reshape(2, 4 * NM)


def constants():
    c = {}
    c["sel_leaf"] = pick_rows(LSIDE, leaf_col, PAR_BASE, 256).astype(BF16)
    sel_par = pick_rows(LSIDE // 2, par_col, PAR_BASE, 64)
    sel_gp = pick_rows(LSIDE // 4, gp_col, GP_BASE, 64)
    c["sel_mom"] = np.concatenate([sel_par, sel_gp], axis=1).astype(BF16)
    table = child_table()
    c["up"] = np.transpose(table, (2, 0, 1)).reshape(NM, 4 * NM)
    c["down"] = table.reshape(4 * NM, NM)
    src = np.zeros((16, 256), np.int32)
    src[:9] = shift_index(LSIDE, leaf_col, PAR_BASE, 0, 256)
    for x in range(LSIDE):
        for y in range(LSIDE):
            src[9, leaf_col(x, y)] = sum(
                (x >> k & 1) << 2 * k | (y >> k & 1) << 2 * k + 1 for k in range(4)
            )
    c["src_leaf"] = src
    msrc = np.full((16, 128), -1, np.int32)
    msrc[:9, :64] = shift_index(LSIDE // 2, par_col, PAR_BASE, 0, 128)
    msrc[:9, 64:80] = shift_index(LSIDE // 4, gp_col, GP_BASE, 64, 128)
    c["src_mom"] = msrc
    coord, cell = cell_vectors()
    rows = np.zeros((160, 128), np.float32)
    rows[:, 0:2] = coord.T
    rows[:, 2:4] = cell.T
    c["t_rows"] = rows
    cols = np.zeros((8, 9, 160), np.float32)
    for o, (ox, oy) in enumerate(OFFS):
        cols[0, o] = coord[0] + 2 * ox
        cols[1, o] = coord[1] + 2 * oy
        cols[2, o] = cell[0] + 2 * ox
        cols[3, o] = cell[1] + 2 * oy
    c["t_cols"] = cols.reshape(8, 1440)
    sides = np.zeros((8, HROWS), np.float32)
    for d, (dx, dy) in enumerate(DIRS):
        sides[0, ROW_OF[d] : ROW_OF[d] + ROWS_IN[d]] = dx
        sides[1, ROW_OF[d] : ROW_OF[d] + ROWS_IN[d]] = dy
    c["sides"] = sides
    return c


CONST = constants()


def split2(x):
    hi = x.astype(BF16)
    return hi, (x - hi.astype(F32)).astype(BF16)


def split3(x):
    hi = x.astype(BF16)
    rest = x - hi.astype(F32)
    mid = rest.astype(BF16)
    return hi, mid, (rest - mid.astype(F32)).astype(BF16)


def nt_dot(a, b):
    return lax.dot_general(a, b, (((1,), (1,)), ((), ())), preferred_element_type=F32)


def tn_none(a, b):
    return lax.dot_general(a, b, (((1,), (0,)), ((), ())), preferred_element_type=F32)


def morton_split(code, bits):
    cx, cy = 0, 0
    for level in range((bits + 1) // 2):
        cx = cx + code // 4**level % 2 * 2**level
        cy = cy + code // (2 * 4**level) % 2 * 2**level
    return cx, cy


def morton_join(cx, cy, bits):
    code = 0
    for level in range((bits + 1) // 2):
        code = code + cx // 2**level % 2 * 4**level
        code = code + cy // 2**level % 2 * 2 * 4**level
    return code


def whole_kernel(dev_count, bits, *refs):
    sources, refs = refs[:OPERANDS], refs[OPERANDS:]
    out, refs = refs[0], refs[1:]
    held, refs = refs[:OPERANDS], refs[OPERANDS:]
    (pos, mass, count, src_leaf, sel_leaf, sel_mom, up, t_rows, t_cols, sides, src_mom,
     down) = held
    arrive_sems = refs[0]
    arrivals = [
        pltpu.make_async_copy(src, dst, arrive_sems.at[i])
        for i, (src, dst) in enumerate(zip(sources, held))
    ]
    for arrival in arrivals:
        arrival.start()
    run_kernel(dev_count, bits, arrivals, pos, mass, count, sel_leaf, sel_mom, up, down, sides,
               src_leaf, src_mom, t_rows, t_cols, out, *refs[1:])


def run_kernel(dev_count, bits, arrivals, pos, mass, count, sel_leaf, sel_mom, up, down, sides,
               src_leaf, src_mom, t_rows, t_cols, out, own, mom, send, recv, part, mid, leaf_mom, first,
                 second, su, sv, sw, lone, xs, hi_leaf, lo_leaf, hi_par, lo_par, leaf_local,
                 result, self_live, edge_s, edge_r, sum_s1, sum_r1, sum_s2, sum_r2):
    code = lax.axis_index("grp") * dev_count + lax.axis_index("dev")
    bx, by = morton_split(code, bits)
    nx, ny = 2 ** ((bits + 1) // 2), 2 ** (bits // 2)
    low_n = 2 ** (bits // 2)
    high_n = 2**bits // low_n
    low, high = code % low_n, code // low_n

    def device(c):
        return {"grp": c // dev_count, "dev": c % dev_count}

    def beside(dx, dy):
        return device(morton_join((bx + dx + nx) % nx, (by + dy + ny) % ny, bits))

    def in_low(k):
        return device(high * low_n + (low + k) % low_n)

    def in_high(k):
        return device((high + k) % high_n * low_n + low)

    barrier = pltpu.get_barrier_semaphore()

    def greet(who):
        pl.semaphore_signal(barrier, inc=1, device_id=who, device_id_type=pl.DeviceIdType.MESH)

    def greet_low(k, carry):
        greet(in_low(k))
        return carry

    def greet_high(k, carry):
        greet(in_high(k))
        return carry

    lax.fori_loop(1, low_n, greet_low, 0)
    for dx, dy in DIRS:
        greet(beside(dx, dy))
    lax.fori_loop(1, high_n, greet_high, 0)

    starts = [qx * 2 + qy * 4 + sy for sy in (0, 1) for qx in (0, 1) for qy in (0, 1)]

    def turned(ref, lead, step):
        rows = jnp.concatenate(
            [ref[pl.ds(lead + step * s, 16, stride=8 * step), :] for s in starts], axis=0
        )
        return rows.T

    for arrival in arrivals[:4]:
        arrival.wait()
    row256 = lax.broadcasted_iota(jnp.int32, (256, 256), 0)
    pick = jnp.where(row256 == src_leaf[9:10, :], 1.0, 0.0).astype(BF16)
    linear = count[...].astype(F32).astype(BF16)
    counts = tn_none(linear[0:1], pick[0:128]) + tn_none(linear[1:2], pick[128:256])
    m_turned = turned(mass, 0, 1)
    slot = lax.broadcasted_iota(jnp.int32, (PPL, 128), 0).astype(F32)
    totals = []
    for tile in (0, 1):
        lanes = slice(tile * 128, tile * 128 + 128)
        live = slot < counts[:, lanes]
        vals = jnp.where(live, m_turned[tile * PPL : tile * PPL + PPL], 0.0)
        own[128:192, lanes] = vals
        totals.append(jnp.sum(vals, axis=0, keepdims=True))
    row = lax.broadcasted_iota(jnp.int32, (8, 128), 0)
    part[...] = jnp.where(
        row == 0,
        totals[0] + totals[1],
        jnp.where(row == 1, counts[:, 0:128] + counts[:, 128:256], 0.0),
    )
    for k in (0, 1):
        vals = turned(pos, k, 2)
        own[k * PPL : (k + 1) * PPL, 0:128] = vals[:PPL]
        own[k * PPL : (k + 1) * PPL, 128:256] = vals[PPL:]

    def low_copy(k):
        return pltpu.make_async_remote_copy(
            src_ref=part, dst_ref=first.at[k], send_sem=sum_s1.at[k], recv_sem=sum_r1.at[k],
            device_id=in_low(k), device_id_type=pl.DeviceIdType.MESH,
        )

    def high_copy(k):
        return pltpu.make_async_remote_copy(
            src_ref=mid, dst_ref=second.at[k], send_sem=sum_s2.at[k], recv_sem=sum_r2.at[k],
            device_id=in_high(k), device_id_type=pl.DeviceIdType.MESH,
        )

    def start_low(k, carry):
        low_copy(k).start()
        return carry

    def start_high(k, carry):
        high_copy(k).start()
        return carry

    def add_low(k, acc):
        low_copy(k).wait()
        return acc + first[k]

    def add_high(k, acc):
        high_copy(k).wait()
        return acc + second[k]

    pl.semaphore_wait(barrier, 8 + low_n - 1 + high_n - 1)
    lax.fori_loop(1, low_n, start_low, 0)

    for arrival in arrivals[4:]:
        arrival.wait()
    leaf_mom[...] = jnp.zeros_like(leaf_mom)
    for tile in (0, 1):
        lanes = slice(tile * 128, tile * 128 + 128)
        bu = basis(own[0:64, lanes])
        bv = basis(own[64:128, lanes])
        m_t = own[128:192, lanes]
        live_t = jnp.where(m_t > 0.0, 1.0, 0.0)
        lone[tile, 0:PPL, :] = live_t
        for kind, weight in enumerate((m_t, live_t)):
            for a in range(NODES):
                wa = bu[a] * weight
                for b in range(NODES):
                    leaf_mom[pl.ds(kind * NM + a * 6 + b, 1), lanes] = jnp.sum(
                        wa * bv[b], axis=0, keepdims=True
                    )
    mom[...] = jnp.zeros_like(mom)
    stacked = []
    for kind in (0, 1):
        block = jnp.concatenate(
            [
                leaf_mom[kind * NM : (kind + 1) * NM, ch * 64 : ch * 64 + 64]
                for ch in range(4)
            ],
            axis=0,
        )
        mom[kind * 160 : kind * 160 + 160, 0:64] = block
        stacked.append(block)
    par = jnp.dot(
        up[...], jnp.concatenate(stacked, axis=1), precision=HIGHEST, preferred_element_type=F32
    )
    for kind in (0, 1):
        for q in range(4):
            at = kind * 64 + q * 16
            mom[pl.ds(kind * 160 + q * NM, NM), 64:80] = par[:, at : at + 16]
    own_cut = split3(own[...])
    send[:, 0:192] = nt_dot(
        jnp.concatenate([sel_leaf[...]] * 3, axis=1), jnp.concatenate(own_cut, axis=1)
    )
    send[:, 192:512] = nt_dot(
        jnp.concatenate([sel_mom[...]] * 3, axis=1),
        jnp.concatenate(split3(mom[...]), axis=1),
    )
    edges = []
    for d, (dx, dy) in enumerate(DIRS):
        rows = pl.ds(ROW_OF[d], ROWS_IN[d])
        copy = pltpu.make_async_remote_copy(
            src_ref=send.at[rows], dst_ref=recv.at[rows], send_sem=edge_s.at[d],
            recv_sem=edge_r.at[d], device_id=beside(-dx, -dy),
            device_id_type=pl.DeviceIdType.MESH,
        )
        copy.start()
        edges.append(copy)
    recv[96:HROWS, :] = jnp.zeros((HROWS - 96, LANES_OUT), F32)

    def fill_tables(scale, table_hi, table_lo):
        def fill(i, carry):
            at = pl.multiple_of(i * 16, 16)
            rows = t_rows[pl.ds(at, 16), :]
            dx = (rows[:, 0:1] - t_cols[0:1, :]) * scale
            dy = (rows[:, 1:2] - t_cols[1:2, :]) * scale
            gap = jnp.maximum(
                jnp.abs(rows[:, 2:3] - t_cols[2:3, :]), jnp.abs(rows[:, 3:4] - t_cols[3:4, :])
            )
            x2 = dx * dx
            y2 = dy * dy
            inv = jnp.where(gap > 1.5, 1.0 / (x2 + y2 + SOFTEN), 0.0)
            inv_sq = inv * inv
            for c, val in enumerate(
                (dx * inv, dy * inv, (y2 - x2) * inv_sq, -2.0 * dx * dy * inv_sq)
            ):
                hi, lo = split2(val)
                table_hi[pl.ds(c * 160 + at, 16), :] = hi
                table_lo[pl.ds(c * 160 + at, 16), :] = lo
            return carry

        lax.fori_loop(0, 10, fill, 0)

    fill_tables(2.0, hi_par, lo_par)
    mid[...] = lax.fori_loop(1, low_n, add_low, part[...])
    lax.fori_loop(1, high_n, start_high, 0)
    fill_tables(1.0, hi_leaf, lo_leaf)

    def at_offset(o):
        return pl.ds(pl.multiple_of(o * PPL, PPL), PPL)

    own_rows = jnp.concatenate(own_cut, axis=0)

    def shift_own(o, carry):
        hot = jnp.where(row256 == src_leaf[pl.ds(o, 1), :], 1.0, 0.0).astype(BF16)
        moved = tn_none(own_rows, hot)
        moved = moved[0:192] + moved[192:384] + moved[384:576]
        for tile in (0, 1):
            lanes = slice(tile * 128, tile * 128 + 128)
            su[tile, at_offset(o), :] = moved[0:64, lanes]
            sv[tile, at_offset(o), :] = moved[64:128, lanes]
            sw[tile, at_offset(o), :] = moved[128:192, lanes]
        return carry

    lax.fori_loop(0, NEIGHBOURS, shift_own, 0)
    self_at = NEIGHBOURS * PPL
    for tile in (0, 1):
        lanes = slice(tile * 128, tile * 128 + 128)
        su[tile, self_at : self_at + PPL, :] = own[0:64, lanes] * 0.5
        sv[tile, self_at : self_at + PPL, :] = own[64:128, lanes] * 0.5
        sw[tile, self_at : self_at + PPL, :] = own[128:192, lanes]

    zero = jnp.zeros((8, 128), F32)

    def targets(tile, base, width):
        lanes = slice(tile * 128, tile * 128 + 128)
        tx = [own[base + 8 * i : base + 8 * i + 8, lanes] * 0.5 for i in range(width)]
        ty = [own[64 + base + 8 * i : 72 + base + 8 * i, lanes] * 0.5 for i in range(width)]
        return tx, ty

    self_width = 2
    for tile in (0, 1):
        for piece in range(PPL // (8 * self_width)):
            base = piece * 8 * self_width
            tx, ty = targets(tile, base, self_width)

            def self_pairs(step, acc, tile=tile, tx=tx, ty=ty):
                acc = list(acc)
                for i in range(4):
                    k = step * 4 + i
                    at = pl.ds(self_at + k, 8, stride=0)
                    sx, sy, m = su[tile, at, :], sv[tile, at, :], sw[tile, at, :]
                    one = lone[tile, pl.ds(k, 8, stride=0), :]
                    for t in range(self_width):
                        dx = tx[t] - sx
                        dy = ty[t] - sy
                        x2 = dx * dx
                        y2 = dy * dy
                        inv = 1.0 / (x2 + y2 + SOFTEN)
                        gap = y2 - x2
                        cross = dx * dy
                        for kind, w in enumerate((m, one)):
                            at_acc = 8 * t + 4 * kind
                            w1 = w * inv
                            w2 = w1 * inv
                            acc[at_acc] = acc[at_acc] + w1 * dx
                            acc[at_acc + 1] = acc[at_acc + 1] + w1 * dy
                            acc[at_acc + 2] = acc[at_acc + 2] + w2 * gap
                            acc[at_acc + 3] = acc[at_acc + 3] + w2 * cross
                return tuple(acc)

            acc = lax.fori_loop(0, PPL // 4, self_pairs, (zero,) * (8 * self_width))
            for t in range(self_width):
                rows = slice(tile * PPL + base + 8 * t, tile * PPL + base + 8 * t + 8)
                for c in range(4):
                    scale = -2.0 if c == 3 else 1.0
                    result[c, rows, :] = acc[8 * t + c] * scale
                    self_live[c, rows, :] = acc[8 * t + 4 + c] * scale

    sums = lax.fori_loop(1, high_n, add_high, mid[...])
    mass_sum = jnp.sum(sums[0:1], axis=1, keepdims=True)
    live_sum = jnp.sum(sums[1:2], axis=1, keepdims=True)
    mean = mass_sum / live_sum
    for copy in edges:
        copy.wait()
    cell_x = sides[0:1] + jnp.full((1, 128), bx, jnp.int32).astype(F32)
    cell_y = sides[1:2] + jnp.full((1, 128), by, jnp.int32).astype(F32)
    inside = jnp.where(
        (cell_x >= 0.0) & (cell_x < float(nx)) & (cell_y >= 0.0) & (cell_y < float(ny)), 1.0, 0.0
    )
    halo = recv[...].T * inside
    halo_rows = jnp.concatenate(split3(halo[0:192]), axis=0)
    row128 = lax.broadcasted_iota(jnp.int32, (128, 256), 0) + 256

    def shift_halo(o, carry):
        hot = jnp.where(row128 == src_leaf[pl.ds(o, 1), :], 1.0, 0.0).astype(BF16)
        moved = tn_none(halo_rows, hot)
        moved = moved[0:192] + moved[192:384] + moved[384:576]
        skip = o + (o >= 4).astype(jnp.int32)
        off_x = (skip // 3 - 1).astype(F32)
        off_y = (skip % 3 - 1).astype(F32)
        for tile in (0, 1):
            lanes = slice(tile * 128, tile * 128 + 128)
            at = at_offset(o)
            su[tile, at, :] = (su[tile, at, :] + moved[0:64, lanes]) * 0.5 + off_x
            sv[tile, at, :] = (sv[tile, at, :] + moved[64:128, lanes]) * 0.5 + off_y
            m = sw[tile, at, :] + moved[128:192, lanes]
            sw[tile, at, :] = jnp.where(m > 0.0, m - mean, 0.0)
        return carry

    lax.fori_loop(0, NEIGHBOURS, shift_halo, 0)

    all_mom = jnp.concatenate([mom[...], halo[192:512]], axis=1)
    all_mom = all_mom[0:160] - mean * all_mom[160:320]
    cut_mom = jnp.concatenate(split2(all_mom), axis=0)

    def shift_moments(o, carry):
        hot = jnp.where(row256[:, 0:128] == src_mom[pl.ds(o, 1), :], 1.0, 0.0).astype(BF16)
        moved = tn_none(cut_mom, hot).astype(BF16)
        at = pl.ds(pl.multiple_of(o * 160, 32), 160)
        xs[at, 0:128] = moved[0:160]
        xs[at, 128:256] = moved[160:320]
        return carry

    lax.fori_loop(0, 9, shift_moments, 0)

    def far(table_hi, table_lo):
        wide = tn_none(table_hi[...], xs[...])
        return wide[:, 0:128] + wide[:, 128:256] + tn_none(table_lo[...], xs[:, 0:128])

    par = far(hi_par, lo_par)
    par_cols = jnp.concatenate(
        [
            jnp.concatenate(
                [par[c * 160 + q * NM : c * 160 + q * NM + NM, 64:80] for q in range(4)], axis=1
            )
            for c in range(4)
        ],
        axis=1,
    )
    from_par = jnp.dot(
        down[...], par_cols, precision=HIGHEST, preferred_element_type=F32
    )
    leaf = far(hi_leaf, lo_leaf)
    for c in range(4):
        leaf_local[c] = jnp.concatenate(
            [
                leaf[c * 160 + ch * NM : c * 160 + ch * NM + NM, 0:64]
                + from_par[ch * NM : ch * NM + NM, c * 64 : c * 64 + 64]
                for ch in range(4)
            ],
            axis=1,
        )

    for tile in (0, 1):
        lanes = slice(tile * 128, tile * 128 + 128)
        bu = basis(own[0:64, lanes])
        bv = basis(own[64:128, lanes])
        for c in range(4):
            rows = slice(tile * PPL, tile * PPL + PPL)
            acc = result[c, rows, :] - mean * self_live[c, rows, :]
            for a in range(NODES):
                half = leaf_local[c, pl.ds(a * 6, 1), lanes] * bv[0]
                for b in range(1, NODES):
                    half = half + leaf_local[c, pl.ds(a * 6 + b, 1), lanes] * bv[b]
                acc = acc + half * bu[a]
            result[c, rows, :] = acc

    width, unroll = 4, 8
    for tile in (0, 1):
        for piece in range(PPL // (8 * width)):
            base = piece * 8 * width
            tx, ty = targets(tile, base, width)

            def pairs(step, acc, tile=tile, tx=tx, ty=ty):
                acc = list(acc)
                for i in range(unroll):
                    at = pl.ds(step * unroll + i, 8, stride=0)
                    sx, sy, w = su[tile, at, :], sv[tile, at, :], sw[tile, at, :]
                    for t in range(width):
                        dx = tx[t] - sx
                        dy = ty[t] - sy
                        x2 = dx * dx
                        y2 = dy * dy
                        inv = 1.0 / (x2 + y2 + SOFTEN)
                        w1 = w * inv
                        w2 = w1 * inv
                        acc[4 * t] = acc[4 * t] + w1 * dx
                        acc[4 * t + 1] = acc[4 * t + 1] + w1 * dy
                        acc[4 * t + 2] = acc[4 * t + 2] + w2 * (y2 - x2)
                        acc[4 * t + 3] = acc[4 * t + 3] + w2 * (dx * dy)
                return tuple(acc)

            acc = lax.fori_loop(0, NEIGHBOURS * PPL // unroll, pairs, (zero,) * (4 * width))
            for t in range(width):
                rows = slice(tile * PPL + base + 8 * t, tile * PPL + base + 8 * t + 8)
                for c in range(4):
                    near = acc[4 * t + c]
                    if c == 3:
                        near = near * -2.0
                    result[c, rows, :] = result[c, rows, :] + near

    for c in range(4):
        back = result[c].T
        for i, s in enumerate(starts):
            out[pl.ds(s * 4 + c, 16, stride=32), :] = back[16 * i : 16 * i + 16]


def vmem():
    return pl.BlockSpec(memory_space=pltpu.VMEM)


NAMES = ("src_leaf", "sel_leaf", "sel_mom", "up", "t_rows", "t_cols", "sides", "src_mom", "down")
OPERANDS = 3 + len(NAMES)


def on_device(particle_pos, particle_mass, leaf_counts):
    dev_count = lax.axis_size("dev")
    bits = (lax.axis_size("grp") * dev_count).bit_length() - 1
    low_n = 2 ** (bits // 2)
    high_n = 2**bits // low_n
    pos = particle_pos.reshape(2, 128, 128).transpose(1, 0, 2).reshape(256, 128)
    mass = particle_mass.reshape(128, 128)
    count = leaf_counts.reshape(2, 128)
    operands = (pos, mass, count, *[jnp.asarray(CONST[k]) for k in NAMES])
    out = pl.pallas_call(
        functools.partial(whole_kernel, dev_count, bits),
        out_shape=jax.ShapeDtypeStruct((512, 128), F32),
        in_specs=[pl.BlockSpec(memory_space=pltpu.HBM)] * OPERANDS,
        out_specs=vmem(),
        scratch_shapes=[pltpu.VMEM(x.shape, x.dtype) for x in operands]
        + [
            pltpu.SemaphoreType.DMA((OPERANDS,)),
            pltpu.VMEM((192, 256), F32),
            pltpu.VMEM((320, 128), F32),
            pltpu.VMEM((HROWS, LANES_OUT), F32),
            pltpu.VMEM((HROWS, LANES_OUT), F32),
            pltpu.VMEM((8, 128), F32),
            pltpu.VMEM((8, 128), F32),
            pltpu.VMEM((2 * NM, 256), F32),
            pltpu.VMEM((low_n, 8, 128), F32),
            pltpu.VMEM((high_n, 8, 128), F32),
            pltpu.VMEM((2, 9 * PPL + 8, 128), F32),
            pltpu.VMEM((2, 9 * PPL + 8, 128), F32),
            pltpu.VMEM((2, 9 * PPL + 8, 128), F32),
            pltpu.VMEM((2, PPL + 8, 128), F32),
            pltpu.VMEM((1440, 256), BF16),
            pltpu.VMEM((640, 1440), BF16),
            pltpu.VMEM((640, 1440), BF16),
            pltpu.VMEM((640, 1440), BF16),
            pltpu.VMEM((640, 1440), BF16),
            pltpu.VMEM((4, NM, 256), F32),
            pltpu.VMEM((4, 128, 128), F32),
            pltpu.VMEM((4, 128, 128), F32),
            pltpu.SemaphoreType.DMA((8,)),
            pltpu.SemaphoreType.DMA((8,)),
            pltpu.SemaphoreType.DMA((low_n,)),
            pltpu.SemaphoreType.DMA((low_n,)),
            pltpu.SemaphoreType.DMA((high_n,)),
            pltpu.SemaphoreType.DMA((high_n,)),
        ],
        compiler_params=pltpu.CompilerParams(
            collective_id=0, has_side_effects=True, vmem_limit_bytes=63 * 2**20
        ),
        name="fields",
    )(*operands)
    return out.reshape(128, 4, 128).transpose(1, 0, 2).reshape(4, LSIDE * LSIDE * PPL)


def solution(mesh):
    in_specs = (P(None, ("grp", "dev")), P(("grp", "dev")), P(("grp", "dev")))
    out_specs = P(None, ("grp", "dev"))
    return jax.shard_map(
        on_device, mesh=mesh, in_specs=in_specs, out_specs=out_specs, check_vma=False
    )
```

```python
import functools

import jax
import jax.numpy as jnp
import numpy as np
from jax import lax
from jax.experimental import pallas as pl
from jax.experimental.pallas import tpu as pltpu
from jax.sharding import PartitionSpec as P

NODES = 6
PPL = 64
LSIDE = 16
SOFTEN = 0.01
NM = 40
HIGHEST = lax.Precision.HIGHEST
F32 = jnp.float32
BF16 = jnp.bfloat16

DIRS = ((-1, 0), (1, 0), (0, -1), (0, 1), (-1, -1), (1, -1), (-1, 1), (1, 1))
ROW_OF = (0, 16, 32, 48, 64, 72, 80, 88)
ROWS_IN = (16, 16, 16, 16, 8, 8, 8, 8)
HROWS = 128
LANES_OUT = 512
OFFS = tuple((ox, oy) for ox in (-1, 0, 1) for oy in (-1, 0, 1) if (ox, oy) != (0, 0)) + ((0, 0),)
NEIGHBOURS = 8
FILL_LANES = 256


def gp_col(gx, gy):
    return (gx & 1) + 2 * (gy & 1) + 4 * (gx >> 1) + 8 * (gy >> 1)


def par_col(px, py):
    return (px & 1) * 32 + (py & 1) * 16 + gp_col(px >> 1, py >> 1)


def leaf_col(x, y):
    return (x & 1) * 128 + (y & 1) * 64 + par_col(x >> 1, y >> 1)


def halo_cells(side):
    cells = []
    for dx, dy in DIRS:
        ex = -1 if dx < 0 else side
        ey = -1 if dy < 0 else side
        if dy == 0:
            cells.append([(ex, j) for j in range(side)])
        elif dx == 0:
            cells.append([(j, ey) for j in range(side)])
        else:
            cells.append([(ex, ey)])
    return cells


def pick_rows(side, col, base, lanes):
    out = np.zeros((HROWS, lanes), np.float32)
    for d, cells in enumerate(halo_cells(side)):
        for j, (cx, cy) in enumerate(cells):
            out[ROW_OF[d] + base[d] + j, col(cx % side, cy % side)] = 1.0
    return out


PAR_BASE = (0,) * 8
GP_BASE = (8,) * 4 + (1,) * 4


def shift_index(side, col, base, own_at, halo_at):
    where = {}
    for x in range(side):
        for y in range(side):
            where[x, y] = own_at + col(x, y)
    for d, cells in enumerate(halo_cells(side)):
        for j, cell in enumerate(cells):
            where[cell] = halo_at + ROW_OF[d] + base[d] + j
    out = np.zeros((9, side * side), np.int32)
    for o, (ox, oy) in enumerate(OFFS):
        for x in range(side):
            for y in range(side):
                out[o, col(x, y)] = where[x + ox, y + oy]
    return out


def cheb(u):
    terms = [u * 0 + 1.0, u]
    for _ in range(NODES - 2):
        terms.append(2.0 * u * terms[-1] - terms[-2])
    return terms


ANGLES = (2.0 * np.arange(NODES) + 1.0) * np.pi / (2.0 * NODES)
POINTS = np.cos(ANGLES)
S_COEF = 2.0 / NODES * np.cos(np.arange(NODES)[:, None] * ANGLES[None, :])
S_COEF[0] = 1.0 / NODES


def basis(u):
    terms = cheb(u)
    out = []
    for k in range(NODES):
        total = S_COEF[0, k] + float(S_COEF[1, k]) * terms[1]
        for n in range(2, NODES):
            total = total + float(S_COEF[n, k]) * terms[n]
        out.append(total)
    return out


def child_table():
    side = []
    for s in (0, 1):
        side.append(np.stack(basis(s - 0.5 + POINTS / 2), axis=1))
    out = np.zeros((4, NM, NM), np.float32)
    for sx in (0, 1):
        for sy in (0, 1):
            prod = side[sx][:, None, :, None] * side[sy][None, :, None, :]
            out[2 * sx + sy, :36, :36] = prod.reshape(36, 36)
    return out


def cell_vectors():
    coord = np.zeros((2, 4, NM), np.float32)
    cell = np.zeros((2, 4, NM), np.float32)
    for sx in (0, 1):
        for sy in (0, 1):
            ch = 2 * sx + sy
            node = np.arange(36)
            coord[0, ch] = sx - 0.5
            coord[1, ch] = sy - 0.5
            coord[0, ch, :36] += 0.5 * POINTS[node // 6]
            coord[1, ch, :36] += 0.5 * POINTS[node % 6]
            cell[0, ch] = sx
            cell[1, ch] = sy
    return coord.reshape(2, 4 * NM), cell.reshape(2, 4 * NM)


def constants():
    c = {}
    c["sel_leaf"] = pick_rows(LSIDE, leaf_col, PAR_BASE, 256).astype(BF16)
    sel_par = pick_rows(LSIDE // 2, par_col, PAR_BASE, 64)
    sel_gp = pick_rows(LSIDE // 4, gp_col, GP_BASE, 64)
    c["sel_mom"] = np.concatenate([sel_par, sel_gp], axis=1).astype(BF16)
    table = child_table()
    c["up"] = np.transpose(table, (2, 0, 1)).reshape(NM, 4 * NM)
    c["down"] = table.reshape(4 * NM, NM)
    src = np.zeros((16, 256), np.int32)
    src[:9] = shift_index(LSIDE, leaf_col, PAR_BASE, 0, 256)
    for x in range(LSIDE):
        for y in range(LSIDE):
            src[9, leaf_col(x, y)] = sum(
                (x >> k & 1) << 2 * k | (y >> k & 1) << 2 * k + 1 for k in range(4)
            )
    c["src_leaf"] = src
    msrc = np.full((16, 128), -1, np.int32)
    msrc[:9, :64] = shift_index(LSIDE // 2, par_col, PAR_BASE, 0, 128)
    msrc[:9, 64:80] = shift_index(LSIDE // 4, gp_col, GP_BASE, 64, 128)
    c["src_mom"] = msrc
    coord, cell = cell_vectors()
    rows = np.zeros((160, 128), np.float32)
    rows[:, 0:2] = coord.T
    rows[:, 2:4] = cell.T
    c["t_rows"] = rows
    cols = np.zeros((8, 9, 160), np.float32)
    for o, (ox, oy) in enumerate(OFFS):
        cols[0, o] = coord[0] + 2 * ox
        cols[1, o] = coord[1] + 2 * oy
        cols[2, o] = cell[0] + 2 * ox
        cols[3, o] = cell[1] + 2 * oy
    c["t_cols"] = cols.reshape(8, 1440)
    sides = np.zeros((8, HROWS), np.float32)
    for d, (dx, dy) in enumerate(DIRS):
        sides[0, ROW_OF[d] : ROW_OF[d] + ROWS_IN[d]] = dx
        sides[1, ROW_OF[d] : ROW_OF[d] + ROWS_IN[d]] = dy
    c["sides"] = sides
    return c


CONST = constants()


def split2(x):
    hi = x.astype(BF16)
    return hi, (x - hi.astype(F32)).astype(BF16)


def split3(x):
    hi = x.astype(BF16)
    rest = x - hi.astype(F32)
    mid = rest.astype(BF16)
    return hi, mid, (rest - mid.astype(F32)).astype(BF16)


def nt_dot(a, b):
    return lax.dot_general(a, b, (((1,), (1,)), ((), ())), preferred_element_type=F32)


def tn_none(a, b):
    return lax.dot_general(a, b, (((1,), (0,)), ((), ())), preferred_element_type=F32)


def morton_split(code, bits):
    cx, cy = 0, 0
    for level in range((bits + 1) // 2):
        cx = cx + code // 4**level % 2 * 2**level
        cy = cy + code // (2 * 4**level) % 2 * 2**level
    return cx, cy


def morton_join(cx, cy, bits):
    code = 0
    for level in range((bits + 1) // 2):
        code = code + cx // 2**level % 2 * 4**level
        code = code + cy // 2**level % 2 * 2 * 4**level
    return code


def whole_kernel(dev_count, bits, *refs):
    sources, refs = refs[:OPERANDS], refs[OPERANDS:]
    out, refs = refs[0], refs[1:]
    held, refs = refs[:OPERANDS], refs[OPERANDS:]
    (pos, mass, count, src_leaf, sel_leaf, sel_mom, up, t_rows, t_cols, sides, src_mom,
     down) = held
    arrive_sems = refs[0]
    arrivals = [
        pltpu.make_async_copy(src, dst, arrive_sems.at[i])
        for i, (src, dst) in enumerate(zip(sources, held))
    ]
    for arrival in arrivals:
        arrival.start()
    run_kernel(dev_count, bits, arrivals, pos, mass, count, sel_leaf, sel_mom, up, down, sides,
               src_leaf, src_mom, t_rows, t_cols, out, *refs[1:])


def run_kernel(dev_count, bits, arrivals, pos, mass, count, sel_leaf, sel_mom, up, down, sides,
               src_leaf, src_mom, t_rows, t_cols, out, own, mom, send, recv, part, mid, leaf_mom, first,
                 second, su, sv, sw, lone, xs, hi_leaf, lo_leaf, hi_par, lo_par, leaf_local,
                 result, self_live, edge_s, edge_r, sum_s1, sum_r1, sum_s2, sum_r2):
    code = lax.axis_index("grp") * dev_count + lax.axis_index("dev")
    bx, by = morton_split(code, bits)
    nx, ny = 2 ** ((bits + 1) // 2), 2 ** (bits // 2)
    low_n = 2 ** (bits // 2)
    high_n = 2**bits // low_n
    low, high = code % low_n, code // low_n

    def device(c):
        return {"grp": c // dev_count, "dev": c % dev_count}

    def beside(dx, dy):
        return device(morton_join((bx + dx + nx) % nx, (by + dy + ny) % ny, bits))

    def in_low(k):
        return device(high * low_n + (low + k) % low_n)

    def in_high(k):
        return device((high + k) % high_n * low_n + low)

    barrier = pltpu.get_barrier_semaphore()

    def greet(who):
        pl.semaphore_signal(barrier, inc=1, device_id=who, device_id_type=pl.DeviceIdType.MESH)

    def greet_low(k, carry):
        greet(in_low(k))
        return carry

    def greet_high(k, carry):
        greet(in_high(k))
        return carry

    lax.fori_loop(1, low_n, greet_low, 0)
    for dx, dy in DIRS:
        greet(beside(dx, dy))
    lax.fori_loop(1, high_n, greet_high, 0)

    starts = [qx * 2 + qy * 4 + sy for sy in (0, 1) for qx in (0, 1) for qy in (0, 1)]

    def turned(ref, lead, step):
        rows = jnp.concatenate(
            [ref[pl.ds(lead + step * s, 16, stride=8 * step), :] for s in starts], axis=0
        )
        return rows.T

    for arrival in arrivals[:4]:
        arrival.wait()
    row256 = lax.broadcasted_iota(jnp.int32, (256, 256), 0)
    pick = jnp.where(row256 == src_leaf[9:10, :], 1.0, 0.0).astype(BF16)
    linear = count[...].astype(F32).astype(BF16)
    counts = tn_none(linear[0:1], pick[0:128]) + tn_none(linear[1:2], pick[128:256])
    m_turned = turned(mass, 0, 1)
    slot = lax.broadcasted_iota(jnp.int32, (PPL, 128), 0).astype(F32)
    totals = []
    for tile in (0, 1):
        lanes = slice(tile * 128, tile * 128 + 128)
        live = slot < counts[:, lanes]
        vals = jnp.where(live, m_turned[tile * PPL : tile * PPL + PPL], 0.0)
        own[128:192, lanes] = vals
        totals.append(jnp.sum(vals, axis=0, keepdims=True))
    row = lax.broadcasted_iota(jnp.int32, (8, 128), 0)
    part[...] = jnp.where(
        row == 0,
        totals[0] + totals[1],
        jnp.where(row == 1, counts[:, 0:128] + counts[:, 128:256], 0.0),
    )
    for k in (0, 1):
        vals = turned(pos, k, 2)
        own[k * PPL : (k + 1) * PPL, 0:128] = vals[:PPL]
        own[k * PPL : (k + 1) * PPL, 128:256] = vals[PPL:]

    def low_copy(k):
        return pltpu.make_async_remote_copy(
            src_ref=part, dst_ref=first.at[k], send_sem=sum_s1.at[k], recv_sem=sum_r1.at[k],
            device_id=in_low(k), device_id_type=pl.DeviceIdType.MESH,
        )

    def high_copy(k):
        return pltpu.make_async_remote_copy(
            src_ref=mid, dst_ref=second.at[k], send_sem=sum_s2.at[k], recv_sem=sum_r2.at[k],
            device_id=in_high(k), device_id_type=pl.DeviceIdType.MESH,
        )

    def start_low(k, carry):
        low_copy(k).start()
        return carry

    def start_high(k, carry):
        high_copy(k).start()
        return carry

    def add_low(k, acc):
        low_copy(k).wait()
        return acc + first[k]

    def add_high(k, acc):
        high_copy(k).wait()
        return acc + second[k]

    pl.semaphore_wait(barrier, 8 + low_n - 1 + high_n - 1)
    lax.fori_loop(1, low_n, start_low, 0)

    for arrival in arrivals[4:]:
        arrival.wait()
    leaf_mom[...] = jnp.zeros_like(leaf_mom)
    for tile in (0, 1):
        lanes = slice(tile * 128, tile * 128 + 128)
        bu = basis(own[0:64, lanes])
        bv = basis(own[64:128, lanes])
        m_t = own[128:192, lanes]
        live_t = jnp.where(m_t > 0.0, 1.0, 0.0)
        lone[tile, 0:PPL, :] = live_t
        for kind, weight in enumerate((m_t, live_t)):
            for a in range(NODES):
                wa = bu[a] * weight
                for b in range(NODES):
                    leaf_mom[pl.ds(kind * NM + a * 6 + b, 1), lanes] = jnp.sum(
                        wa * bv[b], axis=0, keepdims=True
                    )
    mom[...] = jnp.zeros_like(mom)
    stacked = []
    for kind in (0, 1):
        block = jnp.concatenate(
            [
                leaf_mom[kind * NM : (kind + 1) * NM, ch * 64 : ch * 64 + 64]
                for ch in range(4)
            ],
            axis=0,
        )
        mom[kind * 160 : kind * 160 + 160, 0:64] = block
        stacked.append(block)
    par = jnp.dot(
        up[...], jnp.concatenate(stacked, axis=1), precision=HIGHEST, preferred_element_type=F32
    )
    for kind in (0, 1):
        for q in range(4):
            at = kind * 64 + q * 16
            mom[pl.ds(kind * 160 + q * NM, NM), 64:80] = par[:, at : at + 16]
    own_cut = split3(own[...])
    send[:, 0:192] = nt_dot(
        jnp.concatenate([sel_leaf[...]] * 3, axis=1), jnp.concatenate(own_cut, axis=1)
    )
    send[:, 192:512] = nt_dot(
        jnp.concatenate([sel_mom[...]] * 3, axis=1),
        jnp.concatenate(split3(mom[...]), axis=1),
    )
    edges = []
    for d, (dx, dy) in enumerate(DIRS):
        rows = pl.ds(ROW_OF[d], ROWS_IN[d])
        copy = pltpu.make_async_remote_copy(
            src_ref=send.at[rows], dst_ref=recv.at[rows], send_sem=edge_s.at[d],
            recv_sem=edge_r.at[d], device_id=beside(-dx, -dy),
            device_id_type=pl.DeviceIdType.MESH,
        )
        copy.start()
        edges.append(copy)
    recv[96:HROWS, :] = jnp.zeros((HROWS - 96, LANES_OUT), F32)

    def fill_tables(scale, table_hi, table_lo):
        def fill(i, carry):
            at = pl.multiple_of(i * 16, 16)
            rows = t_rows[pl.ds(at, 16), :]
            row_x, row_y = rows[:, 0:1] * scale, rows[:, 1:2] * scale
            cell_x, cell_y = rows[:, 2:3], rows[:, 3:4]
            for start in range(0, 1440, FILL_LANES):
                lanes = slice(start, min(start + FILL_LANES, 1440))
                dx = row_x - t_cols[0:1, lanes] * scale
                dy = row_y - t_cols[1:2, lanes] * scale
                gap = jnp.maximum(
                    jnp.abs(cell_x - t_cols[2:3, lanes]), jnp.abs(cell_y - t_cols[3:4, lanes])
                )
                x2 = dx * dx
                y2 = dy * dy
                inv = jnp.where(gap > 1.5, 1.0 / (x2 + y2 + SOFTEN), 0.0)
                kx = dx * inv
                ky = dy * inv
                for c, val in enumerate((kx, ky, ky * ky - kx * kx, -2.0 * kx * ky)):
                    hi, lo = split2(val)
                    table_hi[pl.ds(c * 160 + at, 16), lanes] = hi
                    table_lo[pl.ds(c * 160 + at, 16), lanes] = lo
            return carry

        lax.fori_loop(0, 10, fill, 0)

    fill_tables(2.0, hi_par, lo_par)
    fill_tables(1.0, hi_leaf, lo_leaf)

    def at_offset(o):
        return slice(o * PPL, o * PPL + PPL)

    own_parts = jnp.concatenate(own_cut, axis=1)

    def shift_own(o):
        hot = jnp.where(row256 == src_leaf[o : o + 1, :], 1.0, 0.0).astype(BF16)
        moved = tn_none(own_parts, jnp.concatenate([hot] * 3, axis=0))
        for tile in (0, 1):
            lanes = slice(tile * 128, tile * 128 + 128)
            su[tile, at_offset(o), :] = moved[0:64, lanes]
            sv[tile, at_offset(o), :] = moved[64:128, lanes]
            sw[tile, at_offset(o), :] = moved[128:192, lanes]

    for o in range(NEIGHBOURS):
        shift_own(o)
    self_at = NEIGHBOURS * PPL
    for tile in (0, 1):
        lanes = slice(tile * 128, tile * 128 + 128)
        su[tile, self_at : self_at + PPL, :] = own[0:64, lanes] * 0.5
        sv[tile, self_at : self_at + PPL, :] = own[64:128, lanes] * 0.5
        sw[tile, self_at : self_at + PPL, :] = own[128:192, lanes]

    mid[...] = lax.fori_loop(1, low_n, add_low, part[...])
    lax.fori_loop(1, high_n, start_high, 0)

    zero = jnp.zeros((8, 128), F32)

    def targets(tile, base, width):
        lanes = slice(tile * 128, tile * 128 + 128)
        tx = [own[base + 8 * i : base + 8 * i + 8, lanes] * 0.5 for i in range(width)]
        ty = [own[64 + base + 8 * i : 72 + base + 8 * i, lanes] * 0.5 for i in range(width)]
        return tx, ty

    self_width = 2
    for tile in (0, 1):
        for piece in range(PPL // (8 * self_width)):
            base = piece * 8 * self_width
            tx, ty = targets(tile, base, self_width)

            def self_pairs(step, acc, tile=tile, tx=tx, ty=ty):
                acc = list(acc)
                for i in range(4):
                    k = step * 4 + i
                    at = pl.ds(self_at + k, 8, stride=0)
                    sx, sy, m = su[tile, at, :], sv[tile, at, :], sw[tile, at, :]
                    one = lone[tile, pl.ds(k, 8, stride=0), :]
                    for t in range(self_width):
                        dx = tx[t] - sx
                        dy = ty[t] - sy
                        x2 = dx * dx
                        y2 = dy * dy
                        inv = 1.0 / (x2 + y2 + SOFTEN)
                        gap = y2 - x2
                        cross = dx * dy
                        for kind, w in enumerate((m, one)):
                            at_acc = 8 * t + 4 * kind
                            w1 = w * inv
                            w2 = w1 * inv
                            acc[at_acc] = acc[at_acc] + w1 * dx
                            acc[at_acc + 1] = acc[at_acc + 1] + w1 * dy
                            acc[at_acc + 2] = acc[at_acc + 2] + w2 * gap
                            acc[at_acc + 3] = acc[at_acc + 3] + w2 * cross
                return tuple(acc)

            acc = lax.fori_loop(0, PPL // 4, self_pairs, (zero,) * (8 * self_width))
            for t in range(self_width):
                rows = slice(tile * PPL + base + 8 * t, tile * PPL + base + 8 * t + 8)
                for c in range(4):
                    scale = -2.0 if c == 3 else 1.0
                    result[c, rows, :] = acc[8 * t + c] * scale
                    self_live[c, rows, :] = acc[8 * t + 4 + c] * scale

    sums = lax.fori_loop(1, high_n, add_high, mid[...])
    mass_sum = jnp.sum(sums[0:1], axis=1, keepdims=True)
    live_sum = jnp.sum(sums[1:2], axis=1, keepdims=True)
    mean = mass_sum / live_sum
    for copy in edges:
        copy.wait()
    cell_x = sides[0:1] + jnp.full((1, 128), bx, jnp.int32).astype(F32)
    cell_y = sides[1:2] + jnp.full((1, 128), by, jnp.int32).astype(F32)
    inside = jnp.where(
        (cell_x >= 0.0) & (cell_x < float(nx)) & (cell_y >= 0.0) & (cell_y < float(ny)), 1.0, 0.0
    )
    halo = recv[...].T * inside
    halo_parts = jnp.concatenate(split3(halo[0:192]), axis=1)
    row128 = lax.broadcasted_iota(jnp.int32, (128, 256), 0) + 256

    def shift_halo(o):
        hot = jnp.where(row128 == src_leaf[o : o + 1, :], 1.0, 0.0).astype(BF16)
        moved = tn_none(halo_parts, jnp.concatenate([hot] * 3, axis=0))
        off_x, off_y = OFFS[o]
        for tile in (0, 1):
            lanes = slice(tile * 128, tile * 128 + 128)
            at = at_offset(o)
            su[tile, at, :] = (su[tile, at, :] + moved[0:64, lanes]) * 0.5 + off_x
            sv[tile, at, :] = (sv[tile, at, :] + moved[64:128, lanes]) * 0.5 + off_y
            m = sw[tile, at, :] + moved[128:192, lanes]
            sw[tile, at, :] = jnp.where(m > 0.0, m - mean, 0.0)

    for o in range(NEIGHBOURS):
        shift_halo(o)

    all_mom = jnp.concatenate([mom[...], halo[192:512]], axis=1)
    all_mom = all_mom[0:160] - mean * all_mom[160:320]
    cut_mom = jnp.concatenate(split2(all_mom), axis=0)

    def shift_moments(o):
        hot = jnp.where(row256[:, 0:128] == src_mom[o : o + 1, :], 1.0, 0.0).astype(BF16)
        moved = tn_none(cut_mom, hot).astype(BF16)
        xs[o * 160 : o * 160 + 160, 0:128] = moved[0:160]
        xs[o * 160 : o * 160 + 160, 128:256] = moved[160:320]

    for o in range(9):
        shift_moments(o)

    def far(table_hi, table_lo):
        wide = tn_none(table_hi[...], xs[...])
        return wide[:, 0:128] + wide[:, 128:256] + tn_none(table_lo[...], xs[:, 0:128])

    par = far(hi_par, lo_par)
    par_cols = jnp.concatenate(
        [
            jnp.concatenate(
                [par[c * 160 + q * NM : c * 160 + q * NM + NM, 64:80] for q in range(4)], axis=1
            )
            for c in range(4)
        ],
        axis=1,
    )
    from_par = jnp.dot(
        down[...], par_cols, precision=HIGHEST, preferred_element_type=F32
    )
    leaf = far(hi_leaf, lo_leaf)
    for c in range(4):
        leaf_local[c] = jnp.concatenate(
            [
                leaf[c * 160 + ch * NM : c * 160 + ch * NM + NM, 0:64]
                + from_par[ch * NM : ch * NM + NM, c * 64 : c * 64 + 64]
                for ch in range(4)
            ],
            axis=1,
        )

    for tile in (0, 1):
        lanes = slice(tile * 128, tile * 128 + 128)
        bu = basis(own[0:64, lanes])
        bv = basis(own[64:128, lanes])
        for c in range(4):
            rows = slice(tile * PPL, tile * PPL + PPL)
            acc = result[c, rows, :] - mean * self_live[c, rows, :]
            for a in range(NODES):
                half = leaf_local[c, pl.ds(a * 6, 1), lanes] * bv[0]
                for b in range(1, NODES):
                    half = half + leaf_local[c, pl.ds(a * 6 + b, 1), lanes] * bv[b]
                acc = acc + half * bu[a]
            result[c, rows, :] = acc

    width, unroll = 4, 8
    for tile in (0, 1):
        for piece in range(PPL // (8 * width)):
            base = piece * 8 * width
            tx, ty = targets(tile, base, width)

            def pairs(step, acc, tile=tile, tx=tx, ty=ty):
                acc = list(acc)
                for i in range(unroll):
                    at = pl.ds(step * unroll + i, 8, stride=0)
                    sx, sy, w = su[tile, at, :], sv[tile, at, :], sw[tile, at, :]
                    for t in range(width):
                        dx = tx[t] - sx
                        dy = ty[t] - sy
                        x2 = dx * dx
                        y2 = dy * dy
                        inv = 1.0 / (x2 + y2 + SOFTEN)
                        w1 = w * inv
                        w2 = w1 * inv
                        acc[4 * t] = acc[4 * t] + w1 * dx
                        acc[4 * t + 1] = acc[4 * t + 1] + w1 * dy
                        acc[4 * t + 2] = acc[4 * t + 2] + w2 * (y2 - x2)
                        acc[4 * t + 3] = acc[4 * t + 3] + w2 * (dx * dy)
                return tuple(acc)

            acc = lax.fori_loop(0, NEIGHBOURS * PPL // unroll, pairs, (zero,) * (4 * width))
            for t in range(width):
                rows = slice(tile * PPL + base + 8 * t, tile * PPL + base + 8 * t + 8)
                for c in range(4):
                    near = acc[4 * t + c]
                    if c == 3:
                        near = near * -2.0
                    result[c, rows, :] = result[c, rows, :] + near

    for c in range(4):
        back = result[c].T
        for i, s in enumerate(starts):
            out[pl.ds(s * 4 + c, 16, stride=32), :] = back[16 * i : 16 * i + 16]


def vmem():
    return pl.BlockSpec(memory_space=pltpu.VMEM)


NAMES = ("src_leaf", "sel_leaf", "sel_mom", "up", "t_rows", "t_cols", "sides", "src_mom", "down")
OPERANDS = 3 + len(NAMES)


def on_device(particle_pos, particle_mass, leaf_counts):
    dev_count = lax.axis_size("dev")
    bits = (lax.axis_size("grp") * dev_count).bit_length() - 1
    low_n = 2 ** (bits // 2)
    high_n = 2**bits // low_n
    pos = particle_pos.reshape(2, 128, 128).transpose(1, 0, 2).reshape(256, 128)
    mass = particle_mass.reshape(128, 128)
    count = leaf_counts.reshape(2, 128)
    operands = (pos, mass, count, *[jnp.asarray(CONST[k]) for k in NAMES])
    out = pl.pallas_call(
        functools.partial(whole_kernel, dev_count, bits),
        out_shape=jax.ShapeDtypeStruct((512, 128), F32),
        in_specs=[pl.BlockSpec(memory_space=pltpu.HBM)] * OPERANDS,
        out_specs=vmem(),
        scratch_shapes=[pltpu.VMEM(x.shape, x.dtype) for x in operands]
        + [
            pltpu.SemaphoreType.DMA((OPERANDS,)),
            pltpu.VMEM((192, 256), F32),
            pltpu.VMEM((320, 128), F32),
            pltpu.VMEM((HROWS, LANES_OUT), F32),
            pltpu.VMEM((HROWS, LANES_OUT), F32),
            pltpu.VMEM((8, 128), F32),
            pltpu.VMEM((8, 128), F32),
            pltpu.VMEM((2 * NM, 256), F32),
            pltpu.VMEM((low_n, 8, 128), F32),
            pltpu.VMEM((high_n, 8, 128), F32),
            pltpu.VMEM((2, 9 * PPL + 8, 128), F32),
            pltpu.VMEM((2, 9 * PPL + 8, 128), F32),
            pltpu.VMEM((2, 9 * PPL + 8, 128), F32),
            pltpu.VMEM((2, PPL + 8, 128), F32),
            pltpu.VMEM((1440, 256), BF16),
            pltpu.VMEM((640, 1440), BF16),
            pltpu.VMEM((640, 1440), BF16),
            pltpu.VMEM((640, 1440), BF16),
            pltpu.VMEM((640, 1440), BF16),
            pltpu.VMEM((4, NM, 256), F32),
            pltpu.VMEM((4, 128, 128), F32),
            pltpu.VMEM((4, 128, 128), F32),
            pltpu.SemaphoreType.DMA((8,)),
            pltpu.SemaphoreType.DMA((8,)),
            pltpu.SemaphoreType.DMA((low_n,)),
            pltpu.SemaphoreType.DMA((low_n,)),
            pltpu.SemaphoreType.DMA((high_n,)),
            pltpu.SemaphoreType.DMA((high_n,)),
        ],
        compiler_params=pltpu.CompilerParams(
            collective_id=0, has_side_effects=True, vmem_limit_bytes=63 * 2**20
        ),
        name="fields",
    )(*operands)
    return out.reshape(128, 4, 128).transpose(1, 0, 2).reshape(4, LSIDE * LSIDE * PPL)


def solution(mesh):
    in_specs = (P(None, ("grp", "dev")), P(("grp", "dev")), P(("grp", "dev")))
    out_specs = P(None, ("grp", "dev"))
    return jax.shard_map(
        on_device, mesh=mesh, in_specs=in_specs, out_specs=out_specs, check_vma=False
    )
```

```python
import functools

import jax
import jax.numpy as jnp
import numpy as np
from jax import lax
from jax.experimental import pallas as pl
from jax.experimental.pallas import tpu as pltpu
from jax.sharding import PartitionSpec as P

NODES = 6
PPL = 64
LSIDE = 16
SOFTEN = 0.01
NM = 40
HIGHEST = lax.Precision.HIGHEST
F32 = jnp.float32
BF16 = jnp.bfloat16

DIRS = ((-1, 0), (1, 0), (0, -1), (0, 1), (-1, -1), (1, -1), (-1, 1), (1, 1))
ROW_OF = (0, 16, 32, 48, 64, 72, 80, 88)
ROWS_IN = (16, 16, 16, 16, 8, 8, 8, 8)
HROWS = 128
LANES_OUT = 512
OFFS = tuple((ox, oy) for ox in (-1, 0, 1) for oy in (-1, 0, 1) if (ox, oy) != (0, 0)) + ((0, 0),)
NEIGHBOURS = 8
FILL_LANES = 256


def gp_col(gx, gy):
    return (gx & 1) + 2 * (gy & 1) + 4 * (gx >> 1) + 8 * (gy >> 1)


def par_col(px, py):
    return (px & 1) * 32 + (py & 1) * 16 + gp_col(px >> 1, py >> 1)


def leaf_col(x, y):
    return (x & 1) * 128 + (y & 1) * 64 + par_col(x >> 1, y >> 1)


def halo_cells(side):
    cells = []
    for dx, dy in DIRS:
        ex = -1 if dx < 0 else side
        ey = -1 if dy < 0 else side
        if dy == 0:
            cells.append([(ex, j) for j in range(side)])
        elif dx == 0:
            cells.append([(j, ey) for j in range(side)])
        else:
            cells.append([(ex, ey)])
    return cells


def pick_rows(side, col, base, lanes):
    out = np.zeros((HROWS, lanes), np.float32)
    for d, cells in enumerate(halo_cells(side)):
        for j, (cx, cy) in enumerate(cells):
            out[ROW_OF[d] + base[d] + j, col(cx % side, cy % side)] = 1.0
    return out


PAR_BASE = (0,) * 8
GP_BASE = (8,) * 4 + (1,) * 4


def shift_index(side, col, base, own_at, halo_at):
    where = {}
    for x in range(side):
        for y in range(side):
            where[x, y] = own_at + col(x, y)
    for d, cells in enumerate(halo_cells(side)):
        for j, cell in enumerate(cells):
            where[cell] = halo_at + ROW_OF[d] + base[d] + j
    out = np.zeros((9, side * side), np.int32)
    for o, (ox, oy) in enumerate(OFFS):
        for x in range(side):
            for y in range(side):
                out[o, col(x, y)] = where[x + ox, y + oy]
    return out


def cheb(u):
    terms = [u * 0 + 1.0, u]
    for _ in range(NODES - 2):
        terms.append(2.0 * u * terms[-1] - terms[-2])
    return terms


ANGLES = (2.0 * np.arange(NODES) + 1.0) * np.pi / (2.0 * NODES)
POINTS = np.cos(ANGLES)
S_COEF = 2.0 / NODES * np.cos(np.arange(NODES)[:, None] * ANGLES[None, :])
S_COEF[0] = 1.0 / NODES


def basis(u):
    terms = cheb(u)
    out = []
    for k in range(NODES):
        total = S_COEF[0, k] + float(S_COEF[1, k]) * terms[1]
        for n in range(2, NODES):
            total = total + float(S_COEF[n, k]) * terms[n]
        out.append(total)
    return out


def child_table():
    side = []
    for s in (0, 1):
        side.append(np.stack(basis(s - 0.5 + POINTS / 2), axis=1))
    out = np.zeros((4, NM, NM), np.float32)
    for sx in (0, 1):
        for sy in (0, 1):
            prod = side[sx][:, None, :, None] * side[sy][None, :, None, :]
            out[2 * sx + sy, :36, :36] = prod.reshape(36, 36)
    return out


def cell_vectors():
    coord = np.zeros((2, 4, NM), np.float32)
    cell = np.zeros((2, 4, NM), np.float32)
    for sx in (0, 1):
        for sy in (0, 1):
            ch = 2 * sx + sy
            node = np.arange(36)
            coord[0, ch] = sx - 0.5
            coord[1, ch] = sy - 0.5
            coord[0, ch, :36] += 0.5 * POINTS[node // 6]
            coord[1, ch, :36] += 0.5 * POINTS[node % 6]
            cell[0, ch] = sx
            cell[1, ch] = sy
    return coord.reshape(2, 4 * NM), cell.reshape(2, 4 * NM)


def constants():
    c = {}
    c["sel_leaf"] = pick_rows(LSIDE, leaf_col, PAR_BASE, 256).astype(BF16)
    sel_par = pick_rows(LSIDE // 2, par_col, PAR_BASE, 64)
    sel_gp = pick_rows(LSIDE // 4, gp_col, GP_BASE, 64)
    c["sel_mom"] = np.concatenate([sel_par, sel_gp], axis=1).astype(BF16)
    table = child_table()
    c["up"] = np.transpose(table, (2, 0, 1)).reshape(NM, 4 * NM)
    c["down"] = table.reshape(4 * NM, NM)
    src = np.zeros((16, 256), np.int32)
    src[:9] = shift_index(LSIDE, leaf_col, PAR_BASE, 0, 256)
    for x in range(LSIDE):
        for y in range(LSIDE):
            src[9, leaf_col(x, y)] = sum(
                (x >> k & 1) << 2 * k | (y >> k & 1) << 2 * k + 1 for k in range(4)
            )
    c["src_leaf"] = src
    msrc = np.full((16, 128), -1, np.int32)
    msrc[:9, :64] = shift_index(LSIDE // 2, par_col, PAR_BASE, 0, 128)
    msrc[:9, 64:80] = shift_index(LSIDE // 4, gp_col, GP_BASE, 64, 128)
    c["src_mom"] = msrc
    coord, cell = cell_vectors()
    rows = np.zeros((160, 128), np.float32)
    rows[:, 0:2] = coord.T
    rows[:, 2:4] = cell.T
    c["t_rows"] = rows
    cols = np.zeros((8, 9, 160), np.float32)
    for o, (ox, oy) in enumerate(OFFS):
        cols[0, o] = coord[0] + 2 * ox
        cols[1, o] = coord[1] + 2 * oy
        cols[2, o] = cell[0] + 2 * ox
        cols[3, o] = cell[1] + 2 * oy
    c["t_cols"] = cols.reshape(8, 1440)
    sides = np.zeros((8, HROWS), np.float32)
    for d, (dx, dy) in enumerate(DIRS):
        sides[0, ROW_OF[d] : ROW_OF[d] + ROWS_IN[d]] = dx
        sides[1, ROW_OF[d] : ROW_OF[d] + ROWS_IN[d]] = dy
    c["sides"] = sides
    return c


CONST = constants()


def split2(x):
    hi = x.astype(BF16)
    return hi, (x - hi.astype(F32)).astype(BF16)


def split3(x):
    hi = x.astype(BF16)
    rest = x - hi.astype(F32)
    mid = rest.astype(BF16)
    return hi, mid, (rest - mid.astype(F32)).astype(BF16)


def nt_dot(a, b):
    return lax.dot_general(a, b, (((1,), (1,)), ((), ())), preferred_element_type=F32)


def tn_none(a, b):
    return lax.dot_general(a, b, (((1,), (0,)), ((), ())), preferred_element_type=F32)


def morton_split(code, bits):
    cx, cy = 0, 0
    for level in range((bits + 1) // 2):
        cx = cx + code // 4**level % 2 * 2**level
        cy = cy + code // (2 * 4**level) % 2 * 2**level
    return cx, cy


def morton_join(cx, cy, bits):
    code = 0
    for level in range((bits + 1) // 2):
        code = code + cx // 2**level % 2 * 4**level
        code = code + cy // 2**level % 2 * 2 * 4**level
    return code


def whole_kernel(dev_count, bits, *refs):
    sources, refs = refs[:OPERANDS], refs[OPERANDS:]
    out, refs = refs[0], refs[1:]
    held, refs = refs[:OPERANDS], refs[OPERANDS:]
    (pos, mass, count, src_leaf, sel_leaf, sel_mom, up, t_rows, t_cols, sides, src_mom,
     down) = held
    arrive_sems = refs[0]
    arrivals = [
        pltpu.make_async_copy(src, dst, arrive_sems.at[i])
        for i, (src, dst) in enumerate(zip(sources, held))
    ]
    for arrival in arrivals:
        arrival.start()
    run_kernel(dev_count, bits, arrivals, pos, mass, count, sel_leaf, sel_mom, up, down, sides,
               src_leaf, src_mom, t_rows, t_cols, out, *refs[1:])


def run_kernel(dev_count, bits, arrivals, pos, mass, count, sel_leaf, sel_mom, up, down, sides,
               src_leaf, src_mom, t_rows, t_cols, out, own, mom, send, recv, part, mid, leaf_mom, first,
                 second, su, sv, sw, lone, xs, xs_par, hi_leaf, lo_leaf, hi_par, lo_par, leaf_kind, leaf_local,
                 result, self_live, edge_s, edge_r, sum_s1, sum_r1, sum_s2, sum_r2):
    code = lax.axis_index("grp") * dev_count + lax.axis_index("dev")
    bx, by = morton_split(code, bits)
    nx, ny = 2 ** ((bits + 1) // 2), 2 ** (bits // 2)
    low_n = 2 ** (bits // 2)
    high_n = 2**bits // low_n
    low, high = code % low_n, code // low_n

    def device(c):
        return {"grp": c // dev_count, "dev": c % dev_count}

    def beside(dx, dy):
        return device(morton_join((bx + dx + nx) % nx, (by + dy + ny) % ny, bits))

    def in_low(k):
        return device(high * low_n + (low + k) % low_n)

    def in_high(k):
        return device((high + k) % high_n * low_n + low)

    barrier = pltpu.get_barrier_semaphore()

    def greet(who):
        pl.semaphore_signal(barrier, inc=1, device_id=who, device_id_type=pl.DeviceIdType.MESH)

    def greet_low(k, carry):
        greet(in_low(k))
        return carry

    def greet_high(k, carry):
        greet(in_high(k))
        return carry

    lax.fori_loop(1, low_n, greet_low, 0)
    for dx, dy in DIRS:
        greet(beside(dx, dy))
    lax.fori_loop(1, high_n, greet_high, 0)

    starts = [qx * 2 + qy * 4 + sy for sy in (0, 1) for qx in (0, 1) for qy in (0, 1)]

    def turned(ref, lead, step):
        rows = jnp.concatenate(
            [ref[pl.ds(lead + step * s, 16, stride=8 * step), :] for s in starts], axis=0
        )
        return rows.T

    for arrival in arrivals[:4]:
        arrival.wait()
    row256 = lax.broadcasted_iota(jnp.int32, (256, 256), 0)
    pick = jnp.where(row256 == src_leaf[9:10, :], 1.0, 0.0).astype(BF16)
    linear = count[...].astype(F32).astype(BF16)
    counts = tn_none(linear[0:1], pick[0:128]) + tn_none(linear[1:2], pick[128:256])
    m_turned = turned(mass, 0, 1)
    slot = lax.broadcasted_iota(jnp.int32, (PPL, 128), 0).astype(F32)
    totals = []
    for tile in (0, 1):
        lanes = slice(tile * 128, tile * 128 + 128)
        live = slot < counts[:, lanes]
        vals = jnp.where(live, m_turned[tile * PPL : tile * PPL + PPL], 0.0)
        own[128:192, lanes] = vals
        totals.append(jnp.sum(vals, axis=0, keepdims=True))
    row = lax.broadcasted_iota(jnp.int32, (8, 128), 0)
    part[...] = jnp.where(
        row == 0,
        totals[0] + totals[1],
        jnp.where(row == 1, counts[:, 0:128] + counts[:, 128:256], 0.0),
    )

    def low_copy(k):
        return pltpu.make_async_remote_copy(
            src_ref=part, dst_ref=first.at[k], send_sem=sum_s1.at[k], recv_sem=sum_r1.at[k],
            device_id=in_low(k), device_id_type=pl.DeviceIdType.MESH,
        )

    def high_copy(k):
        return pltpu.make_async_remote_copy(
            src_ref=mid, dst_ref=second.at[k], send_sem=sum_s2.at[k], recv_sem=sum_r2.at[k],
            device_id=in_high(k), device_id_type=pl.DeviceIdType.MESH,
        )

    def start_low(k, carry):
        low_copy(k).start()
        return carry

    def start_high(k, carry):
        high_copy(k).start()
        return carry

    def add_low(k, acc):
        low_copy(k).wait()
        return acc + first[k]

    def add_high(k, acc):
        high_copy(k).wait()
        return acc + second[k]

    pl.semaphore_wait(barrier, 8 + low_n - 1 + high_n - 1)
    lax.fori_loop(1, low_n, start_low, 0)
    for k in (0, 1):
        vals = turned(pos, k, 2)
        own[k * PPL : (k + 1) * PPL, 0:128] = vals[:PPL]
        own[k * PPL : (k + 1) * PPL, 128:256] = vals[PPL:]

    for arrival in arrivals[4:]:
        arrival.wait()
    leaf_mom[...] = jnp.zeros_like(leaf_mom)
    for tile in (0, 1):
        lanes = slice(tile * 128, tile * 128 + 128)
        bu = basis(own[0:64, lanes])
        bv = basis(own[64:128, lanes])
        m_t = own[128:192, lanes]
        live_t = jnp.where(m_t > 0.0, 1.0, 0.0)
        lone[tile, 0:PPL, :] = live_t
        for kind, weight in enumerate((m_t, live_t)):
            for a in range(NODES):
                wa = bu[a] * weight
                for b in range(NODES):
                    leaf_mom[pl.ds(kind * NM + a * 6 + b, 1), lanes] = jnp.sum(
                        wa * bv[b], axis=0, keepdims=True
                    )
    mom[...] = jnp.zeros_like(mom)
    stacked = []
    for kind in (0, 1):
        block = jnp.concatenate(
            [
                leaf_mom[kind * NM : (kind + 1) * NM, ch * 64 : ch * 64 + 64]
                for ch in range(4)
            ],
            axis=0,
        )
        mom[kind * 160 : kind * 160 + 160, 0:64] = block
        stacked.append(block)
    par = jnp.dot(
        up[...], jnp.concatenate(stacked, axis=1), precision=HIGHEST, preferred_element_type=F32
    )
    for kind in (0, 1):
        for q in range(4):
            at = kind * 64 + q * 16
            mom[pl.ds(kind * 160 + q * NM, NM), 64:80] = par[:, at : at + 16]
    own_cut = split3(own[...])
    send[:, 0:192] = nt_dot(
        jnp.concatenate([sel_leaf[...]] * 3, axis=1), jnp.concatenate(own_cut, axis=1)
    )
    send[:, 192:512] = nt_dot(
        jnp.concatenate([sel_mom[...]] * 3, axis=1),
        jnp.concatenate(split3(mom[...]), axis=1),
    )
    edges = []
    for d, (dx, dy) in enumerate(DIRS):
        rows = pl.ds(ROW_OF[d], ROWS_IN[d])
        copy = pltpu.make_async_remote_copy(
            src_ref=send.at[rows], dst_ref=recv.at[rows], send_sem=edge_s.at[d],
            recv_sem=edge_r.at[d], device_id=beside(-dx, -dy),
            device_id_type=pl.DeviceIdType.MESH,
        )
        copy.start()
        edges.append(copy)
    recv[96:HROWS, :] = jnp.zeros((HROWS - 96, LANES_OUT), F32)

    def fill_tables(scale, table_hi, table_lo):
        def fill(i, carry):
            at = pl.multiple_of(i * 16, 16)
            rows = t_rows[pl.ds(at, 16), :]
            row_x, row_y = rows[:, 0:1] * scale, rows[:, 1:2] * scale
            cell_x, cell_y = rows[:, 2:3], rows[:, 3:4]
            for start in range(0, 1440, FILL_LANES):
                lanes = slice(start, min(start + FILL_LANES, 1440))
                dx = row_x - t_cols[0:1, lanes] * scale
                dy = row_y - t_cols[1:2, lanes] * scale
                gap = jnp.maximum(
                    jnp.abs(cell_x - t_cols[2:3, lanes]), jnp.abs(cell_y - t_cols[3:4, lanes])
                )
                x2 = dx * dx
                y2 = dy * dy
                inv = jnp.where(gap > 1.5, 1.0 / (x2 + y2 + SOFTEN), 0.0)
                kx = dx * inv
                ky = dy * inv
                for c, val in enumerate((kx, ky, ky * ky - kx * kx, -2.0 * kx * ky)):
                    hi, lo = split2(val)
                    table_hi[pl.ds(c * 160 + at, 16), lanes] = hi
                    table_lo[pl.ds(c * 160 + at, 16), lanes] = lo
            return carry

        lax.fori_loop(0, 10, fill, 0)

    fill_tables(2.0, hi_par, lo_par)
    fill_tables(1.0, hi_leaf, lo_leaf)

    def at_offset(o):
        return slice(o * PPL, o * PPL + PPL)

    own_parts = jnp.concatenate(own_cut, axis=1)

    def shift_own(o):
        hot = jnp.where(row256 == src_leaf[o : o + 1, :], 1.0, 0.0).astype(BF16)
        moved = tn_none(own_parts, jnp.concatenate([hot] * 3, axis=0))
        for tile in (0, 1):
            lanes = slice(tile * 128, tile * 128 + 128)
            su[tile, at_offset(o), :] = moved[0:64, lanes]
            sv[tile, at_offset(o), :] = moved[64:128, lanes]
            sw[tile, at_offset(o), :] = moved[128:192, lanes]

    for o in range(NEIGHBOURS):
        shift_own(o)
    self_at = NEIGHBOURS * PPL
    for tile in (0, 1):
        lanes = slice(tile * 128, tile * 128 + 128)
        su[tile, self_at : self_at + PPL, :] = own[0:64, lanes] * 0.5
        sv[tile, self_at : self_at + PPL, :] = own[64:128, lanes] * 0.5
        sw[tile, self_at : self_at + PPL, :] = own[128:192, lanes]

    mid[...] = lax.fori_loop(1, low_n, add_low, part[...])
    lax.fori_loop(1, high_n, start_high, 0)

    zero = jnp.zeros((8, 128), F32)

    def targets(tile, base, width):
        lanes = slice(tile * 128, tile * 128 + 128)
        tx = [own[base + 8 * i : base + 8 * i + 8, lanes] * 0.5 for i in range(width)]
        ty = [own[64 + base + 8 * i : 72 + base + 8 * i, lanes] * 0.5 for i in range(width)]
        return tx, ty

    self_width = 2
    for tile in (0, 1):
        for piece in range(PPL // (8 * self_width)):
            base = piece * 8 * self_width
            tx, ty = targets(tile, base, self_width)

            def self_pairs(step, acc, tile=tile, tx=tx, ty=ty):
                acc = list(acc)
                for i in range(4):
                    k = step * 4 + i
                    at = pl.ds(self_at + k, 8, stride=0)
                    sx, sy, m = su[tile, at, :], sv[tile, at, :], sw[tile, at, :]
                    one = lone[tile, pl.ds(k, 8, stride=0), :]
                    for t in range(self_width):
                        dx = tx[t] - sx
                        dy = ty[t] - sy
                        x2 = dx * dx
                        y2 = dy * dy
                        inv = 1.0 / (x2 + y2 + SOFTEN)
                        gap = y2 - x2
                        cross = dx * dy
                        for kind, w in enumerate((m, one)):
                            at_acc = 8 * t + 4 * kind
                            w1 = w * inv
                            w2 = w1 * inv
                            acc[at_acc] = acc[at_acc] + w1 * dx
                            acc[at_acc + 1] = acc[at_acc + 1] + w1 * dy
                            acc[at_acc + 2] = acc[at_acc + 2] + w2 * gap
                            acc[at_acc + 3] = acc[at_acc + 3] + w2 * cross
                return tuple(acc)

            acc = lax.fori_loop(0, PPL // 4, self_pairs, (zero,) * (8 * self_width))
            for t in range(self_width):
                rows = slice(tile * PPL + base + 8 * t, tile * PPL + base + 8 * t + 8)
                for c in range(4):
                    scale = -2.0 if c == 3 else 1.0
                    result[c, rows, :] = acc[8 * t + c] * scale
                    self_live[c, rows, :] = acc[8 * t + 4 + c] * scale

    for copy in edges:
        copy.wait()
    cell_x = sides[0:1] + jnp.full((1, 128), bx, jnp.int32).astype(F32)
    cell_y = sides[1:2] + jnp.full((1, 128), by, jnp.int32).astype(F32)
    inside = jnp.where(
        (cell_x >= 0.0) & (cell_x < float(nx)) & (cell_y >= 0.0) & (cell_y < float(ny)), 1.0, 0.0
    )
    halo = recv[...].T * inside
    halo_parts = jnp.concatenate(split3(halo[0:192]), axis=1)
    row128 = lax.broadcasted_iota(jnp.int32, (128, 256), 0) + 256

    def shift_halo(o):
        hot = jnp.where(row128 == src_leaf[o : o + 1, :], 1.0, 0.0).astype(BF16)
        moved = tn_none(halo_parts, jnp.concatenate([hot] * 3, axis=0))
        off_x, off_y = OFFS[o]
        for tile in (0, 1):
            lanes = slice(tile * 128, tile * 128 + 128)
            at = at_offset(o)
            su[tile, at, :] = (su[tile, at, :] + moved[0:64, lanes]) * 0.5 + off_x
            sv[tile, at, :] = (sv[tile, at, :] + moved[64:128, lanes]) * 0.5 + off_y
            sw[tile, at, :] = sw[tile, at, :] + moved[128:192, lanes]

    for o in range(NEIGHBOURS):
        shift_halo(o)

    all_mom = jnp.concatenate([mom[...], halo[192:512]], axis=1)
    cut_mom = jnp.concatenate(split2(all_mom), axis=0)

    def shift_moments(o):
        hot = jnp.where(row256[:, 0:128] == src_mom[o : o + 1, :], 1.0, 0.0).astype(BF16)
        moved = tn_none(cut_mom, hot)
        at = slice(o * 160, o * 160 + 160)
        pieces = [moved[160 * i : 160 * i + 160] for i in range(4)]
        xs[at, :] = jnp.concatenate([p[:, 0:64] for p in pieces], axis=1).astype(BF16)
        xs_par[at, :] = jnp.concatenate([p[:, 64:80] for p in pieces], axis=1).astype(BF16)

    for o in range(9):
        shift_moments(o)

    wide = tn_none(hi_par[...], xs_par[...])
    par = wide[:, 0:32] + wide[:, 32:64] + tn_none(lo_par[...], xs_par[:, 0:32])
    par_cols = jnp.concatenate(
        [
            par[c * 160 + q * NM : c * 160 + q * NM + NM, kind * 16 : kind * 16 + 16]
            for kind in (0, 1)
            for c in range(4)
            for q in range(4)
        ],
        axis=1,
    )
    from_par = jnp.dot(
        down[...], par_cols, precision=HIGHEST, preferred_element_type=F32
    )
    wide = tn_none(hi_leaf[...], xs[...])
    leaf = wide[:, 0:128] + wide[:, 128:256] + tn_none(lo_leaf[...], xs[:, 0:128])
    for kind in (0, 1):
        for c in range(4):
            at = kind * 256 + c * 64
            leaf_kind[kind, c] = jnp.concatenate(
                [
                    leaf[c * 160 + ch * NM : c * 160 + ch * NM + NM, kind * 64 : kind * 64 + 64]
                    + from_par[ch * NM : ch * NM + NM, at : at + 64]
                    for ch in range(4)
                ],
                axis=1,
            )

    sums = lax.fori_loop(1, high_n, add_high, mid[...])
    mass_sum = jnp.sum(sums[0:1], axis=1, keepdims=True)
    live_sum = jnp.sum(sums[1:2], axis=1, keepdims=True)
    mean = mass_sum / live_sum
    for tile in (0, 1):
        m = sw[tile, 0:self_at, :]
        sw[tile, 0:self_at, :] = jnp.where(m > 0.0, m - mean, 0.0)
    for c in range(4):
        leaf_local[c] = leaf_kind[0, c] - mean * leaf_kind[1, c]

    for tile in (0, 1):
        lanes = slice(tile * 128, tile * 128 + 128)
        bu = basis(own[0:64, lanes])
        bv = basis(own[64:128, lanes])
        for c in range(4):
            rows = slice(tile * PPL, tile * PPL + PPL)
            acc = result[c, rows, :] - mean * self_live[c, rows, :]
            for a in range(NODES):
                half = leaf_local[c, pl.ds(a * 6, 1), lanes] * bv[0]
                for b in range(1, NODES):
                    half = half + leaf_local[c, pl.ds(a * 6 + b, 1), lanes] * bv[b]
                acc = acc + half * bu[a]
            result[c, rows, :] = acc

    width, unroll = 4, 16
    for tile in (0, 1):
        for piece in range(PPL // (8 * width)):
            base = piece * 8 * width
            tx, ty = targets(tile, base, width)

            def pairs(step, acc, tile=tile, tx=tx, ty=ty):
                acc = list(acc)
                for i in range(unroll):
                    at = pl.ds(step * unroll + i, 8, stride=0)
                    sx, sy, w = su[tile, at, :], sv[tile, at, :], sw[tile, at, :]
                    for t in range(width):
                        dx = tx[t] - sx
                        dy = ty[t] - sy
                        inv = 1.0 / (dy * dy + (dx * dx + SOFTEN))
                        kx = dx * inv
                        ky = dy * inv
                        wx = w * kx
                        wy = w * ky
                        acc[4 * t] = acc[4 * t] + wx
                        acc[4 * t + 1] = acc[4 * t + 1] + wy
                        acc[4 * t + 2] = (acc[4 * t + 2] + wy * ky) - wx * kx
                        acc[4 * t + 3] = acc[4 * t + 3] + wx * ky
                return tuple(acc)

            acc = lax.fori_loop(0, NEIGHBOURS * PPL // unroll, pairs, (zero,) * (4 * width))
            for t in range(width):
                rows = slice(tile * PPL + base + 8 * t, tile * PPL + base + 8 * t + 8)
                for c in range(4):
                    near = acc[4 * t + c]
                    if c == 3:
                        near = near * -2.0
                    result[c, rows, :] = result[c, rows, :] + near

    for c in range(4):
        back = result[c].T
        for i, s in enumerate(starts):
            out[pl.ds(s * 4 + c, 16, stride=32), :] = back[16 * i : 16 * i + 16]


def vmem():
    return pl.BlockSpec(memory_space=pltpu.VMEM)


NAMES = ("src_leaf", "sel_leaf", "sel_mom", "up", "t_rows", "t_cols", "sides", "src_mom", "down")
OPERANDS = 3 + len(NAMES)


def on_device(particle_pos, particle_mass, leaf_counts):
    dev_count = lax.axis_size("dev")
    bits = (lax.axis_size("grp") * dev_count).bit_length() - 1
    low_n = 2 ** (bits // 2)
    high_n = 2**bits // low_n
    pos = particle_pos.reshape(2, 128, 128).transpose(1, 0, 2).reshape(256, 128)
    mass = particle_mass.reshape(128, 128)
    count = leaf_counts.reshape(2, 128)
    operands = (pos, mass, count, *[jnp.asarray(CONST[k]) for k in NAMES])
    out = pl.pallas_call(
        functools.partial(whole_kernel, dev_count, bits),
        out_shape=jax.ShapeDtypeStruct((512, 128), F32),
        in_specs=[pl.BlockSpec(memory_space=pltpu.HBM)] * OPERANDS,
        out_specs=vmem(),
        scratch_shapes=[pltpu.VMEM(x.shape, x.dtype) for x in operands]
        + [
            pltpu.SemaphoreType.DMA((OPERANDS,)),
            pltpu.VMEM((192, 256), F32),
            pltpu.VMEM((320, 128), F32),
            pltpu.VMEM((HROWS, LANES_OUT), F32),
            pltpu.VMEM((HROWS, LANES_OUT), F32),
            pltpu.VMEM((8, 128), F32),
            pltpu.VMEM((8, 128), F32),
            pltpu.VMEM((2 * NM, 256), F32),
            pltpu.VMEM((low_n, 8, 128), F32),
            pltpu.VMEM((high_n, 8, 128), F32),
            pltpu.VMEM((2, 9 * PPL + 8, 128), F32),
            pltpu.VMEM((2, 9 * PPL + 8, 128), F32),
            pltpu.VMEM((2, 9 * PPL + 8, 128), F32),
            pltpu.VMEM((2, PPL + 8, 128), F32),
            pltpu.VMEM((1440, 256), BF16),
            pltpu.VMEM((1440, 64), BF16),
            pltpu.VMEM((640, 1440), BF16),
            pltpu.VMEM((640, 1440), BF16),
            pltpu.VMEM((640, 1440), BF16),
            pltpu.VMEM((640, 1440), BF16),
            pltpu.VMEM((2, 4, NM, 256), F32),
            pltpu.VMEM((4, NM, 256), F32),
            pltpu.VMEM((4, 128, 128), F32),
            pltpu.VMEM((4, 128, 128), F32),
            pltpu.SemaphoreType.DMA((8,)),
            pltpu.SemaphoreType.DMA((8,)),
            pltpu.SemaphoreType.DMA((low_n,)),
            pltpu.SemaphoreType.DMA((low_n,)),
            pltpu.SemaphoreType.DMA((high_n,)),
            pltpu.SemaphoreType.DMA((high_n,)),
        ],
        compiler_params=pltpu.CompilerParams(
            collective_id=0, has_side_effects=True, vmem_limit_bytes=63 * 2**20
        ),
        name="fields",
    )(*operands)
    return out.reshape(128, 4, 128).transpose(1, 0, 2).reshape(4, LSIDE * LSIDE * PPL)


def solution(mesh):
    in_specs = (P(None, ("grp", "dev")), P(("grp", "dev")), P(("grp", "dev")))
    out_specs = P(None, ("grp", "dev"))
    return jax.shard_map(
        on_device, mesh=mesh, in_specs=in_specs, out_specs=out_specs, check_vma=False
    )
```

```python
import functools

import jax
import jax.numpy as jnp
import numpy as np
from jax import lax
from jax.experimental import pallas as pl
from jax.experimental.pallas import tpu as pltpu
from jax.sharding import PartitionSpec as P

NODES = 6
PPL = 64
LSIDE = 16
SOFTEN = 0.01
NM = 40
HIGHEST = lax.Precision.HIGHEST
F32 = jnp.float32
BF16 = jnp.bfloat16

DIRS = ((-1, 0), (1, 0), (0, -1), (0, 1), (-1, -1), (1, -1), (-1, 1), (1, 1))
ROW_OF = (0, 16, 32, 48, 64, 72, 80, 88)
ROWS_IN = (16, 16, 16, 16, 8, 8, 8, 8)
HROWS = 128
LANES_OUT = 512
OFFS = tuple((ox, oy) for ox in (-1, 0, 1) for oy in (-1, 0, 1) if (ox, oy) != (0, 0)) + ((0, 0),)
NEIGHBOURS = 8
FILL_LANES = 256


def gp_col(gx, gy):
    return (gx & 1) + 2 * (gy & 1) + 4 * (gx >> 1) + 8 * (gy >> 1)


def par_col(px, py):
    return (px & 1) * 32 + (py & 1) * 16 + gp_col(px >> 1, py >> 1)


def leaf_col(x, y):
    return (x & 1) * 128 + (y & 1) * 64 + par_col(x >> 1, y >> 1)


def halo_cells(side):
    cells = []
    for dx, dy in DIRS:
        ex = -1 if dx < 0 else side
        ey = -1 if dy < 0 else side
        if dy == 0:
            cells.append([(ex, j) for j in range(side)])
        elif dx == 0:
            cells.append([(j, ey) for j in range(side)])
        else:
            cells.append([(ex, ey)])
    return cells


def pick_rows(side, col, base, lanes):
    out = np.zeros((HROWS, lanes), np.float32)
    for d, cells in enumerate(halo_cells(side)):
        for j, (cx, cy) in enumerate(cells):
            out[ROW_OF[d] + base[d] + j, col(cx % side, cy % side)] = 1.0
    return out


PAR_BASE = (0,) * 8
GP_BASE = (8,) * 4 + (1,) * 4


def shift_index(side, col, base, own_at, halo_at):
    where = {}
    for x in range(side):
        for y in range(side):
            where[x, y] = own_at + col(x, y)
    for d, cells in enumerate(halo_cells(side)):
        for j, cell in enumerate(cells):
            where[cell] = halo_at + ROW_OF[d] + base[d] + j
    out = np.zeros((9, side * side), np.int32)
    for o, (ox, oy) in enumerate(OFFS):
        for x in range(side):
            for y in range(side):
                out[o, col(x, y)] = where[x + ox, y + oy]
    return out


def cheb(u):
    terms = [u * 0 + 1.0, u]
    for _ in range(NODES - 2):
        terms.append(2.0 * u * terms[-1] - terms[-2])
    return terms


ANGLES = (2.0 * np.arange(NODES) + 1.0) * np.pi / (2.0 * NODES)
POINTS = np.cos(ANGLES)
S_COEF = 2.0 / NODES * np.cos(np.arange(NODES)[:, None] * ANGLES[None, :])
S_COEF[0] = 1.0 / NODES


def basis(u):
    terms = cheb(u)
    out = []
    for k in range(NODES):
        total = S_COEF[0, k] + float(S_COEF[1, k]) * terms[1]
        for n in range(2, NODES):
            total = total + float(S_COEF[n, k]) * terms[n]
        out.append(total)
    return out


def child_table():
    side = []
    for s in (0, 1):
        side.append(np.stack(basis(s - 0.5 + POINTS / 2), axis=1))
    out = np.zeros((4, NM, NM), np.float32)
    for sx in (0, 1):
        for sy in (0, 1):
            prod = side[sx][:, None, :, None] * side[sy][None, :, None, :]
            out[2 * sx + sy, :36, :36] = prod.reshape(36, 36)
    return out


def cell_vectors():
    coord = np.zeros((2, 4, NM), np.float32)
    cell = np.zeros((2, 4, NM), np.float32)
    for sx in (0, 1):
        for sy in (0, 1):
            ch = 2 * sx + sy
            node = np.arange(36)
            coord[0, ch] = sx - 0.5
            coord[1, ch] = sy - 0.5
            coord[0, ch, :36] += 0.5 * POINTS[node // 6]
            coord[1, ch, :36] += 0.5 * POINTS[node % 6]
            cell[0, ch] = sx
            cell[1, ch] = sy
    return coord.reshape(2, 4 * NM), cell.reshape(2, 4 * NM)


def constants():
    c = {}
    c["sel_leaf"] = pick_rows(LSIDE, leaf_col, PAR_BASE, 256).astype(BF16)
    sel_par = pick_rows(LSIDE // 2, par_col, PAR_BASE, 64)
    sel_gp = pick_rows(LSIDE // 4, gp_col, GP_BASE, 64)
    c["sel_mom"] = np.concatenate([sel_par, sel_gp], axis=1).astype(BF16)
    table = child_table()
    c["up"] = np.transpose(table, (2, 0, 1)).reshape(NM, 4 * NM)
    c["down"] = table.reshape(4 * NM, NM)
    src = np.zeros((16, 256), np.int32)
    src[:9] = shift_index(LSIDE, leaf_col, PAR_BASE, 0, 256)
    for x in range(LSIDE):
        for y in range(LSIDE):
            src[9, leaf_col(x, y)] = sum(
                (x >> k & 1) << 2 * k | (y >> k & 1) << 2 * k + 1 for k in range(4)
            )
    c["src_leaf"] = src
    msrc = np.full((16, 128), -1, np.int32)
    msrc[:9, :64] = shift_index(LSIDE // 2, par_col, PAR_BASE, 0, 128)
    msrc[:9, 64:80] = shift_index(LSIDE // 4, gp_col, GP_BASE, 64, 128)
    c["src_mom"] = msrc
    coord, cell = cell_vectors()
    rows = np.zeros((160, 128), np.float32)
    rows[:, 0:2] = coord.T
    rows[:, 2:4] = cell.T
    c["t_rows"] = rows
    cols = np.zeros((8, 9, 160), np.float32)
    for o, (ox, oy) in enumerate(OFFS):
        cols[0, o] = coord[0] + 2 * ox
        cols[1, o] = coord[1] + 2 * oy
        cols[2, o] = cell[0] + 2 * ox
        cols[3, o] = cell[1] + 2 * oy
    c["t_cols"] = cols.reshape(8, 1440)
    sides = np.zeros((8, HROWS), np.float32)
    for d, (dx, dy) in enumerate(DIRS):
        sides[0, ROW_OF[d] : ROW_OF[d] + ROWS_IN[d]] = dx
        sides[1, ROW_OF[d] : ROW_OF[d] + ROWS_IN[d]] = dy
    c["sides"] = sides
    return c


CONST = constants()


def split2(x):
    hi = x.astype(BF16)
    return hi, (x - hi.astype(F32)).astype(BF16)


def split3(x):
    hi = x.astype(BF16)
    rest = x - hi.astype(F32)
    mid = rest.astype(BF16)
    return hi, mid, (rest - mid.astype(F32)).astype(BF16)


def nt_dot(a, b):
    return lax.dot_general(a, b, (((1,), (1,)), ((), ())), preferred_element_type=F32)


def tn_none(a, b):
    return lax.dot_general(a, b, (((1,), (0,)), ((), ())), preferred_element_type=F32)


def morton_split(code, bits):
    cx, cy = 0, 0
    for level in range((bits + 1) // 2):
        cx = cx + code // 4**level % 2 * 2**level
        cy = cy + code // (2 * 4**level) % 2 * 2**level
    return cx, cy


def morton_join(cx, cy, bits):
    code = 0
    for level in range((bits + 1) // 2):
        code = code + cx // 2**level % 2 * 4**level
        code = code + cy // 2**level % 2 * 2 * 4**level
    return code


def whole_kernel(dev_count, bits, *refs):
    sources, refs = refs[:OPERANDS], refs[OPERANDS:]
    out, refs = refs[0], refs[1:]
    held, refs = refs[:OPERANDS], refs[OPERANDS:]
    (pos, mass, count, src_leaf, sel_leaf, sel_mom, up, t_rows, t_cols, sides, src_mom,
     down) = held
    arrive_sems = refs[0]
    arrivals = [
        pltpu.make_async_copy(src, dst, arrive_sems.at[i])
        for i, (src, dst) in enumerate(zip(sources, held))
    ]
    for arrival in arrivals:
        arrival.start()
    run_kernel(dev_count, bits, arrivals, pos, mass, count, sel_leaf, sel_mom, up, down, sides,
               src_leaf, src_mom, t_rows, t_cols, out, *refs[1:])


def run_kernel(dev_count, bits, arrivals, pos, mass, count, sel_leaf, sel_mom, up, down, sides,
               src_leaf, src_mom, t_rows, t_cols, out, own, mom, send, recv, part, mid, leaf_mom, first,
                 second, su, sv, sw, xs, hi_leaf, lo_leaf, hi_par, lo_par, leaf_local,
                 result, edge_s, edge_r, sum_s1, sum_r1, sum_s2, sum_r2):
    code = lax.axis_index("grp") * dev_count + lax.axis_index("dev")
    bx, by = morton_split(code, bits)
    nx, ny = 2 ** ((bits + 1) // 2), 2 ** (bits // 2)
    low_n = 2 ** (bits // 2)
    high_n = 2**bits // low_n
    low, high = code % low_n, code // low_n

    def device(c):
        return {"grp": c // dev_count, "dev": c % dev_count}

    def beside(dx, dy):
        return device(morton_join((bx + dx + nx) % nx, (by + dy + ny) % ny, bits))

    def in_low(k):
        return device(high * low_n + (low + k) % low_n)

    def in_high(k):
        return device((high + k) % high_n * low_n + low)

    barrier = pltpu.get_barrier_semaphore()

    def greet(who):
        pl.semaphore_signal(barrier, inc=1, device_id=who, device_id_type=pl.DeviceIdType.MESH)

    def greet_low(k, carry):
        greet(in_low(k))
        return carry

    def greet_high(k, carry):
        greet(in_high(k))
        return carry

    lax.fori_loop(1, low_n, greet_low, 0)
    for dx, dy in DIRS:
        greet(beside(dx, dy))
    lax.fori_loop(1, high_n, greet_high, 0)

    starts = [qx * 2 + qy * 4 + sy for sy in (0, 1) for qx in (0, 1) for qy in (0, 1)]

    def turned(ref, lead, step):
        rows = jnp.concatenate(
            [ref[pl.ds(lead + step * s, 16, stride=8 * step), :] for s in starts], axis=0
        )
        return rows.T

    for arrival in arrivals[:4]:
        arrival.wait()
    row256 = lax.broadcasted_iota(jnp.int32, (256, 256), 0)
    pick = jnp.where(row256 == src_leaf[9:10, :], 1.0, 0.0).astype(BF16)
    linear = count[...].astype(F32).astype(BF16)
    counts = tn_none(linear[0:1], pick[0:128]) + tn_none(linear[1:2], pick[128:256])
    m_turned = turned(mass, 0, 1)
    slot = lax.broadcasted_iota(jnp.int32, (PPL, 128), 0).astype(F32)
    totals = []
    for tile in (0, 1):
        lanes = slice(tile * 128, tile * 128 + 128)
        live = slot < counts[:, lanes]
        vals = jnp.where(live, m_turned[tile * PPL : tile * PPL + PPL], 0.0)
        own[128:192, lanes] = vals
        totals.append(jnp.sum(vals, axis=0, keepdims=True))
    row = lax.broadcasted_iota(jnp.int32, (8, 128), 0)
    part[...] = jnp.where(
        row == 0,
        totals[0] + totals[1],
        jnp.where(row == 1, counts[:, 0:128] + counts[:, 128:256], 0.0),
    )

    def low_copy(k):
        return pltpu.make_async_remote_copy(
            src_ref=part, dst_ref=first.at[k], send_sem=sum_s1.at[k], recv_sem=sum_r1.at[k],
            device_id=in_low(k), device_id_type=pl.DeviceIdType.MESH,
        )

    def high_copy(k):
        return pltpu.make_async_remote_copy(
            src_ref=mid, dst_ref=second.at[k], send_sem=sum_s2.at[k], recv_sem=sum_r2.at[k],
            device_id=in_high(k), device_id_type=pl.DeviceIdType.MESH,
        )

    def start_low(k, carry):
        low_copy(k).start()
        return carry

    def start_high(k, carry):
        high_copy(k).start()
        return carry

    def add_low(k, acc):
        low_copy(k).wait()
        return acc + first[k]

    def add_high(k, acc):
        high_copy(k).wait()
        return acc + second[k]

    pl.semaphore_wait(barrier, 8 + low_n - 1 + high_n - 1)
    lax.fori_loop(1, low_n, start_low, 0)
    for k in (0, 1):
        vals = turned(pos, k, 2)
        own[k * PPL : (k + 1) * PPL, 0:128] = vals[:PPL]
        own[k * PPL : (k + 1) * PPL, 128:256] = vals[PPL:]

    for arrival in arrivals[4:]:
        arrival.wait()
    leaf_mom[...] = jnp.zeros_like(leaf_mom)
    for tile in (0, 1):
        lanes = slice(tile * 128, tile * 128 + 128)
        bu = basis(own[0:64, lanes])
        bv = basis(own[64:128, lanes])
        m_t = own[128:192, lanes]
        live_t = jnp.where(m_t > 0.0, 1.0, 0.0)
        for kind, weight in enumerate((m_t, live_t)):
            for a in range(NODES):
                wa = bu[a] * weight
                for b in range(NODES):
                    leaf_mom[pl.ds(kind * NM + a * 6 + b, 1), lanes] = jnp.sum(
                        wa * bv[b], axis=0, keepdims=True
                    )
    mom[...] = jnp.zeros_like(mom)
    stacked = []
    for kind in (0, 1):
        block = jnp.concatenate(
            [
                leaf_mom[kind * NM : (kind + 1) * NM, ch * 64 : ch * 64 + 64]
                for ch in range(4)
            ],
            axis=0,
        )
        mom[kind * 160 : kind * 160 + 160, 0:64] = block
        stacked.append(block)
    par = jnp.dot(
        up[...], jnp.concatenate(stacked, axis=1), precision=HIGHEST, preferred_element_type=F32
    )
    for kind in (0, 1):
        for q in range(4):
            at = kind * 64 + q * 16
            mom[pl.ds(kind * 160 + q * NM, NM), 64:80] = par[:, at : at + 16]
    own_cut = split3(own[...])
    send[:, 0:192] = nt_dot(
        jnp.concatenate([sel_leaf[...]] * 3, axis=1), jnp.concatenate(own_cut, axis=1)
    )
    send[:, 192:512] = nt_dot(
        jnp.concatenate([sel_mom[...]] * 3, axis=1),
        jnp.concatenate(split3(mom[...]), axis=1),
    )
    edges = []
    for d, (dx, dy) in enumerate(DIRS):
        rows = pl.ds(ROW_OF[d], ROWS_IN[d])
        copy = pltpu.make_async_remote_copy(
            src_ref=send.at[rows], dst_ref=recv.at[rows], send_sem=edge_s.at[d],
            recv_sem=edge_r.at[d], device_id=beside(-dx, -dy),
            device_id_type=pl.DeviceIdType.MESH,
        )
        copy.start()
        edges.append(copy)
    recv[96:HROWS, :] = jnp.zeros((HROWS - 96, LANES_OUT), F32)
    mid[...] = lax.fori_loop(1, low_n, add_low, part[...])
    lax.fori_loop(1, high_n, start_high, 0)

    def fill_tables(scale, table_hi, table_lo):
        def fill(i, carry):
            at = pl.multiple_of(i * 16, 16)
            rows = t_rows[pl.ds(at, 16), :]
            row_x, row_y = rows[:, 0:1] * scale, rows[:, 1:2] * scale
            cell_x, cell_y = rows[:, 2:3], rows[:, 3:4]
            for start in range(0, 1440, FILL_LANES):
                lanes = slice(start, min(start + FILL_LANES, 1440))
                dx = row_x - t_cols[0:1, lanes] * scale
                dy = row_y - t_cols[1:2, lanes] * scale
                gap = jnp.maximum(
                    jnp.abs(cell_x - t_cols[2:3, lanes]), jnp.abs(cell_y - t_cols[3:4, lanes])
                )
                x2 = dx * dx
                y2 = dy * dy
                inv = jnp.where(gap > 1.5, 1.0 / (x2 + y2 + SOFTEN), 0.0)
                kx = dx * inv
                ky = dy * inv
                for c, val in enumerate((kx, ky, ky * ky - kx * kx, -2.0 * kx * ky)):
                    hi, lo = split2(val)
                    table_hi[pl.ds(c * 160 + at, 16), lanes] = hi
                    table_lo[pl.ds(c * 160 + at, 16), lanes] = lo
            return carry

        lax.fori_loop(0, 10, fill, 0)

    fill_tables(2.0, hi_par, lo_par)
    fill_tables(1.0, hi_leaf, lo_leaf)

    def at_offset(o):
        return slice(o * PPL, o * PPL + PPL)

    own_parts = jnp.concatenate(own_cut, axis=1)

    def shift_own(o):
        hot = jnp.where(row256 == src_leaf[o : o + 1, :], 1.0, 0.0).astype(BF16)
        moved = tn_none(own_parts, jnp.concatenate([hot] * 3, axis=0))
        for tile in (0, 1):
            lanes = slice(tile * 128, tile * 128 + 128)
            su[tile, at_offset(o), :] = moved[0:64, lanes]
            sv[tile, at_offset(o), :] = moved[64:128, lanes]
            sw[tile, at_offset(o), :] = moved[128:192, lanes]

    for o in range(NEIGHBOURS):
        shift_own(o)
    sums = lax.fori_loop(1, high_n, add_high, mid[...])
    mass_sum = jnp.sum(sums[0:1], axis=1, keepdims=True)
    live_sum = jnp.sum(sums[1:2], axis=1, keepdims=True)
    mean = mass_sum / live_sum
    self_at = NEIGHBOURS * PPL
    for tile in (0, 1):
        lanes = slice(tile * 128, tile * 128 + 128)
        su[tile, self_at : self_at + PPL, :] = own[0:64, lanes] * 0.5
        sv[tile, self_at : self_at + PPL, :] = own[64:128, lanes] * 0.5
        m = own[128:192, lanes]
        sw[tile, self_at : self_at + PPL, :] = jnp.where(m > 0.0, m - mean, 0.0)

    def targets(tile, base, width):
        lanes = slice(tile * 128, tile * 128 + 128)
        tx = [own[base + 8 * i : base + 8 * i + 8, lanes] * 0.5 for i in range(width)]
        ty = [own[64 + base + 8 * i : 72 + base + 8 * i, lanes] * 0.5 for i in range(width)]
        return tx, ty

    def near_field(first_row, row_count, fresh):
        width, unroll = 4, 16
        zero = jnp.zeros((8, 128), F32)
        for tile in (0, 1):
            for piece in range(PPL // (8 * width)):
                base = piece * 8 * width
                tx, ty = targets(tile, base, width)

                def pairs(step, acc, tile=tile, tx=tx, ty=ty):
                    acc = list(acc)
                    for i in range(unroll):
                        at = pl.ds(first_row + step * unroll + i, 8, stride=0)
                        sx, sy, w = su[tile, at, :], sv[tile, at, :], sw[tile, at, :]
                        for t in range(width):
                            dx = tx[t] - sx
                            dy = ty[t] - sy
                            inv = 1.0 / (dy * dy + (dx * dx + SOFTEN))
                            kx = dx * inv
                            ky = dy * inv
                            wx = w * kx
                            wy = w * ky
                            acc[4 * t] = acc[4 * t] + wx
                            acc[4 * t + 1] = acc[4 * t + 1] + wy
                            acc[4 * t + 2] = (acc[4 * t + 2] + wy * ky) - wx * kx
                            acc[4 * t + 3] = acc[4 * t + 3] + wx * ky
                    return tuple(acc)

                acc = lax.fori_loop(0, row_count // unroll, pairs, (zero,) * (4 * width))
                for t in range(width):
                    rows = slice(tile * PPL + base + 8 * t, tile * PPL + base + 8 * t + 8)
                    for c in range(4):
                        near = acc[4 * t + c]
                        if c == 3:
                            near = near * -2.0
                        result[c, rows, :] = near if fresh else result[c, rows, :] + near

    near_field(self_at, PPL, True)

    for copy in edges:
        copy.wait()
    cell_x = sides[0:1] + jnp.full((1, 128), bx, jnp.int32).astype(F32)
    cell_y = sides[1:2] + jnp.full((1, 128), by, jnp.int32).astype(F32)
    inside = jnp.where(
        (cell_x >= 0.0) & (cell_x < float(nx)) & (cell_y >= 0.0) & (cell_y < float(ny)), 1.0, 0.0
    )
    halo = recv[...].T * inside
    halo_parts = jnp.concatenate(split3(halo[0:192]), axis=1)
    row128 = lax.broadcasted_iota(jnp.int32, (128, 256), 0) + 256

    def shift_halo(o):
        hot = jnp.where(row128 == src_leaf[o : o + 1, :], 1.0, 0.0).astype(BF16)
        moved = tn_none(halo_parts, jnp.concatenate([hot] * 3, axis=0))
        off_x, off_y = OFFS[o]
        for tile in (0, 1):
            lanes = slice(tile * 128, tile * 128 + 128)
            at = at_offset(o)
            su[tile, at, :] = (su[tile, at, :] + moved[0:64, lanes]) * 0.5 + off_x
            sv[tile, at, :] = (sv[tile, at, :] + moved[64:128, lanes]) * 0.5 + off_y
            m = sw[tile, at, :] + moved[128:192, lanes]
            sw[tile, at, :] = jnp.where(m > 0.0, m - mean, 0.0)

    for o in range(NEIGHBOURS):
        shift_halo(o)

    all_mom = jnp.concatenate([mom[...], halo[192:512]], axis=1)
    all_mom = all_mom[0:160] - mean * all_mom[160:320]
    cut_mom = jnp.concatenate(split2(all_mom), axis=0)

    def shift_moments(o):
        hot = jnp.where(row256[:, 0:128] == src_mom[o : o + 1, :], 1.0, 0.0).astype(BF16)
        moved = tn_none(cut_mom, hot).astype(BF16)
        xs[o * 160 : o * 160 + 160, 0:128] = moved[0:160]
        xs[o * 160 : o * 160 + 160, 128:256] = moved[160:320]

    for o in range(9):
        shift_moments(o)

    def far(table_hi, table_lo):
        wide = tn_none(table_hi[...], xs[...])
        return wide[:, 0:128] + wide[:, 128:256] + tn_none(table_lo[...], xs[:, 0:128])

    par = far(hi_par, lo_par)
    par_cols = jnp.concatenate(
        [
            jnp.concatenate(
                [par[c * 160 + q * NM : c * 160 + q * NM + NM, 64:80] for q in range(4)], axis=1
            )
            for c in range(4)
        ],
        axis=1,
    )
    from_par = jnp.dot(
        down[...], par_cols, precision=HIGHEST, preferred_element_type=F32
    )
    leaf = far(hi_leaf, lo_leaf)
    for c in range(4):
        leaf_local[c] = jnp.concatenate(
            [
                leaf[c * 160 + ch * NM : c * 160 + ch * NM + NM, 0:64]
                + from_par[ch * NM : ch * NM + NM, c * 64 : c * 64 + 64]
                for ch in range(4)
            ],
            axis=1,
        )

    for tile in (0, 1):
        lanes = slice(tile * 128, tile * 128 + 128)
        bu = basis(own[0:64, lanes])
        bv = basis(own[64:128, lanes])
        for c in range(4):
            rows = slice(tile * PPL, tile * PPL + PPL)
            acc = result[c, rows, :]
            for a in range(NODES):
                half = leaf_local[c, pl.ds(a * 6, 1), lanes] * bv[0]
                for b in range(1, NODES):
                    half = half + leaf_local[c, pl.ds(a * 6 + b, 1), lanes] * bv[b]
                acc = acc + half * bu[a]
            result[c, rows, :] = acc

    near_field(0, self_at, False)

    for c in range(4):
        back = result[c].T
        for i, s in enumerate(starts):
            out[pl.ds(s * 4 + c, 16, stride=32), :] = back[16 * i : 16 * i + 16]


def vmem():
    return pl.BlockSpec(memory_space=pltpu.VMEM)


NAMES = ("src_leaf", "sel_leaf", "sel_mom", "up", "t_rows", "t_cols", "sides", "src_mom", "down")
OPERANDS = 3 + len(NAMES)


def on_device(particle_pos, particle_mass, leaf_counts):
    dev_count = lax.axis_size("dev")
    bits = (lax.axis_size("grp") * dev_count).bit_length() - 1
    low_n = 2 ** (bits // 2)
    high_n = 2**bits // low_n
    pos = particle_pos.reshape(2, 128, 128).transpose(1, 0, 2).reshape(256, 128)
    mass = particle_mass.reshape(128, 128)
    count = leaf_counts.reshape(2, 128)
    operands = (pos, mass, count, *[jnp.asarray(CONST[k]) for k in NAMES])
    out = pl.pallas_call(
        functools.partial(whole_kernel, dev_count, bits),
        out_shape=jax.ShapeDtypeStruct((512, 128), F32),
        in_specs=[pl.BlockSpec(memory_space=pltpu.HBM)] * OPERANDS,
        out_specs=vmem(),
        scratch_shapes=[pltpu.VMEM(x.shape, x.dtype) for x in operands]
        + [
            pltpu.SemaphoreType.DMA((OPERANDS,)),
            pltpu.VMEM((192, 256), F32),
            pltpu.VMEM((320, 128), F32),
            pltpu.VMEM((HROWS, LANES_OUT), F32),
            pltpu.VMEM((HROWS, LANES_OUT), F32),
            pltpu.VMEM((8, 128), F32),
            pltpu.VMEM((8, 128), F32),
            pltpu.VMEM((2 * NM, 256), F32),
            pltpu.VMEM((low_n, 8, 128), F32),
            pltpu.VMEM((high_n, 8, 128), F32),
            pltpu.VMEM((2, 9 * PPL + 8, 128), F32),
            pltpu.VMEM((2, 9 * PPL + 8, 128), F32),
            pltpu.VMEM((2, 9 * PPL + 8, 128), F32),
            pltpu.VMEM((1440, 256), BF16),
            pltpu.VMEM((640, 1440), BF16),
            pltpu.VMEM((640, 1440), BF16),
            pltpu.VMEM((640, 1440), BF16),
            pltpu.VMEM((640, 1440), BF16),
            pltpu.VMEM((4, NM, 256), F32),
            pltpu.VMEM((4, 128, 128), F32),
            pltpu.SemaphoreType.DMA((8,)),
            pltpu.SemaphoreType.DMA((8,)),
            pltpu.SemaphoreType.DMA((low_n,)),
            pltpu.SemaphoreType.DMA((low_n,)),
            pltpu.SemaphoreType.DMA((high_n,)),
            pltpu.SemaphoreType.DMA((high_n,)),
        ],
        compiler_params=pltpu.CompilerParams(
            collective_id=0, has_side_effects=True, vmem_limit_bytes=63 * 2**20
        ),
        name="fields",
    )(*operands)
    return out.reshape(128, 4, 128).transpose(1, 0, 2).reshape(4, LSIDE * LSIDE * PPL)


def solution(mesh):
    in_specs = (P(None, ("grp", "dev")), P(("grp", "dev")), P(("grp", "dev")))
    out_specs = P(None, ("grp", "dev"))
    return jax.shard_map(
        on_device, mesh=mesh, in_specs=in_specs, out_specs=out_specs, check_vma=False
    )
```

```python
import functools

import jax
import jax.numpy as jnp
import numpy as np
from jax import lax
from jax.experimental import pallas as pl
from jax.experimental.pallas import tpu as pltpu
from jax.sharding import PartitionSpec as P

NODES = 6
PPL = 64
LSIDE = 16
SOFTEN = 0.01
NM = 40
HIGHEST = lax.Precision.HIGHEST
F32 = jnp.float32
BF16 = jnp.bfloat16

DIRS = ((-1, 0), (1, 0), (0, -1), (0, 1), (-1, -1), (1, -1), (-1, 1), (1, 1))
ROW_OF = (0, 16, 32, 48, 64, 72, 80, 88)
ROWS_IN = (16, 16, 16, 16, 8, 8, 8, 8)
HROWS = 128
LANES_OUT = 512
OFFS = tuple((ox, oy) for ox in (-1, 0, 1) for oy in (-1, 0, 1) if (ox, oy) != (0, 0)) + ((0, 0),)
NEIGHBOURS = 8
FILL_LANES = 256


def gp_col(gx, gy):
    return (gx & 1) + 2 * (gy & 1) + 4 * (gx >> 1) + 8 * (gy >> 1)


def par_col(px, py):
    return (px & 1) * 32 + (py & 1) * 16 + gp_col(px >> 1, py >> 1)


def leaf_col(x, y):
    return (x & 1) * 128 + (y & 1) * 64 + par_col(x >> 1, y >> 1)


def halo_cells(side):
    cells = []
    for dx, dy in DIRS:
        ex = -1 if dx < 0 else side
        ey = -1 if dy < 0 else side
        if dy == 0:
            cells.append([(ex, j) for j in range(side)])
        elif dx == 0:
            cells.append([(j, ey) for j in range(side)])
        else:
            cells.append([(ex, ey)])
    return cells


def pick_rows(side, col, base, lanes):
    out = np.zeros((HROWS, lanes), np.float32)
    for d, cells in enumerate(halo_cells(side)):
        for j, (cx, cy) in enumerate(cells):
            out[ROW_OF[d] + base[d] + j, col(cx % side, cy % side)] = 1.0
    return out


PAR_BASE = (0,) * 8
GP_BASE = (8,) * 4 + (1,) * 4


def shift_index(side, col, base, own_at, halo_at):
    where = {}
    for x in range(side):
        for y in range(side):
            where[x, y] = own_at + col(x, y)
    for d, cells in enumerate(halo_cells(side)):
        for j, cell in enumerate(cells):
            where[cell] = halo_at + ROW_OF[d] + base[d] + j
    out = np.zeros((9, side * side), np.int32)
    for o, (ox, oy) in enumerate(OFFS):
        for x in range(side):
            for y in range(side):
                out[o, col(x, y)] = where[x + ox, y + oy]
    return out


def cheb(u):
    terms = [u * 0 + 1.0, u]
    for _ in range(NODES - 2):
        terms.append(2.0 * u * terms[-1] - terms[-2])
    return terms


ANGLES = (2.0 * np.arange(NODES) + 1.0) * np.pi / (2.0 * NODES)
POINTS = np.cos(ANGLES)
S_COEF = 2.0 / NODES * np.cos(np.arange(NODES)[:, None] * ANGLES[None, :])
S_COEF[0] = 1.0 / NODES


def basis(u):
    terms = cheb(u)
    out = []
    for k in range(NODES):
        total = S_COEF[0, k] + float(S_COEF[1, k]) * terms[1]
        for n in range(2, NODES):
            total = total + float(S_COEF[n, k]) * terms[n]
        out.append(total)
    return out


def child_table():
    side = []
    for s in (0, 1):
        side.append(np.stack(basis(s - 0.5 + POINTS / 2), axis=1))
    out = np.zeros((4, NM, NM), np.float32)
    for sx in (0, 1):
        for sy in (0, 1):
            prod = side[sx][:, None, :, None] * side[sy][None, :, None, :]
            out[2 * sx + sy, :36, :36] = prod.reshape(36, 36)
    return out


def cell_vectors():
    coord = np.zeros((2, 4, NM), np.float32)
    cell = np.zeros((2, 4, NM), np.float32)
    for sx in (0, 1):
        for sy in (0, 1):
            ch = 2 * sx + sy
            node = np.arange(36)
            coord[0, ch] = sx - 0.5
            coord[1, ch] = sy - 0.5
            coord[0, ch, :36] += 0.5 * POINTS[node // 6]
            coord[1, ch, :36] += 0.5 * POINTS[node % 6]
            cell[0, ch] = sx
            cell[1, ch] = sy
    return coord.reshape(2, 4 * NM), cell.reshape(2, 4 * NM)


def constants():
    c = {}
    c["sel_leaf"] = pick_rows(LSIDE, leaf_col, PAR_BASE, 256).astype(BF16)
    sel_par = pick_rows(LSIDE // 2, par_col, PAR_BASE, 64)
    sel_gp = pick_rows(LSIDE // 4, gp_col, GP_BASE, 64)
    c["sel_mom"] = np.concatenate([sel_par, sel_gp], axis=1).astype(BF16)
    table = child_table()
    c["up"] = np.transpose(table, (2, 0, 1)).reshape(NM, 4 * NM)
    c["down"] = table.reshape(4 * NM, NM)
    src = np.zeros((16, 256), np.int32)
    src[:9] = shift_index(LSIDE, leaf_col, PAR_BASE, 0, 256)
    for x in range(LSIDE):
        for y in range(LSIDE):
            src[9, leaf_col(x, y)] = sum(
                (x >> k & 1) << 2 * k | (y >> k & 1) << 2 * k + 1 for k in range(4)
            )
    c["src_leaf"] = src
    msrc = np.full((16, 128), -1, np.int32)
    msrc[:9, :64] = shift_index(LSIDE // 2, par_col, PAR_BASE, 0, 128)
    msrc[:9, 64:80] = shift_index(LSIDE // 4, gp_col, GP_BASE, 64, 128)
    c["src_mom"] = msrc
    coord, cell = cell_vectors()
    rows = np.zeros((160, 128), np.float32)
    rows[:, 0:2] = coord.T
    rows[:, 2:4] = cell.T
    c["t_rows"] = rows
    cols = np.zeros((8, 9, 160), np.float32)
    for o, (ox, oy) in enumerate(OFFS):
        cols[0, o] = coord[0] + 2 * ox
        cols[1, o] = coord[1] + 2 * oy
        cols[2, o] = cell[0] + 2 * ox
        cols[3, o] = cell[1] + 2 * oy
    c["t_cols"] = cols.reshape(8, 1440)
    sides = np.zeros((8, HROWS), np.float32)
    for d, (dx, dy) in enumerate(DIRS):
        sides[0, ROW_OF[d] : ROW_OF[d] + ROWS_IN[d]] = dx
        sides[1, ROW_OF[d] : ROW_OF[d] + ROWS_IN[d]] = dy
    c["sides"] = sides
    return c


CONST = constants()


def split2(x):
    hi = x.astype(BF16)
    return hi, (x - hi.astype(F32)).astype(BF16)


def split3(x):
    hi = x.astype(BF16)
    rest = x - hi.astype(F32)
    mid = rest.astype(BF16)
    return hi, mid, (rest - mid.astype(F32)).astype(BF16)


def nt_dot(a, b):
    return lax.dot_general(a, b, (((1,), (1,)), ((), ())), preferred_element_type=F32)


def tn_none(a, b):
    return lax.dot_general(a, b, (((1,), (0,)), ((), ())), preferred_element_type=F32)


def morton_split(code, bits):
    cx, cy = 0, 0
    for level in range((bits + 1) // 2):
        cx = cx + code // 4**level % 2 * 2**level
        cy = cy + code // (2 * 4**level) % 2 * 2**level
    return cx, cy


def morton_join(cx, cy, bits):
    code = 0
    for level in range((bits + 1) // 2):
        code = code + cx // 2**level % 2 * 4**level
        code = code + cy // 2**level % 2 * 2 * 4**level
    return code


def whole_kernel(dev_count, bits, *refs):
    sources, refs = refs[:OPERANDS], refs[OPERANDS:]
    out, refs = refs[0], refs[1:]
    held, refs = refs[:OPERANDS], refs[OPERANDS:]
    (pos, mass, count, src_leaf, sel_leaf, sel_mom, up, t_rows, t_cols, sides, src_mom,
     down) = held
    arrive_sems = refs[0]
    arrivals = [
        pltpu.make_async_copy(src, dst, arrive_sems.at[i])
        for i, (src, dst) in enumerate(zip(sources, held))
    ]
    for i in (1, 2, 3, 0, *range(4, OPERANDS)):
        arrivals[i].start()
    run_kernel(dev_count, bits, arrivals, pos, mass, count, sel_leaf, sel_mom, up, down, sides,
               src_leaf, src_mom, t_rows, t_cols, out, *refs[1:])


def run_kernel(dev_count, bits, arrivals, pos, mass, count, sel_leaf, sel_mom, up, down, sides,
               src_leaf, src_mom, t_rows, t_cols, out, own, mom, send, recv, part, mid, leaf_mom, first,
                 second, su, sv, sw, xs, xs_par, hi_leaf, lo_leaf, hi_par, lo_par, leaf_kind, leaf_local,
                 result, edge_s, edge_r, sum_s1, sum_r1, sum_s2, sum_r2):
    code = lax.axis_index("grp") * dev_count + lax.axis_index("dev")
    bx, by = morton_split(code, bits)
    nx, ny = 2 ** ((bits + 1) // 2), 2 ** (bits // 2)
    low_n = 2 ** (bits // 2)
    high_n = 2**bits // low_n
    low, high = code % low_n, code // low_n

    def device(c):
        return {"grp": c // dev_count, "dev": c % dev_count}

    def beside(dx, dy):
        return device(morton_join((bx + dx + nx) % nx, (by + dy + ny) % ny, bits))

    def in_low(k):
        return device(high * low_n + (low + k) % low_n)

    def in_high(k):
        return device((high + k) % high_n * low_n + low)

    barrier = pltpu.get_barrier_semaphore()

    def greet(who):
        pl.semaphore_signal(barrier, inc=1, device_id=who, device_id_type=pl.DeviceIdType.MESH)

    def greet_low(k, carry):
        greet(in_low(k))
        return carry

    def greet_high(k, carry):
        greet(in_high(k))
        return carry

    lax.fori_loop(1, low_n, greet_low, 0)
    for dx, dy in DIRS:
        greet(beside(dx, dy))
    lax.fori_loop(1, high_n, greet_high, 0)

    starts = [qx * 2 + qy * 4 + sy for sy in (0, 1) for qx in (0, 1) for qy in (0, 1)]

    def turned(ref, lead, step):
        rows = jnp.concatenate(
            [ref[pl.ds(lead + step * s, 16, stride=8 * step), :] for s in starts], axis=0
        )
        return rows.T

    for arrival in arrivals[1:4]:
        arrival.wait()
    row256 = lax.broadcasted_iota(jnp.int32, (256, 256), 0)
    pick = jnp.where(row256 == src_leaf[9:10, :], 1.0, 0.0).astype(BF16)
    linear = count[...].astype(F32).astype(BF16)
    counts = tn_none(linear[0:1], pick[0:128]) + tn_none(linear[1:2], pick[128:256])
    m_turned = turned(mass, 0, 1)
    slot = lax.broadcasted_iota(jnp.int32, (PPL, 128), 0).astype(F32)
    totals = []
    for tile in (0, 1):
        lanes = slice(tile * 128, tile * 128 + 128)
        live = slot < counts[:, lanes]
        vals = jnp.where(live, m_turned[tile * PPL : tile * PPL + PPL], 0.0)
        own[128:192, lanes] = vals
        totals.append(jnp.sum(vals, axis=0, keepdims=True))
    near_mean = jnp.sum(totals[0] + totals[1], axis=1, keepdims=True) / jnp.sum(
        counts, axis=1, keepdims=True
    )
    row = lax.broadcasted_iota(jnp.int32, (8, 128), 0)
    part[...] = jnp.where(
        row == 0,
        totals[0] + totals[1],
        jnp.where(row == 1, counts[:, 0:128] + counts[:, 128:256], 0.0),
    )

    def low_copy(k):
        return pltpu.make_async_remote_copy(
            src_ref=part, dst_ref=first.at[k], send_sem=sum_s1.at[k], recv_sem=sum_r1.at[k],
            device_id=in_low(k), device_id_type=pl.DeviceIdType.MESH,
        )

    def high_copy(k):
        return pltpu.make_async_remote_copy(
            src_ref=mid, dst_ref=second.at[k], send_sem=sum_s2.at[k], recv_sem=sum_r2.at[k],
            device_id=in_high(k), device_id_type=pl.DeviceIdType.MESH,
        )

    def start_low(k, carry):
        low_copy(k).start()
        return carry

    def start_high(k, carry):
        high_copy(k).start()
        return carry

    def add_low(k, acc):
        low_copy(k).wait()
        return acc + first[k]

    def add_high(k, acc):
        high_copy(k).wait()
        return acc + second[k]

    pl.semaphore_wait(barrier, 8 + low_n - 1 + high_n - 1)
    lax.fori_loop(1, low_n, start_low, 0)
    arrivals[0].wait()
    for k in (0, 1):
        vals = turned(pos, k, 2)
        own[k * PPL : (k + 1) * PPL, 0:128] = vals[:PPL]
        own[k * PPL : (k + 1) * PPL, 128:256] = vals[PPL:]

    for arrival in arrivals[4:]:
        arrival.wait()
    leaf_mom[...] = jnp.zeros_like(leaf_mom)
    for tile in (0, 1):
        lanes = slice(tile * 128, tile * 128 + 128)
        bu = basis(own[0:64, lanes])
        bv = basis(own[64:128, lanes])
        m_t = own[128:192, lanes]
        live_t = jnp.where(m_t > 0.0, 1.0, 0.0)
        for kind, weight in enumerate((m_t, live_t)):
            for a in range(NODES):
                wa = bu[a] * weight
                for b in range(NODES):
                    leaf_mom[pl.ds(kind * NM + a * 6 + b, 1), lanes] = jnp.sum(
                        wa * bv[b], axis=0, keepdims=True
                    )
    mom[...] = jnp.zeros_like(mom)
    stacked = []
    for kind in (0, 1):
        block = jnp.concatenate(
            [
                leaf_mom[kind * NM : (kind + 1) * NM, ch * 64 : ch * 64 + 64]
                for ch in range(4)
            ],
            axis=0,
        )
        mom[kind * 160 : kind * 160 + 160, 0:64] = block
        stacked.append(block)
    par = jnp.dot(
        up[...], jnp.concatenate(stacked, axis=1), precision=HIGHEST, preferred_element_type=F32
    )
    for kind in (0, 1):
        for q in range(4):
            at = kind * 64 + q * 16
            mom[pl.ds(kind * 160 + q * NM, NM), 64:80] = par[:, at : at + 16]
    own_cut = split3(own[...])
    send[:, 0:192] = nt_dot(
        jnp.concatenate([sel_leaf[...]] * 3, axis=1), jnp.concatenate(own_cut, axis=1)
    )
    send[:, 192:512] = nt_dot(
        jnp.concatenate([sel_mom[...]] * 3, axis=1),
        jnp.concatenate(split3(mom[...]), axis=1),
    )
    edges = []
    for d, (dx, dy) in enumerate(DIRS):
        rows = pl.ds(ROW_OF[d], ROWS_IN[d])
        copy = pltpu.make_async_remote_copy(
            src_ref=send.at[rows], dst_ref=recv.at[rows], send_sem=edge_s.at[d],
            recv_sem=edge_r.at[d], device_id=beside(-dx, -dy),
            device_id_type=pl.DeviceIdType.MESH,
        )
        copy.start()
        edges.append(copy)
    recv[96:HROWS, :] = jnp.zeros((HROWS - 96, LANES_OUT), F32)
    mid[...] = lax.fori_loop(1, low_n, add_low, part[...])
    lax.fori_loop(1, high_n, start_high, 0)

    def fill_tables(scale, table_hi, table_lo):
        def fill(i, carry):
            at = pl.multiple_of(i * 16, 16)
            rows = t_rows[pl.ds(at, 16), :]
            row_x, row_y = rows[:, 0:1] * scale, rows[:, 1:2] * scale
            cell_x, cell_y = rows[:, 2:3], rows[:, 3:4]
            for start in range(0, 1440, FILL_LANES):
                lanes = slice(start, min(start + FILL_LANES, 1440))
                dx = row_x - t_cols[0:1, lanes] * scale
                dy = row_y - t_cols[1:2, lanes] * scale
                gap = jnp.maximum(
                    jnp.abs(cell_x - t_cols[2:3, lanes]), jnp.abs(cell_y - t_cols[3:4, lanes])
                )
                x2 = dx * dx
                y2 = dy * dy
                inv = jnp.where(gap > 1.5, 1.0 / (x2 + y2 + SOFTEN), 0.0)
                kx = dx * inv
                ky = dy * inv
                for c, val in enumerate((kx, ky, ky * ky - kx * kx, -2.0 * kx * ky)):
                    hi, lo = split2(val)
                    table_hi[pl.ds(c * 160 + at, 16), lanes] = hi
                    table_lo[pl.ds(c * 160 + at, 16), lanes] = lo
            return carry

        lax.fori_loop(0, 10, fill, 0)

    fill_tables(2.0, hi_par, lo_par)
    fill_tables(1.0, hi_leaf, lo_leaf)

    def at_offset(o):
        return slice(o * PPL, o * PPL + PPL)

    own_parts = jnp.concatenate(own_cut, axis=1)

    def shift_own(o):
        hot = jnp.where(row256 == src_leaf[o : o + 1, :], 1.0, 0.0).astype(BF16)
        moved = tn_none(own_parts, jnp.concatenate([hot] * 3, axis=0))
        for tile in (0, 1):
            lanes = slice(tile * 128, tile * 128 + 128)
            su[tile, at_offset(o), :] = moved[0:64, lanes]
            sv[tile, at_offset(o), :] = moved[64:128, lanes]
            sw[tile, at_offset(o), :] = moved[128:192, lanes]

    for o in range(NEIGHBOURS):
        shift_own(o)
    self_at = NEIGHBOURS * PPL
    for tile in (0, 1):
        lanes = slice(tile * 128, tile * 128 + 128)
        su[tile, self_at : self_at + PPL, :] = own[0:64, lanes] * 0.5
        sv[tile, self_at : self_at + PPL, :] = own[64:128, lanes] * 0.5
        sw[tile, self_at : self_at + PPL, :] = own[128:192, lanes]

    def targets(tile, base, width):
        lanes = slice(tile * 128, tile * 128 + 128)
        tx = [own[base + 8 * i : base + 8 * i + 8, lanes] * 0.5 for i in range(width)]
        ty = [own[64 + base + 8 * i : 72 + base + 8 * i, lanes] * 0.5 for i in range(width)]
        return tx, ty

    def near_field(first_row, row_count):
        width, unroll = 4, 16
        zero = jnp.zeros((8, 128), F32)
        for tile in (0, 1):
            for piece in range(PPL // (8 * width)):
                base = piece * 8 * width
                tx, ty = targets(tile, base, width)

                def pairs(step, acc, tile=tile, tx=tx, ty=ty):
                    acc = list(acc)
                    for i in range(unroll):
                        at = pl.ds(first_row + step * unroll + i, 8, stride=0)
                        sx, sy, w = su[tile, at, :], sv[tile, at, :], sw[tile, at, :]
                        for t in range(width):
                            dx = tx[t] - sx
                            dy = ty[t] - sy
                            inv = 1.0 / (dy * dy + (dx * dx + SOFTEN))
                            kx = dx * inv
                            ky = dy * inv
                            wx = w * kx
                            wy = w * ky
                            acc[4 * t] = acc[4 * t] + wx
                            acc[4 * t + 1] = acc[4 * t + 1] + wy
                            acc[4 * t + 2] = (acc[4 * t + 2] + wy * ky) - wx * kx
                            acc[4 * t + 3] = acc[4 * t + 3] + wx * ky
                    return tuple(acc)

                acc = lax.fori_loop(0, row_count // unroll, pairs, (zero,) * (4 * width))
                for t in range(width):
                    rows = slice(tile * PPL + base + 8 * t, tile * PPL + base + 8 * t + 8)
                    for c in range(4):
                        near = acc[4 * t + c]
                        if c == 3:
                            near = near * -2.0
                        result[c, rows, :] = result[c, rows, :] + near

    for copy in edges:
        copy.wait()
    cell_x = sides[0:1] + jnp.full((1, 128), bx, jnp.int32).astype(F32)
    cell_y = sides[1:2] + jnp.full((1, 128), by, jnp.int32).astype(F32)
    inside = jnp.where(
        (cell_x >= 0.0) & (cell_x < float(nx)) & (cell_y >= 0.0) & (cell_y < float(ny)), 1.0, 0.0
    )
    halo = recv[...].T * inside
    halo_parts = jnp.concatenate(split3(halo[0:192]), axis=1)
    row128 = lax.broadcasted_iota(jnp.int32, (128, 256), 0) + 256

    def shift_halo(o):
        hot = jnp.where(row128 == src_leaf[o : o + 1, :], 1.0, 0.0).astype(BF16)
        moved = tn_none(halo_parts, jnp.concatenate([hot] * 3, axis=0))
        off_x, off_y = OFFS[o]
        for tile in (0, 1):
            lanes = slice(tile * 128, tile * 128 + 128)
            at = at_offset(o)
            su[tile, at, :] = (su[tile, at, :] + moved[0:64, lanes]) * 0.5 + off_x
            sv[tile, at, :] = (sv[tile, at, :] + moved[64:128, lanes]) * 0.5 + off_y
            sw[tile, at, :] = sw[tile, at, :] + moved[128:192, lanes]

    for o in range(NEIGHBOURS):
        shift_halo(o)

    all_mom = jnp.concatenate([mom[...], halo[192:512]], axis=1)
    all_mom = jnp.concatenate(
        [all_mom[0:160] - near_mean * all_mom[160:320], all_mom[160:320]], axis=0
    )
    cut_mom = jnp.concatenate(split2(all_mom), axis=0)

    def shift_moments(o):
        hot = jnp.where(row256[:, 0:128] == src_mom[o : o + 1, :], 1.0, 0.0).astype(BF16)
        moved = tn_none(cut_mom, hot)
        at = slice(o * 160, o * 160 + 160)
        pieces = [moved[160 * i : 160 * i + 160] for i in range(4)]
        xs[at, :] = jnp.concatenate([p[:, 0:64] for p in pieces], axis=1).astype(BF16)
        xs_par[at, :] = jnp.concatenate([p[:, 64:80] for p in pieces], axis=1).astype(BF16)

    for o in range(9):
        shift_moments(o)

    wide = tn_none(hi_par[...], xs_par[...])
    par = wide[:, 0:32] + wide[:, 32:64] + tn_none(lo_par[...], xs_par[:, 0:32])
    par_cols = jnp.concatenate(
        [
            par[c * 160 + q * NM : c * 160 + q * NM + NM, kind * 16 : kind * 16 + 16]
            for kind in (0, 1)
            for c in range(4)
            for q in range(4)
        ],
        axis=1,
    )
    from_par = jnp.dot(
        down[...], par_cols, precision=HIGHEST, preferred_element_type=F32
    )
    wide = tn_none(hi_leaf[...], xs[...])
    leaf = wide[:, 0:128] + wide[:, 128:256] + tn_none(lo_leaf[...], xs[:, 0:128])
    for kind in (0, 1):
        for c in range(4):
            at = kind * 256 + c * 64
            leaf_kind[kind, c] = jnp.concatenate(
                [
                    leaf[c * 160 + ch * NM : c * 160 + ch * NM + NM, kind * 64 : kind * 64 + 64]
                    + from_par[ch * NM : ch * NM + NM, at : at + 64]
                    for ch in range(4)
                ],
                axis=1,
            )

    sums = lax.fori_loop(1, high_n, add_high, mid[...])
    mass_sum = jnp.sum(sums[0:1], axis=1, keepdims=True)
    live_sum = jnp.sum(sums[1:2], axis=1, keepdims=True)
    mean = mass_sum / live_sum
    for tile in (0, 1):
        m = sw[tile, 0 : 9 * PPL, :]
        sw[tile, 0 : 9 * PPL, :] = jnp.where(m > 0.0, m - mean, 0.0)
    for c in range(4):
        leaf_local[c] = leaf_kind[0, c] - (mean - near_mean) * leaf_kind[1, c]

    for tile in (0, 1):
        lanes = slice(tile * 128, tile * 128 + 128)
        bu = basis(own[0:64, lanes])
        bv = basis(own[64:128, lanes])
        for c in range(4):
            rows = slice(tile * PPL, tile * PPL + PPL)
            acc = None
            for a in range(NODES):
                half = leaf_local[c, pl.ds(a * 6, 1), lanes] * bv[0]
                for b in range(1, NODES):
                    half = half + leaf_local[c, pl.ds(a * 6 + b, 1), lanes] * bv[b]
                acc = half * bu[a] if acc is None else acc + half * bu[a]
            result[c, rows, :] = acc

    near_field(0, 9 * PPL)

    for c in range(4):
        back = result[c].T
        for i, s in enumerate(starts):
            out[pl.ds(s * 4 + c, 16, stride=32), :] = back[16 * i : 16 * i + 16]


def vmem():
    return pl.BlockSpec(memory_space=pltpu.VMEM)


NAMES = ("src_leaf", "sel_leaf", "sel_mom", "up", "t_rows", "t_cols", "sides", "src_mom", "down")
OPERANDS = 3 + len(NAMES)


def on_device(particle_pos, particle_mass, leaf_counts):
    dev_count = lax.axis_size("dev")
    bits = (lax.axis_size("grp") * dev_count).bit_length() - 1
    low_n = 2 ** (bits // 2)
    high_n = 2**bits // low_n
    pos = particle_pos.reshape(2, 128, 128).transpose(1, 0, 2).reshape(256, 128)
    mass = particle_mass.reshape(128, 128)
    count = leaf_counts.reshape(2, 128)
    operands = (pos, mass, count, *[jnp.asarray(CONST[k]) for k in NAMES])
    out = pl.pallas_call(
        functools.partial(whole_kernel, dev_count, bits),
        out_shape=jax.ShapeDtypeStruct((512, 128), F32),
        in_specs=[pl.BlockSpec(memory_space=pltpu.HBM)] * OPERANDS,
        out_specs=vmem(),
        scratch_shapes=[pltpu.VMEM(x.shape, x.dtype) for x in operands]
        + [
            pltpu.SemaphoreType.DMA((OPERANDS,)),
            pltpu.VMEM((192, 256), F32),
            pltpu.VMEM((320, 128), F32),
            pltpu.VMEM((HROWS, LANES_OUT), F32),
            pltpu.VMEM((HROWS, LANES_OUT), F32),
            pltpu.VMEM((8, 128), F32),
            pltpu.VMEM((8, 128), F32),
            pltpu.VMEM((2 * NM, 256), F32),
            pltpu.VMEM((low_n, 8, 128), F32),
            pltpu.VMEM((high_n, 8, 128), F32),
            pltpu.VMEM((2, 9 * PPL + 8, 128), F32),
            pltpu.VMEM((2, 9 * PPL + 8, 128), F32),
            pltpu.VMEM((2, 9 * PPL + 8, 128), F32),
            pltpu.VMEM((1440, 256), BF16),
            pltpu.VMEM((1440, 64), BF16),
            pltpu.VMEM((640, 1440), BF16),
            pltpu.VMEM((640, 1440), BF16),
            pltpu.VMEM((640, 1440), BF16),
            pltpu.VMEM((640, 1440), BF16),
            pltpu.VMEM((2, 4, NM, 256), F32),
            pltpu.VMEM((4, NM, 256), F32),
            pltpu.VMEM((4, 128, 128), F32),
            pltpu.SemaphoreType.DMA((8,)),
            pltpu.SemaphoreType.DMA((8,)),
            pltpu.SemaphoreType.DMA((low_n,)),
            pltpu.SemaphoreType.DMA((low_n,)),
            pltpu.SemaphoreType.DMA((high_n,)),
            pltpu.SemaphoreType.DMA((high_n,)),
        ],
        compiler_params=pltpu.CompilerParams(
            collective_id=0, has_side_effects=True, vmem_limit_bytes=63 * 2**20
        ),
        name="fields",
    )(*operands)
    return out.reshape(128, 4, 128).transpose(1, 0, 2).reshape(4, LSIDE * LSIDE * PPL)


def solution(mesh):
    in_specs = (P(None, ("grp", "dev")), P(("grp", "dev")), P(("grp", "dev")))
    out_specs = P(None, ("grp", "dev"))
    return jax.shard_map(
        on_device, mesh=mesh, in_specs=in_specs, out_specs=out_specs, check_vma=False
    )
```

```python
import functools

import jax
import jax.numpy as jnp
import numpy as np
from jax import lax
from jax.experimental import pallas as pl
from jax.experimental.pallas import tpu as pltpu
from jax.sharding import PartitionSpec as P

NODES = 6
PPL = 64
LSIDE = 16
SOFTEN = 0.01
NM = 40
HIGHEST = lax.Precision.HIGHEST
F32 = jnp.float32
BF16 = jnp.bfloat16

DIRS = ((-1, 0), (1, 0), (0, -1), (0, 1), (-1, -1), (1, -1), (-1, 1), (1, 1))
ROW_OF = (0, 16, 32, 48, 64, 72, 80, 88)
ROWS_IN = (16, 16, 16, 16, 8, 8, 8, 8)
HROWS = 128
LANES_OUT = 512
OFFS = tuple((ox, oy) for ox in (-1, 0, 1) for oy in (-1, 0, 1) if (ox, oy) != (0, 0)) + ((0, 0),)
NEIGHBOURS = 8
FILL_LANES = 256


def gp_col(gx, gy):
    return (gx & 1) + 2 * (gy & 1) + 4 * (gx >> 1) + 8 * (gy >> 1)


def par_col(px, py):
    return (px & 1) * 32 + (py & 1) * 16 + gp_col(px >> 1, py >> 1)


def leaf_col(x, y):
    return (x & 1) * 128 + (y & 1) * 64 + par_col(x >> 1, y >> 1)


def halo_cells(side):
    cells = []
    for dx, dy in DIRS:
        ex = -1 if dx < 0 else side
        ey = -1 if dy < 0 else side
        if dy == 0:
            cells.append([(ex, j) for j in range(side)])
        elif dx == 0:
            cells.append([(j, ey) for j in range(side)])
        else:
            cells.append([(ex, ey)])
    return cells


def pick_rows(side, col, base, lanes):
    out = np.zeros((HROWS, lanes), np.float32)
    for d, cells in enumerate(halo_cells(side)):
        for j, (cx, cy) in enumerate(cells):
            out[ROW_OF[d] + base[d] + j, col(cx % side, cy % side)] = 1.0
    return out


PAR_BASE = (0,) * 8
GP_BASE = (8,) * 4 + (1,) * 4


def shift_index(side, col, base, own_at, halo_at):
    where = {}
    for x in range(side):
        for y in range(side):
            where[x, y] = own_at + col(x, y)
    for d, cells in enumerate(halo_cells(side)):
        for j, cell in enumerate(cells):
            where[cell] = halo_at + ROW_OF[d] + base[d] + j
    out = np.zeros((9, side * side), np.int32)
    for o, (ox, oy) in enumerate(OFFS):
        for x in range(side):
            for y in range(side):
                out[o, col(x, y)] = where[x + ox, y + oy]
    return out


def cheb(u):
    terms = [u * 0 + 1.0, u]
    for _ in range(NODES - 2):
        terms.append(2.0 * u * terms[-1] - terms[-2])
    return terms


ANGLES = (2.0 * np.arange(NODES) + 1.0) * np.pi / (2.0 * NODES)
POINTS = np.cos(ANGLES)
S_COEF = 2.0 / NODES * np.cos(np.arange(NODES)[:, None] * ANGLES[None, :])
S_COEF[0] = 1.0 / NODES


def basis(u):
    terms = cheb(u)
    out = []
    for k in range(NODES):
        total = S_COEF[0, k] + float(S_COEF[1, k]) * terms[1]
        for n in range(2, NODES):
            total = total + float(S_COEF[n, k]) * terms[n]
        out.append(total)
    return out


def child_table():
    side = []
    for s in (0, 1):
        side.append(np.stack(basis(s - 0.5 + POINTS / 2), axis=1))
    out = np.zeros((4, NM, NM), np.float32)
    for sx in (0, 1):
        for sy in (0, 1):
            prod = side[sx][:, None, :, None] * side[sy][None, :, None, :]
            out[2 * sx + sy, :36, :36] = prod.reshape(36, 36)
    return out


def cell_vectors():
    coord = np.zeros((2, 4, NM), np.float32)
    cell = np.zeros((2, 4, NM), np.float32)
    for sx in (0, 1):
        for sy in (0, 1):
            ch = 2 * sx + sy
            node = np.arange(36)
            coord[0, ch] = sx - 0.5
            coord[1, ch] = sy - 0.5
            coord[0, ch, :36] += 0.5 * POINTS[node // 6]
            coord[1, ch, :36] += 0.5 * POINTS[node % 6]
            cell[0, ch] = sx
            cell[1, ch] = sy
    return coord.reshape(2, 4 * NM), cell.reshape(2, 4 * NM)


def constants():
    c = {}
    c["sel_leaf"] = pick_rows(LSIDE, leaf_col, PAR_BASE, 256).astype(BF16)
    sel_par = pick_rows(LSIDE // 2, par_col, PAR_BASE, 64)
    sel_gp = pick_rows(LSIDE // 4, gp_col, GP_BASE, 64)
    c["sel_mom"] = np.concatenate([sel_par, sel_gp], axis=1).astype(BF16)
    table = child_table()
    c["up"] = np.transpose(table, (2, 0, 1)).reshape(NM, 4 * NM)
    c["down"] = table.reshape(4 * NM, NM)
    src = np.zeros((16, 256), np.int32)
    src[:9] = shift_index(LSIDE, leaf_col, PAR_BASE, 0, 256)
    for x in range(LSIDE):
        for y in range(LSIDE):
            src[9, leaf_col(x, y)] = sum(
                (x >> k & 1) << 2 * k | (y >> k & 1) << 2 * k + 1 for k in range(4)
            )
    c["src_leaf"] = src
    msrc = np.full((16, 128), -1, np.int32)
    msrc[:9, :64] = shift_index(LSIDE // 2, par_col, PAR_BASE, 0, 128)
    msrc[:9, 64:80] = shift_index(LSIDE // 4, gp_col, GP_BASE, 64, 128)
    c["src_mom"] = msrc
    coord, cell = cell_vectors()
    rows = np.zeros((160, 128), np.float32)
    rows[:, 0:2] = coord.T
    rows[:, 2:4] = cell.T
    c["t_rows"] = rows
    cols = np.zeros((8, 9, 160), np.float32)
    for o, (ox, oy) in enumerate(OFFS):
        cols[0, o] = coord[0] + 2 * ox
        cols[1, o] = coord[1] + 2 * oy
        cols[2, o] = cell[0] + 2 * ox
        cols[3, o] = cell[1] + 2 * oy
    c["t_cols"] = cols.reshape(8, 1440)
    far_x = coord[0][:, None] - cols[0].reshape(1440)[None, :]
    far_y = coord[1][:, None] - cols[1].reshape(1440)[None, :]
    gap = np.maximum(
        np.abs(cell[0][:, None] - cols[2].reshape(1440)[None, :]),
        np.abs(cell[1][:, None] - cols[3].reshape(1440)[None, :]),
    )
    inv = np.where(gap > 1.5, 1.0 / (far_x**2 + far_y**2 + SOFTEN), 0.0)
    kx, ky = far_x * inv, far_y * inv
    full = np.concatenate([kx, ky, ky * ky - kx * kx, -2.0 * kx * ky]).astype(np.float32)
    c["hi_leaf"] = full.astype(BF16)
    c["lo_leaf"] = (full - c["hi_leaf"].astype(np.float32)).astype(BF16)
    sides = np.zeros((8, HROWS), np.float32)
    for d, (dx, dy) in enumerate(DIRS):
        sides[0, ROW_OF[d] : ROW_OF[d] + ROWS_IN[d]] = dx
        sides[1, ROW_OF[d] : ROW_OF[d] + ROWS_IN[d]] = dy
    c["sides"] = sides
    return c


CONST = constants()


def split2(x):
    hi = x.astype(BF16)
    return hi, (x - hi.astype(F32)).astype(BF16)


def split3(x):
    hi = x.astype(BF16)
    rest = x - hi.astype(F32)
    mid = rest.astype(BF16)
    return hi, mid, (rest - mid.astype(F32)).astype(BF16)


def nt_dot(a, b):
    return lax.dot_general(a, b, (((1,), (1,)), ((), ())), preferred_element_type=F32)


def tn_none(a, b):
    return lax.dot_general(a, b, (((1,), (0,)), ((), ())), preferred_element_type=F32)


def morton_split(code, bits):
    cx, cy = 0, 0
    for level in range((bits + 1) // 2):
        cx = cx + code // 4**level % 2 * 2**level
        cy = cy + code // (2 * 4**level) % 2 * 2**level
    return cx, cy


def morton_join(cx, cy, bits):
    code = 0
    for level in range((bits + 1) // 2):
        code = code + cx // 2**level % 2 * 4**level
        code = code + cy // 2**level % 2 * 2 * 4**level
    return code


def whole_kernel(dev_count, bits, *refs):
    sources, refs = refs[:OPERANDS], refs[OPERANDS:]
    out, refs = refs[0], refs[1:]
    held, refs = refs[:OPERANDS], refs[OPERANDS:]
    (pos, mass, count, src_leaf, sel_leaf, sel_mom, up, t_rows, t_cols, sides, src_mom,
     down, hi_leaf, lo_leaf) = held
    arrive_sems = refs[0]
    arrivals = [
        pltpu.make_async_copy(src, dst, arrive_sems.at[i])
        for i, (src, dst) in enumerate(zip(sources, held))
    ]
    for i in (1, 2, 3, 0, *range(4, OPERANDS)):
        arrivals[i].start()
    run_kernel(dev_count, bits, arrivals, pos, mass, count, sel_leaf, sel_mom, up, down, sides,
               src_leaf, src_mom, t_rows, t_cols, hi_leaf, lo_leaf, out, *refs[1:])


def run_kernel(dev_count, bits, arrivals, pos, mass, count, sel_leaf, sel_mom, up, down, sides,
               src_leaf, src_mom, t_rows, t_cols, hi_leaf, lo_leaf, out, own, mom, send, recv, part, mid, leaf_mom, first,
                 second, su, sv, sw, lone, xs, xs_par, hi_par, lo_par, leaf_kind, leaf_local,
                 result, self_live, edge_s, edge_r, sum_s1, sum_r1, sum_s2, sum_r2):
    code = lax.axis_index("grp") * dev_count + lax.axis_index("dev")
    bx, by = morton_split(code, bits)
    nx, ny = 2 ** ((bits + 1) // 2), 2 ** (bits // 2)
    low_n = 2 ** (bits // 2)
    high_n = 2**bits // low_n
    low, high = code % low_n, code // low_n

    def device(c):
        return {"grp": c // dev_count, "dev": c % dev_count}

    def beside(dx, dy):
        return device(morton_join((bx + dx + nx) % nx, (by + dy + ny) % ny, bits))

    def in_low(k):
        return device(high * low_n + (low + k) % low_n)

    def in_high(k):
        return device((high + k) % high_n * low_n + low)

    barrier = pltpu.get_barrier_semaphore()

    def greet(who):
        pl.semaphore_signal(barrier, inc=1, device_id=who, device_id_type=pl.DeviceIdType.MESH)

    def greet_low(k, carry):
        greet(in_low(k))
        return carry

    def greet_high(k, carry):
        greet(in_high(k))
        return carry

    lax.fori_loop(1, low_n, greet_low, 0)
    for dx, dy in DIRS:
        greet(beside(dx, dy))
    lax.fori_loop(1, high_n, greet_high, 0)

    starts = [qx * 2 + qy * 4 + sy for sy in (0, 1) for qx in (0, 1) for qy in (0, 1)]

    def turned(ref, lead, step):
        rows = jnp.concatenate(
            [ref[pl.ds(lead + step * s, 16, stride=8 * step), :] for s in starts], axis=0
        )
        return rows.T

    for arrival in arrivals[1:4]:
        arrival.wait()
    row256 = lax.broadcasted_iota(jnp.int32, (256, 256), 0)
    pick = jnp.where(row256 == src_leaf[9:10, :], 1.0, 0.0).astype(BF16)
    linear = count[...].astype(F32).astype(BF16)
    counts = tn_none(linear[0:1], pick[0:128]) + tn_none(linear[1:2], pick[128:256])
    m_turned = turned(mass, 0, 1)
    slot = lax.broadcasted_iota(jnp.int32, (PPL, 128), 0).astype(F32)
    totals = []
    for tile in (0, 1):
        lanes = slice(tile * 128, tile * 128 + 128)
        live = slot < counts[:, lanes]
        vals = jnp.where(live, m_turned[tile * PPL : tile * PPL + PPL], 0.0)
        own[128:192, lanes] = vals
        totals.append(jnp.sum(vals, axis=0, keepdims=True))
    near_mean = jnp.sum(totals[0] + totals[1], axis=1, keepdims=True) / jnp.sum(
        counts, axis=1, keepdims=True
    )
    row = lax.broadcasted_iota(jnp.int32, (8, 128), 0)
    part[...] = jnp.where(
        row == 0,
        totals[0] + totals[1],
        jnp.where(row == 1, counts[:, 0:128] + counts[:, 128:256], 0.0),
    )

    def low_copy(k):
        return pltpu.make_async_remote_copy(
            src_ref=part, dst_ref=first.at[k], send_sem=sum_s1.at[k], recv_sem=sum_r1.at[k],
            device_id=in_low(k), device_id_type=pl.DeviceIdType.MESH,
        )

    def high_copy(k):
        return pltpu.make_async_remote_copy(
            src_ref=mid, dst_ref=second.at[k], send_sem=sum_s2.at[k], recv_sem=sum_r2.at[k],
            device_id=in_high(k), device_id_type=pl.DeviceIdType.MESH,
        )

    def start_low(k, carry):
        low_copy(k).start()
        return carry

    def start_high(k, carry):
        high_copy(k).start()
        return carry

    def add_low(k, acc):
        low_copy(k).wait()
        return acc + first[k]

    def add_high(k, acc):
        high_copy(k).wait()
        return acc + second[k]

    pl.semaphore_wait(barrier, 8 + low_n - 1 + high_n - 1)
    lax.fori_loop(1, low_n, start_low, 0)
    arrivals[0].wait()
    for k in (0, 1):
        vals = turned(pos, k, 2)
        own[k * PPL : (k + 1) * PPL, 0:128] = vals[:PPL]
        own[k * PPL : (k + 1) * PPL, 128:256] = vals[PPL:]

    for arrival in arrivals[4:12]:
        arrival.wait()
    leaf_mom[...] = jnp.zeros_like(leaf_mom)
    for tile in (0, 1):
        lanes = slice(tile * 128, tile * 128 + 128)
        bu = basis(own[0:64, lanes])
        bv = basis(own[64:128, lanes])
        m_t = own[128:192, lanes]
        live_t = jnp.where(m_t > 0.0, 1.0, 0.0)
        for kind, weight in enumerate((m_t, live_t)):
            for a in range(NODES):
                wa = bu[a] * weight
                for b in range(NODES):
                    leaf_mom[pl.ds(kind * NM + a * 6 + b, 1), lanes] = jnp.sum(
                        wa * bv[b], axis=0, keepdims=True
                    )
    mom[...] = jnp.zeros_like(mom)
    stacked = []
    for kind in (0, 1):
        block = jnp.concatenate(
            [
                leaf_mom[kind * NM : (kind + 1) * NM, ch * 64 : ch * 64 + 64]
                for ch in range(4)
            ],
            axis=0,
        )
        mom[kind * 160 : kind * 160 + 160, 0:64] = block
        stacked.append(block)
    par = jnp.dot(
        up[...], jnp.concatenate(stacked, axis=1), precision=HIGHEST, preferred_element_type=F32
    )
    for kind in (0, 1):
        for q in range(4):
            at = kind * 64 + q * 16
            mom[pl.ds(kind * 160 + q * NM, NM), 64:80] = par[:, at : at + 16]
    own_cut = split3(own[...])
    send[:, 0:192] = nt_dot(
        jnp.concatenate([sel_leaf[...]] * 3, axis=1), jnp.concatenate(own_cut, axis=1)
    )
    send[:, 192:512] = nt_dot(
        jnp.concatenate([sel_mom[...]] * 3, axis=1),
        jnp.concatenate(split3(mom[...]), axis=1),
    )
    edges = []
    for d, (dx, dy) in enumerate(DIRS):
        rows = pl.ds(ROW_OF[d], ROWS_IN[d])
        copy = pltpu.make_async_remote_copy(
            src_ref=send.at[rows], dst_ref=recv.at[rows], send_sem=edge_s.at[d],
            recv_sem=edge_r.at[d], device_id=beside(-dx, -dy),
            device_id_type=pl.DeviceIdType.MESH,
        )
        copy.start()
        edges.append(copy)
    recv[96:HROWS, :] = jnp.zeros((HROWS - 96, LANES_OUT), F32)
    mid[...] = lax.fori_loop(1, low_n, add_low, part[...])
    lax.fori_loop(1, high_n, start_high, 0)

    def fill_tables(scale, table_hi, table_lo):
        def fill(i, carry):
            at = pl.multiple_of(i * 16, 16)
            rows = t_rows[pl.ds(at, 16), :]
            row_x, row_y = rows[:, 0:1] * scale, rows[:, 1:2] * scale
            cell_x, cell_y = rows[:, 2:3], rows[:, 3:4]
            for start in range(0, 1440, FILL_LANES):
                lanes = slice(start, min(start + FILL_LANES, 1440))
                dx = row_x - t_cols[0:1, lanes] * scale
                dy = row_y - t_cols[1:2, lanes] * scale
                gap = jnp.maximum(
                    jnp.abs(cell_x - t_cols[2:3, lanes]), jnp.abs(cell_y - t_cols[3:4, lanes])
                )
                x2 = dx * dx
                y2 = dy * dy
                inv = jnp.where(gap > 1.5, 1.0 / (x2 + y2 + SOFTEN), 0.0)
                kx = dx * inv
                ky = dy * inv
                for c, val in enumerate((kx, ky, ky * ky - kx * kx, -2.0 * kx * ky)):
                    hi, lo = split2(val)
                    table_hi[pl.ds(c * 160 + at, 16), lanes] = hi
                    table_lo[pl.ds(c * 160 + at, 16), lanes] = lo
            return carry

        lax.fori_loop(0, 10, fill, 0)

    fill_tables(2.0, hi_par, lo_par)

    def at_offset(o):
        return slice(o * PPL, o * PPL + PPL)

    own_parts = jnp.concatenate(own_cut, axis=1)

    def shift_own(o):
        hot = jnp.where(row256 == src_leaf[o : o + 1, :], 1.0, 0.0).astype(BF16)
        moved = tn_none(own_parts, jnp.concatenate([hot] * 3, axis=0))
        for tile in (0, 1):
            lanes = slice(tile * 128, tile * 128 + 128)
            su[tile, at_offset(o), :] = moved[0:64, lanes]
            sv[tile, at_offset(o), :] = moved[64:128, lanes]
            sw[tile, at_offset(o), :] = moved[128:192, lanes]

    for o in range(NEIGHBOURS):
        shift_own(o)
    self_at = NEIGHBOURS * PPL
    for tile in (0, 1):
        lanes = slice(tile * 128, tile * 128 + 128)
        su[tile, self_at : self_at + PPL, :] = own[0:64, lanes] * 0.5
        sv[tile, self_at : self_at + PPL, :] = own[64:128, lanes] * 0.5
        m = own[128:192, lanes]
        sw[tile, self_at : self_at + PPL, :] = jnp.where(m > 0.0, m - near_mean, 0.0)
        lone[tile, 0:PPL, :] = jnp.where(m > 0.0, 1.0, 0.0)

    def near_field(first_row, row_count):
        width, unroll = 4, 16
        for tile in (0, 1):
            for piece in range(PPL // (8 * width)):
                base = piece * 8 * width
                tx, ty = targets(tile, base, width)

                def pairs(step, acc, tile=tile, tx=tx, ty=ty):
                    acc = list(acc)
                    for i in range(unroll):
                        at = pl.ds(first_row + step * unroll + i, 8, stride=0)
                        sx, sy, w = su[tile, at, :], sv[tile, at, :], sw[tile, at, :]
                        for t in range(width):
                            dx = tx[t] - sx
                            dy = ty[t] - sy
                            inv = 1.0 / (dy * dy + (dx * dx + SOFTEN))
                            kx = dx * inv
                            ky = dy * inv
                            wx = w * kx
                            wy = w * ky
                            acc[4 * t] = acc[4 * t] + wx
                            acc[4 * t + 1] = acc[4 * t + 1] + wy
                            acc[4 * t + 2] = (acc[4 * t + 2] + wy * ky) - wx * kx
                            acc[4 * t + 3] = acc[4 * t + 3] + wx * ky
                    return tuple(acc)

                acc = lax.fori_loop(0, row_count // unroll, pairs, (zero,) * (4 * width))
                for t in range(width):
                    rows = slice(tile * PPL + base + 8 * t, tile * PPL + base + 8 * t + 8)
                    for c in range(4):
                        near = acc[4 * t + c]
                        if c == 3:
                            near = near * -2.0
                        result[c, rows, :] = result[c, rows, :] + near

    zero = jnp.zeros((8, 128), F32)

    def targets(tile, base, width):
        lanes = slice(tile * 128, tile * 128 + 128)
        tx = [own[base + 8 * i : base + 8 * i + 8, lanes] * 0.5 for i in range(width)]
        ty = [own[64 + base + 8 * i : 72 + base + 8 * i, lanes] * 0.5 for i in range(width)]
        return tx, ty

    self_width = 2
    for tile in (0, 1):
        for piece in range(PPL // (8 * self_width)):
            base = piece * 8 * self_width
            tx, ty = targets(tile, base, self_width)

            def self_pairs(step, acc, tile=tile, tx=tx, ty=ty):
                acc = list(acc)
                for i in range(4):
                    k = step * 4 + i
                    at = pl.ds(self_at + k, 8, stride=0)
                    sx, sy, m = su[tile, at, :], sv[tile, at, :], sw[tile, at, :]
                    one = lone[tile, pl.ds(k, 8, stride=0), :]
                    for t in range(self_width):
                        dx = tx[t] - sx
                        dy = ty[t] - sy
                        x2 = dx * dx
                        y2 = dy * dy
                        inv = 1.0 / (x2 + y2 + SOFTEN)
                        gap = y2 - x2
                        cross = dx * dy
                        for kind, w in enumerate((m, one)):
                            at_acc = 8 * t + 4 * kind
                            w1 = w * inv
                            w2 = w1 * inv
                            acc[at_acc] = acc[at_acc] + w1 * dx
                            acc[at_acc + 1] = acc[at_acc + 1] + w1 * dy
                            acc[at_acc + 2] = acc[at_acc + 2] + w2 * gap
                            acc[at_acc + 3] = acc[at_acc + 3] + w2 * cross
                return tuple(acc)

            acc = lax.fori_loop(0, PPL // 4, self_pairs, (zero,) * (8 * self_width))
            for t in range(self_width):
                rows = slice(tile * PPL + base + 8 * t, tile * PPL + base + 8 * t + 8)
                for c in range(4):
                    scale = -2.0 if c == 3 else 1.0
                    result[c, rows, :] = acc[8 * t + c] * scale
                    self_live[c, rows, :] = acc[8 * t + 4 + c] * scale

    for copy in edges:
        copy.wait()
    cell_x = sides[0:1] + jnp.full((1, 128), bx, jnp.int32).astype(F32)
    cell_y = sides[1:2] + jnp.full((1, 128), by, jnp.int32).astype(F32)
    inside = jnp.where(
        (cell_x >= 0.0) & (cell_x < float(nx)) & (cell_y >= 0.0) & (cell_y < float(ny)), 1.0, 0.0
    )
    halo = recv[...].T * inside
    halo_parts = jnp.concatenate(split3(halo[0:192]), axis=1)
    row128 = lax.broadcasted_iota(jnp.int32, (128, 256), 0) + 256

    def shift_halo(o):
        hot = jnp.where(row128 == src_leaf[o : o + 1, :], 1.0, 0.0).astype(BF16)
        moved = tn_none(halo_parts, jnp.concatenate([hot] * 3, axis=0))
        off_x, off_y = OFFS[o]
        for tile in (0, 1):
            lanes = slice(tile * 128, tile * 128 + 128)
            at = at_offset(o)
            su[tile, at, :] = (su[tile, at, :] + moved[0:64, lanes]) * 0.5 + off_x
            sv[tile, at, :] = (sv[tile, at, :] + moved[64:128, lanes]) * 0.5 + off_y
            sw[tile, at, :] = sw[tile, at, :] + moved[128:192, lanes]

    for o in range(NEIGHBOURS):
        shift_halo(o)

    all_mom = jnp.concatenate([mom[...], halo[192:512]], axis=1)
    all_mom = jnp.concatenate(
        [all_mom[0:160] - near_mean * all_mom[160:320], all_mom[160:320]], axis=0
    )
    cut_mom = jnp.concatenate(split2(all_mom), axis=0)

    def shift_moments(o):
        hot = jnp.where(row256[:, 0:128] == src_mom[o : o + 1, :], 1.0, 0.0).astype(BF16)
        moved = tn_none(cut_mom, hot)
        at = slice(o * 160, o * 160 + 160)
        pieces = [moved[160 * i : 160 * i + 160] for i in range(4)]
        xs[at, :] = jnp.concatenate([p[:, 0:64] for p in pieces], axis=1).astype(BF16)
        xs_par[at, :] = jnp.concatenate([p[:, 64:80] for p in pieces], axis=1).astype(BF16)

    for o in range(9):
        shift_moments(o)

    wide = tn_none(hi_par[...], xs_par[...])
    par = wide[:, 0:32] + wide[:, 32:64] + tn_none(lo_par[...], xs_par[:, 0:32])
    par_cols = jnp.concatenate(
        [
            par[c * 160 + q * NM : c * 160 + q * NM + NM, kind * 16 : kind * 16 + 16]
            for kind in (0, 1)
            for c in range(4)
            for q in range(4)
        ],
        axis=1,
    )
    from_par = jnp.dot(
        down[...], par_cols, precision=HIGHEST, preferred_element_type=F32
    )
    for arrival in arrivals[12:]:
        arrival.wait()
    wide = tn_none(hi_leaf[...], xs[...])
    leaf = wide[:, 0:128] + wide[:, 128:256] + tn_none(lo_leaf[...], xs[:, 0:128])
    for kind in (0, 1):
        for c in range(4):
            at = kind * 256 + c * 64
            leaf_kind[kind, c] = jnp.concatenate(
                [
                    leaf[c * 160 + ch * NM : c * 160 + ch * NM + NM, kind * 64 : kind * 64 + 64]
                    + from_par[ch * NM : ch * NM + NM, at : at + 64]
                    for ch in range(4)
                ],
                axis=1,
            )

    sums = lax.fori_loop(1, high_n, add_high, mid[...])
    mass_sum = jnp.sum(sums[0:1], axis=1, keepdims=True)
    live_sum = jnp.sum(sums[1:2], axis=1, keepdims=True)
    mean = mass_sum / live_sum
    for tile in (0, 1):
        m = sw[tile, 0:self_at, :]
        sw[tile, 0:self_at, :] = jnp.where(m > 0.0, m - mean, 0.0)
    for c in range(4):
        leaf_local[c] = leaf_kind[0, c] - (mean - near_mean) * leaf_kind[1, c]

    for tile in (0, 1):
        lanes = slice(tile * 128, tile * 128 + 128)
        bu = basis(own[0:64, lanes])
        bv = basis(own[64:128, lanes])
        for c in range(4):
            rows = slice(tile * PPL, tile * PPL + PPL)
            acc = result[c, rows, :] - (mean - near_mean) * self_live[c, rows, :]
            for a in range(NODES):
                half = leaf_local[c, pl.ds(a * 6, 1), lanes] * bv[0]
                for b in range(1, NODES):
                    half = half + leaf_local[c, pl.ds(a * 6 + b, 1), lanes] * bv[b]
                acc = acc + half * bu[a]
            result[c, rows, :] = acc

    near_field(0, self_at)

    for c in range(4):
        back = result[c].T
        for i, s in enumerate(starts):
            out[pl.ds(s * 4 + c, 16, stride=32), :] = back[16 * i : 16 * i + 16]


def vmem():
    return pl.BlockSpec(memory_space=pltpu.VMEM)


NAMES = ("src_leaf", "sel_leaf", "sel_mom", "up", "t_rows", "t_cols", "sides", "src_mom", "down",
         "hi_leaf", "lo_leaf")
OPERANDS = 3 + len(NAMES)


def on_device(particle_pos, particle_mass, leaf_counts):
    dev_count = lax.axis_size("dev")
    bits = (lax.axis_size("grp") * dev_count).bit_length() - 1
    low_n = 2 ** (bits // 2)
    high_n = 2**bits // low_n
    pos = particle_pos.reshape(2, 128, 128).transpose(1, 0, 2).reshape(256, 128)
    mass = particle_mass.reshape(128, 128)
    count = leaf_counts.reshape(2, 128)
    operands = (pos, mass, count, *[jnp.asarray(CONST[k]) for k in NAMES])
    out = pl.pallas_call(
        functools.partial(whole_kernel, dev_count, bits),
        out_shape=jax.ShapeDtypeStruct((512, 128), F32),
        in_specs=[pl.BlockSpec(memory_space=pltpu.HBM)] * OPERANDS,
        out_specs=vmem(),
        scratch_shapes=[pltpu.VMEM(x.shape, x.dtype) for x in operands]
        + [
            pltpu.SemaphoreType.DMA((OPERANDS,)),
            pltpu.VMEM((192, 256), F32),
            pltpu.VMEM((320, 128), F32),
            pltpu.VMEM((HROWS, LANES_OUT), F32),
            pltpu.VMEM((HROWS, LANES_OUT), F32),
            pltpu.VMEM((8, 128), F32),
            pltpu.VMEM((8, 128), F32),
            pltpu.VMEM((2 * NM, 256), F32),
            pltpu.VMEM((low_n, 8, 128), F32),
            pltpu.VMEM((high_n, 8, 128), F32),
            pltpu.VMEM((2, 9 * PPL + 8, 128), F32),
            pltpu.VMEM((2, 9 * PPL + 8, 128), F32),
            pltpu.VMEM((2, 9 * PPL + 8, 128), F32),
            pltpu.VMEM((2, PPL + 8, 128), F32),
            pltpu.VMEM((1440, 256), BF16),
            pltpu.VMEM((1440, 64), BF16),
            pltpu.VMEM((640, 1440), BF16),
            pltpu.VMEM((640, 1440), BF16),
            pltpu.VMEM((2, 4, NM, 256), F32),
            pltpu.VMEM((4, NM, 256), F32),
            pltpu.VMEM((4, 128, 128), F32),
            pltpu.VMEM((4, 128, 128), F32),
            pltpu.SemaphoreType.DMA((8,)),
            pltpu.SemaphoreType.DMA((8,)),
            pltpu.SemaphoreType.DMA((low_n,)),
            pltpu.SemaphoreType.DMA((low_n,)),
            pltpu.SemaphoreType.DMA((high_n,)),
            pltpu.SemaphoreType.DMA((high_n,)),
        ],
        compiler_params=pltpu.CompilerParams(
            collective_id=0, has_side_effects=True, vmem_limit_bytes=63 * 2**20
        ),
        name="fields",
    )(*operands)
    return out.reshape(128, 4, 128).transpose(1, 0, 2).reshape(4, LSIDE * LSIDE * PPL)


def solution(mesh):
    in_specs = (P(None, ("grp", "dev")), P(("grp", "dev")), P(("grp", "dev")))
    out_specs = P(None, ("grp", "dev"))
    return jax.shard_map(
        on_device, mesh=mesh, in_specs=in_specs, out_specs=out_specs, check_vma=False
    )
```

```python
import functools

import jax
import jax.numpy as jnp
import numpy as np
from jax import lax
from jax.experimental import pallas as pl
from jax.experimental.pallas import tpu as pltpu
from jax.sharding import PartitionSpec as P

NODES = 6
PPL = 64
LSIDE = 16
SOFTEN = 0.01
NM = 40
HIGHEST = lax.Precision.HIGHEST
F32 = jnp.float32
BF16 = jnp.bfloat16

DIRS = ((-1, 0), (1, 0), (0, -1), (0, 1), (-1, -1), (1, -1), (-1, 1), (1, 1))
ROW_OF = (0, 16, 32, 48, 64, 72, 80, 88)
ROWS_IN = (16, 16, 16, 16, 8, 8, 8, 8)
HROWS = 128
LANES_OUT = 512
OFFS = tuple((ox, oy) for ox in (-1, 0, 1) for oy in (-1, 0, 1) if (ox, oy) != (0, 0)) + ((0, 0),)
NEIGHBOURS = 8
FILL_LANES = 256


def gp_col(gx, gy):
    return (gx & 1) + 2 * (gy & 1) + 4 * (gx >> 1) + 8 * (gy >> 1)


def par_col(px, py):
    return (px & 1) * 32 + (py & 1) * 16 + gp_col(px >> 1, py >> 1)


def leaf_col(x, y):
    return (x & 1) * 128 + (y & 1) * 64 + par_col(x >> 1, y >> 1)


def halo_cells(side):
    cells = []
    for dx, dy in DIRS:
        ex = -1 if dx < 0 else side
        ey = -1 if dy < 0 else side
        if dy == 0:
            cells.append([(ex, j) for j in range(side)])
        elif dx == 0:
            cells.append([(j, ey) for j in range(side)])
        else:
            cells.append([(ex, ey)])
    return cells


def pick_rows(side, col, base, lanes):
    out = np.zeros((HROWS, lanes), np.float32)
    for d, cells in enumerate(halo_cells(side)):
        for j, (cx, cy) in enumerate(cells):
            out[ROW_OF[d] + base[d] + j, col(cx % side, cy % side)] = 1.0
    return out


PAR_BASE = (0,) * 8
GP_BASE = (8,) * 4 + (1,) * 4


def shift_index(side, col, base, own_at, halo_at):
    where = {}
    for x in range(side):
        for y in range(side):
            where[x, y] = own_at + col(x, y)
    for d, cells in enumerate(halo_cells(side)):
        for j, cell in enumerate(cells):
            where[cell] = halo_at + ROW_OF[d] + base[d] + j
    out = np.zeros((9, side * side), np.int32)
    for o, (ox, oy) in enumerate(OFFS):
        for x in range(side):
            for y in range(side):
                out[o, col(x, y)] = where[x + ox, y + oy]
    return out


def cheb(u):
    terms = [u * 0 + 1.0, u]
    for _ in range(NODES - 2):
        terms.append(2.0 * u * terms[-1] - terms[-2])
    return terms


ANGLES = (2.0 * np.arange(NODES) + 1.0) * np.pi / (2.0 * NODES)
POINTS = np.cos(ANGLES)
S_COEF = 2.0 / NODES * np.cos(np.arange(NODES)[:, None] * ANGLES[None, :])
S_COEF[0] = 1.0 / NODES


def basis(u):
    terms = cheb(u)
    out = []
    for k in range(NODES):
        total = S_COEF[0, k] + float(S_COEF[1, k]) * terms[1]
        for n in range(2, NODES):
            total = total + float(S_COEF[n, k]) * terms[n]
        out.append(total)
    return out


def child_table():
    side = []
    for s in (0, 1):
        side.append(np.stack(basis(s - 0.5 + POINTS / 2), axis=1))
    out = np.zeros((4, NM, NM), np.float32)
    for sx in (0, 1):
        for sy in (0, 1):
            prod = side[sx][:, None, :, None] * side[sy][None, :, None, :]
            out[2 * sx + sy, :36, :36] = prod.reshape(36, 36)
    return out


def cell_vectors():
    coord = np.zeros((2, 4, NM), np.float32)
    cell = np.zeros((2, 4, NM), np.float32)
    for sx in (0, 1):
        for sy in (0, 1):
            ch = 2 * sx + sy
            node = np.arange(36)
            coord[0, ch] = sx - 0.5
            coord[1, ch] = sy - 0.5
            coord[0, ch, :36] += 0.5 * POINTS[node // 6]
            coord[1, ch, :36] += 0.5 * POINTS[node % 6]
            cell[0, ch] = sx
            cell[1, ch] = sy
    return coord.reshape(2, 4 * NM), cell.reshape(2, 4 * NM)


def constants():
    c = {}
    c["sel_leaf"] = pick_rows(LSIDE, leaf_col, PAR_BASE, 256).astype(BF16)
    sel_par = pick_rows(LSIDE // 2, par_col, PAR_BASE, 64)
    sel_gp = pick_rows(LSIDE // 4, gp_col, GP_BASE, 64)
    c["sel_mom"] = np.concatenate([sel_par, sel_gp], axis=1).astype(BF16)
    table = child_table()
    c["up"] = np.transpose(table, (2, 0, 1)).reshape(NM, 4 * NM)
    c["down"] = table.reshape(4 * NM, NM)
    src = np.zeros((16, 256), np.int32)
    src[:9] = shift_index(LSIDE, leaf_col, PAR_BASE, 0, 256)
    for x in range(LSIDE):
        for y in range(LSIDE):
            src[9, leaf_col(x, y)] = sum(
                (x >> k & 1) << 2 * k | (y >> k & 1) << 2 * k + 1 for k in range(4)
            )
    c["src_leaf"] = src
    msrc = np.full((16, 128), -1, np.int32)
    msrc[:9, :64] = shift_index(LSIDE // 2, par_col, PAR_BASE, 0, 128)
    msrc[:9, 64:80] = shift_index(LSIDE // 4, gp_col, GP_BASE, 64, 128)
    c["src_mom"] = msrc
    coord, cell = cell_vectors()
    rows = np.zeros((160, 128), np.float32)
    rows[:, 0:2] = coord.T
    rows[:, 2:4] = cell.T
    c["t_rows"] = rows
    cols = np.zeros((8, 9, 160), np.float32)
    for o, (ox, oy) in enumerate(OFFS):
        cols[0, o] = coord[0] + 2 * ox
        cols[1, o] = coord[1] + 2 * oy
        cols[2, o] = cell[0] + 2 * ox
        cols[3, o] = cell[1] + 2 * oy
    c["t_cols"] = cols.reshape(8, 1440)
    far_x = coord[0][:, None] - cols[0].reshape(1440)[None, :]
    far_y = coord[1][:, None] - cols[1].reshape(1440)[None, :]
    gap = np.maximum(
        np.abs(cell[0][:, None] - cols[2].reshape(1440)[None, :]),
        np.abs(cell[1][:, None] - cols[3].reshape(1440)[None, :]),
    )
    inv = np.where(gap > 1.5, 1.0 / (far_x**2 + far_y**2 + SOFTEN), 0.0)
    kx, ky = far_x * inv, far_y * inv
    full = np.concatenate([kx, ky, ky * ky - kx * kx, -2.0 * kx * ky]).astype(np.float32)
    c["hi_leaf"] = full.astype(BF16)
    c["lo_leaf"] = (full - c["hi_leaf"].astype(np.float32)).astype(BF16)
    sides = np.zeros((8, HROWS), np.float32)
    for d, (dx, dy) in enumerate(DIRS):
        sides[0, ROW_OF[d] : ROW_OF[d] + ROWS_IN[d]] = dx
        sides[1, ROW_OF[d] : ROW_OF[d] + ROWS_IN[d]] = dy
    c["sides"] = sides
    return c


CONST = constants()


def split2(x):
    hi = x.astype(BF16)
    return hi, (x - hi.astype(F32)).astype(BF16)


def split3(x):
    hi = x.astype(BF16)
    rest = x - hi.astype(F32)
    mid = rest.astype(BF16)
    return hi, mid, (rest - mid.astype(F32)).astype(BF16)


def nt_dot(a, b):
    return lax.dot_general(a, b, (((1,), (1,)), ((), ())), preferred_element_type=F32)


def tn_none(a, b):
    return lax.dot_general(a, b, (((1,), (0,)), ((), ())), preferred_element_type=F32)


def morton_split(code, bits):
    cx, cy = 0, 0
    for level in range((bits + 1) // 2):
        cx = cx + code // 4**level % 2 * 2**level
        cy = cy + code // (2 * 4**level) % 2 * 2**level
    return cx, cy


def morton_join(cx, cy, bits):
    code = 0
    for level in range((bits + 1) // 2):
        code = code + cx // 2**level % 2 * 4**level
        code = code + cy // 2**level % 2 * 2 * 4**level
    return code


def whole_kernel(dev_count, bits, *refs):
    sources, refs = refs[:OPERANDS], refs[OPERANDS:]
    out, refs = refs[0], refs[1:]
    held, refs = refs[:OPERANDS], refs[OPERANDS:]
    (pos, mass, count, src_leaf, sel_leaf, sel_mom, up, t_rows, t_cols, sides, src_mom,
     down, hi_leaf, lo_leaf) = held
    arrive_sems = refs[0]
    arrivals = [
        pltpu.make_async_copy(src, dst, arrive_sems.at[i])
        for i, (src, dst) in enumerate(zip(sources, held))
    ]
    for i in (1, 2, 3, 0, *range(4, OPERANDS)):
        arrivals[i].start()
    run_kernel(dev_count, bits, arrivals, pos, mass, count, sel_leaf, sel_mom, up, down, sides,
               src_leaf, src_mom, t_rows, t_cols, hi_leaf, lo_leaf, out, *refs[1:])


def run_kernel(dev_count, bits, arrivals, pos, mass, count, sel_leaf, sel_mom, up, down, sides,
               src_leaf, src_mom, t_rows, t_cols, hi_leaf, lo_leaf, out, own, mom, send, recv, part, mid, leaf_mom, first,
                 second, su, sv, sw, lone, xs, xs_par, hi_par, lo_par, leaf_kind, leaf_local,
                 result, self_live, edge_s, edge_r, sum_s1, sum_r1, sum_s2, sum_r2):
    code = lax.axis_index("grp") * dev_count + lax.axis_index("dev")
    bx, by = morton_split(code, bits)
    nx, ny = 2 ** ((bits + 1) // 2), 2 ** (bits // 2)
    low_n = 2 ** (bits // 2)
    high_n = 2**bits // low_n
    low, high = code % low_n, code // low_n

    def device(c):
        return {"grp": c // dev_count, "dev": c % dev_count}

    def beside(dx, dy):
        return device(morton_join((bx + dx + nx) % nx, (by + dy + ny) % ny, bits))

    def in_low(k):
        return device(high * low_n + (low + k) % low_n)

    def in_high(k):
        return device((high + k) % high_n * low_n + low)

    barrier = pltpu.get_barrier_semaphore()

    def greet(who):
        pl.semaphore_signal(barrier, inc=1, device_id=who, device_id_type=pl.DeviceIdType.MESH)

    def greet_low(k, carry):
        greet(in_low(k))
        return carry

    def greet_high(k, carry):
        greet(in_high(k))
        return carry

    lax.fori_loop(1, low_n, greet_low, 0)
    for dx, dy in DIRS:
        greet(beside(dx, dy))
    lax.fori_loop(1, high_n, greet_high, 0)

    starts = [qx * 2 + qy * 4 + sy for sy in (0, 1) for qx in (0, 1) for qy in (0, 1)]

    def turned(ref, lead, step):
        rows = jnp.concatenate(
            [ref[pl.ds(lead + step * s, 16, stride=8 * step), :] for s in starts], axis=0
        )
        return rows.T

    for arrival in arrivals[1:4]:
        arrival.wait()
    row256 = lax.broadcasted_iota(jnp.int32, (256, 256), 0)
    pick = jnp.where(row256 == src_leaf[9:10, :], 1.0, 0.0).astype(BF16)
    linear = count[...].astype(F32).astype(BF16)
    counts = tn_none(linear[0:1], pick[0:128]) + tn_none(linear[1:2], pick[128:256])
    m_turned = turned(mass, 0, 1)
    slot = lax.broadcasted_iota(jnp.int32, (PPL, 128), 0).astype(F32)
    totals = []
    for tile in (0, 1):
        lanes = slice(tile * 128, tile * 128 + 128)
        live = slot < counts[:, lanes]
        vals = jnp.where(live, m_turned[tile * PPL : tile * PPL + PPL], 0.0)
        own[128:192, lanes] = vals
        totals.append(jnp.sum(vals, axis=0, keepdims=True))
    near_mean = jnp.sum(totals[0] + totals[1], axis=1, keepdims=True) / jnp.sum(
        counts, axis=1, keepdims=True
    )
    row = lax.broadcasted_iota(jnp.int32, (8, 128), 0)
    part[...] = jnp.where(
        row == 0,
        totals[0] + totals[1],
        jnp.where(row == 1, counts[:, 0:128] + counts[:, 128:256], 0.0),
    )

    def low_copy(k):
        return pltpu.make_async_remote_copy(
            src_ref=part, dst_ref=first.at[k], send_sem=sum_s1.at[k], recv_sem=sum_r1.at[k],
            device_id=in_low(k), device_id_type=pl.DeviceIdType.MESH,
        )

    def high_copy(k):
        return pltpu.make_async_remote_copy(
            src_ref=mid, dst_ref=second.at[k], send_sem=sum_s2.at[k], recv_sem=sum_r2.at[k],
            device_id=in_high(k), device_id_type=pl.DeviceIdType.MESH,
        )

    def start_low(k, carry):
        low_copy(k).start()
        return carry

    def start_high(k, carry):
        high_copy(k).start()
        return carry

    def add_low(k, acc):
        low_copy(k).wait()
        return acc + first[k]

    def add_high(k, acc):
        high_copy(k).wait()
        return acc + second[k]

    pl.semaphore_wait(barrier, 8 + low_n - 1 + high_n - 1)
    lax.fori_loop(1, low_n, start_low, 0)
    arrivals[0].wait()
    for k in (0, 1):
        vals = turned(pos, k, 2)
        own[k * PPL : (k + 1) * PPL, 0:128] = vals[:PPL]
        own[k * PPL : (k + 1) * PPL, 128:256] = vals[PPL:]

    for arrival in arrivals[4:12]:
        arrival.wait()
    leaf_mom[...] = jnp.zeros_like(leaf_mom)
    for tile in (0, 1):
        lanes = slice(tile * 128, tile * 128 + 128)
        bu = basis(own[0:64, lanes])
        bv = basis(own[64:128, lanes])
        m_t = own[128:192, lanes]
        live_t = jnp.where(m_t > 0.0, 1.0, 0.0)
        for kind, weight in enumerate((m_t, live_t)):
            for a in range(NODES):
                wa = bu[a] * weight
                for b in range(NODES):
                    leaf_mom[pl.ds(kind * NM + a * 6 + b, 1), lanes] = jnp.sum(
                        wa * bv[b], axis=0, keepdims=True
                    )
    mom[...] = jnp.zeros_like(mom)
    stacked = []
    for kind in (0, 1):
        block = jnp.concatenate(
            [
                leaf_mom[kind * NM : (kind + 1) * NM, ch * 64 : ch * 64 + 64]
                for ch in range(4)
            ],
            axis=0,
        )
        mom[kind * 160 : kind * 160 + 160, 0:64] = block
        stacked.append(block)
    par = jnp.dot(
        up[...], jnp.concatenate(stacked, axis=1), precision=HIGHEST, preferred_element_type=F32
    )
    for kind in (0, 1):
        for q in range(4):
            at = kind * 64 + q * 16
            mom[pl.ds(kind * 160 + q * NM, NM), 64:80] = par[:, at : at + 16]
    own_cut = split3(own[...])
    send[:, 0:192] = nt_dot(
        jnp.concatenate([sel_leaf[...]] * 3, axis=1), jnp.concatenate(own_cut, axis=1)
    )
    send[:, 192:512] = nt_dot(
        jnp.concatenate([sel_mom[...]] * 3, axis=1),
        jnp.concatenate(split3(mom[...]), axis=1),
    )
    edges = []
    for d, (dx, dy) in enumerate(DIRS):
        rows = pl.ds(ROW_OF[d], ROWS_IN[d])
        copy = pltpu.make_async_remote_copy(
            src_ref=send.at[rows], dst_ref=recv.at[rows], send_sem=edge_s.at[d],
            recv_sem=edge_r.at[d], device_id=beside(-dx, -dy),
            device_id_type=pl.DeviceIdType.MESH,
        )
        copy.start()
        edges.append(copy)
    recv[96:HROWS, :] = jnp.zeros((HROWS - 96, LANES_OUT), F32)

    def fill_tables(scale, table_hi, table_lo):
        def fill(i, carry):
            at = pl.multiple_of(i * 16, 16)
            rows = t_rows[pl.ds(at, 16), :]
            row_x, row_y = rows[:, 0:1] * scale, rows[:, 1:2] * scale
            cell_x, cell_y = rows[:, 2:3], rows[:, 3:4]
            for start in range(0, 1440, FILL_LANES):
                lanes = slice(start, min(start + FILL_LANES, 1440))
                dx = row_x - t_cols[0:1, lanes] * scale
                dy = row_y - t_cols[1:2, lanes] * scale
                gap = jnp.maximum(
                    jnp.abs(cell_x - t_cols[2:3, lanes]), jnp.abs(cell_y - t_cols[3:4, lanes])
                )
                x2 = dx * dx
                y2 = dy * dy
                inv = jnp.where(gap > 1.5, 1.0 / (x2 + y2 + SOFTEN), 0.0)
                kx = dx * inv
                ky = dy * inv
                for c, val in enumerate((kx, ky, ky * ky - kx * kx, -2.0 * kx * ky)):
                    hi, lo = split2(val)
                    table_hi[pl.ds(c * 160 + at, 16), lanes] = hi
                    table_lo[pl.ds(c * 160 + at, 16), lanes] = lo
            return carry

        lax.fori_loop(0, 10, fill, 0)

    fill_tables(2.0, hi_par, lo_par)

    def at_offset(o):
        return slice(o * PPL, o * PPL + PPL)

    own_parts = jnp.concatenate(own_cut, axis=1)

    def shift_own(o):
        hot = jnp.where(row256 == src_leaf[o : o + 1, :], 1.0, 0.0).astype(BF16)
        moved = tn_none(own_parts, jnp.concatenate([hot] * 3, axis=0))
        for tile in (0, 1):
            lanes = slice(tile * 128, tile * 128 + 128)
            su[tile, at_offset(o), :] = moved[0:64, lanes]
            sv[tile, at_offset(o), :] = moved[64:128, lanes]
            sw[tile, at_offset(o), :] = moved[128:192, lanes]

    for o in range(NEIGHBOURS):
        shift_own(o)
    self_at = NEIGHBOURS * PPL
    for tile in (0, 1):
        lanes = slice(tile * 128, tile * 128 + 128)
        su[tile, self_at : self_at + PPL, :] = own[0:64, lanes] * 0.5
        sv[tile, self_at : self_at + PPL, :] = own[64:128, lanes] * 0.5
        m = own[128:192, lanes]
        sw[tile, self_at : self_at + PPL, :] = jnp.where(m > 0.0, m - near_mean, 0.0)
        lone[tile, 0:PPL, :] = jnp.where(m > 0.0, 1.0, 0.0)

    def near_field(first_row, row_count):
        width, unroll = 4, 16
        for tile in (0, 1):
            for piece in range(PPL // (8 * width)):
                base = piece * 8 * width
                tx, ty = targets(tile, base, width)

                def pairs(step, acc, tile=tile, tx=tx, ty=ty):
                    acc = list(acc)
                    for i in range(unroll):
                        at = pl.ds(first_row + step * unroll + i, 8, stride=0)
                        sx, sy, w = su[tile, at, :], sv[tile, at, :], sw[tile, at, :]
                        for t in range(width):
                            dx = tx[t] - sx
                            dy = ty[t] - sy
                            inv = 1.0 / (dy * dy + (dx * dx + SOFTEN))
                            kx = dx * inv
                            ky = dy * inv
                            wx = w * kx
                            wy = w * ky
                            acc[4 * t] = acc[4 * t] + wx
                            acc[4 * t + 1] = acc[4 * t + 1] + wy
                            acc[4 * t + 2] = (acc[4 * t + 2] + wy * ky) - wx * kx
                            acc[4 * t + 3] = acc[4 * t + 3] + wx * ky
                    return tuple(acc)

                acc = lax.fori_loop(0, row_count // unroll, pairs, (zero,) * (4 * width))
                for t in range(width):
                    rows = slice(tile * PPL + base + 8 * t, tile * PPL + base + 8 * t + 8)
                    for c in range(4):
                        near = acc[4 * t + c]
                        if c == 3:
                            near = near * -2.0
                        result[c, rows, :] = result[c, rows, :] + near

    mid[...] = lax.fori_loop(1, low_n, add_low, part[...])
    lax.fori_loop(1, high_n, start_high, 0)

    zero = jnp.zeros((8, 128), F32)

    def targets(tile, base, width):
        lanes = slice(tile * 128, tile * 128 + 128)
        tx = [own[base + 8 * i : base + 8 * i + 8, lanes] * 0.5 for i in range(width)]
        ty = [own[64 + base + 8 * i : 72 + base + 8 * i, lanes] * 0.5 for i in range(width)]
        return tx, ty

    self_width = 2
    for tile in (0, 1):
        for piece in range(PPL // (8 * self_width)):
            base = piece * 8 * self_width
            tx, ty = targets(tile, base, self_width)

            def self_pairs(step, acc, tile=tile, tx=tx, ty=ty):
                acc = list(acc)
                for i in range(4):
                    k = step * 4 + i
                    at = pl.ds(self_at + k, 8, stride=0)
                    sx, sy, m = su[tile, at, :], sv[tile, at, :], sw[tile, at, :]
                    one = lone[tile, pl.ds(k, 8, stride=0), :]
                    for t in range(self_width):
                        dx = tx[t] - sx
                        dy = ty[t] - sy
                        x2 = dx * dx
                        y2 = dy * dy
                        inv = 1.0 / (x2 + y2 + SOFTEN)
                        gap = y2 - x2
                        cross = dx * dy
                        for kind, w in enumerate((m, one)):
                            at_acc = 8 * t + 4 * kind
                            w1 = w * inv
                            w2 = w1 * inv
                            acc[at_acc] = acc[at_acc] + w1 * dx
                            acc[at_acc + 1] = acc[at_acc + 1] + w1 * dy
                            acc[at_acc + 2] = acc[at_acc + 2] + w2 * gap
                            acc[at_acc + 3] = acc[at_acc + 3] + w2 * cross
                return tuple(acc)

            acc = lax.fori_loop(0, PPL // 4, self_pairs, (zero,) * (8 * self_width))
            for t in range(self_width):
                rows = slice(tile * PPL + base + 8 * t, tile * PPL + base + 8 * t + 8)
                for c in range(4):
                    scale = -2.0 if c == 3 else 1.0
                    result[c, rows, :] = acc[8 * t + c] * scale
                    self_live[c, rows, :] = acc[8 * t + 4 + c] * scale

    for copy in edges:
        copy.wait()
    cell_x = sides[0:1] + jnp.full((1, 128), bx, jnp.int32).astype(F32)
    cell_y = sides[1:2] + jnp.full((1, 128), by, jnp.int32).astype(F32)
    inside = jnp.where(
        (cell_x >= 0.0) & (cell_x < float(nx)) & (cell_y >= 0.0) & (cell_y < float(ny)), 1.0, 0.0
    )
    halo = recv[...].T * inside
    halo_parts = jnp.concatenate(split3(halo[0:192]), axis=1)
    row128 = lax.broadcasted_iota(jnp.int32, (128, 256), 0) + 256

    def shift_halo(o):
        hot = jnp.where(row128 == src_leaf[o : o + 1, :], 1.0, 0.0).astype(BF16)
        moved = tn_none(halo_parts, jnp.concatenate([hot] * 3, axis=0))
        off_x, off_y = OFFS[o]
        for tile in (0, 1):
            lanes = slice(tile * 128, tile * 128 + 128)
            at = at_offset(o)
            su[tile, at, :] = (su[tile, at, :] + moved[0:64, lanes]) * 0.5 + off_x
            sv[tile, at, :] = (sv[tile, at, :] + moved[64:128, lanes]) * 0.5 + off_y
            sw[tile, at, :] = sw[tile, at, :] + moved[128:192, lanes]

    for o in range(NEIGHBOURS):
        shift_halo(o)

    all_mom = jnp.concatenate([mom[...], halo[192:512]], axis=1)
    all_mom = jnp.concatenate(
        [all_mom[0:160] - near_mean * all_mom[160:320], all_mom[160:320]], axis=0
    )
    cut_mom = jnp.concatenate(split2(all_mom), axis=0)

    def shift_moments(o):
        hot = jnp.where(row256[:, 0:128] == src_mom[o : o + 1, :], 1.0, 0.0).astype(BF16)
        moved = tn_none(cut_mom, hot)
        at = slice(o * 160, o * 160 + 160)
        pieces = [moved[160 * i : 160 * i + 160] for i in range(4)]
        xs[at, :] = jnp.concatenate([p[:, 0:64] for p in pieces], axis=1).astype(BF16)
        xs_par[at, :] = jnp.concatenate([p[:, 64:80] for p in pieces], axis=1).astype(BF16)

    for o in range(9):
        shift_moments(o)

    wide = tn_none(hi_par[...], xs_par[...])
    par = wide[:, 0:32] + wide[:, 32:64] + tn_none(lo_par[...], xs_par[:, 0:32])
    par_cols = jnp.concatenate(
        [
            par[c * 160 + q * NM : c * 160 + q * NM + NM, kind * 16 : kind * 16 + 16]
            for kind in (0, 1)
            for c in range(4)
            for q in range(4)
        ],
        axis=1,
    )
    from_par = jnp.dot(
        down[...], par_cols, precision=HIGHEST, preferred_element_type=F32
    )
    for arrival in arrivals[12:]:
        arrival.wait()
    wide = tn_none(hi_leaf[...], xs[...])
    leaf = wide[:, 0:128] + wide[:, 128:256] + tn_none(lo_leaf[...], xs[:, 0:128])
    for kind in (0, 1):
        for c in range(4):
            at = kind * 256 + c * 64
            leaf_kind[kind, c] = jnp.concatenate(
                [
                    leaf[c * 160 + ch * NM : c * 160 + ch * NM + NM, kind * 64 : kind * 64 + 64]
                    + from_par[ch * NM : ch * NM + NM, at : at + 64]
                    for ch in range(4)
                ],
                axis=1,
            )

    sums = lax.fori_loop(1, high_n, add_high, mid[...])
    mass_sum = jnp.sum(sums[0:1], axis=1, keepdims=True)
    live_sum = jnp.sum(sums[1:2], axis=1, keepdims=True)
    mean = mass_sum / live_sum
    for tile in (0, 1):
        m = sw[tile, 0:self_at, :]
        sw[tile, 0:self_at, :] = jnp.where(m > 0.0, m - mean, 0.0)
    for c in range(4):
        leaf_local[c] = leaf_kind[0, c] - (mean - near_mean) * leaf_kind[1, c]

    for tile in (0, 1):
        lanes = slice(tile * 128, tile * 128 + 128)
        bu = basis(own[0:64, lanes])
        bv = basis(own[64:128, lanes])
        for c in range(4):
            rows = slice(tile * PPL, tile * PPL + PPL)
            acc = result[c, rows, :] - (mean - near_mean) * self_live[c, rows, :]
            for a in range(NODES):
                half = leaf_local[c, pl.ds(a * 6, 1), lanes] * bv[0]
                for b in range(1, NODES):
                    half = half + leaf_local[c, pl.ds(a * 6 + b, 1), lanes] * bv[b]
                acc = acc + half * bu[a]
            result[c, rows, :] = acc

    near_field(0, self_at)

    for c in range(4):
        back = result[c].T
        for i, s in enumerate(starts):
            out[pl.ds(s * 4 + c, 16, stride=32), :] = back[16 * i : 16 * i + 16]


def vmem():
    return pl.BlockSpec(memory_space=pltpu.VMEM)


NAMES = ("src_leaf", "sel_leaf", "sel_mom", "up", "t_rows", "t_cols", "sides", "src_mom", "down",
         "hi_leaf", "lo_leaf")
OPERANDS = 3 + len(NAMES)


def on_device(particle_pos, particle_mass, leaf_counts):
    dev_count = lax.axis_size("dev")
    bits = (lax.axis_size("grp") * dev_count).bit_length() - 1
    low_n = 2 ** (bits // 2)
    high_n = 2**bits // low_n
    pos = particle_pos.reshape(2, 128, 128).transpose(1, 0, 2).reshape(256, 128)
    mass = particle_mass.reshape(128, 128)
    count = leaf_counts.reshape(2, 128)
    operands = (pos, mass, count, *[jnp.asarray(CONST[k]) for k in NAMES])
    out = pl.pallas_call(
        functools.partial(whole_kernel, dev_count, bits),
        out_shape=jax.ShapeDtypeStruct((512, 128), F32),
        in_specs=[pl.BlockSpec(memory_space=pltpu.HBM)] * OPERANDS,
        out_specs=vmem(),
        scratch_shapes=[pltpu.VMEM(x.shape, x.dtype) for x in operands]
        + [
            pltpu.SemaphoreType.DMA((OPERANDS,)),
            pltpu.VMEM((192, 256), F32),
            pltpu.VMEM((320, 128), F32),
            pltpu.VMEM((HROWS, LANES_OUT), F32),
            pltpu.VMEM((HROWS, LANES_OUT), F32),
            pltpu.VMEM((8, 128), F32),
            pltpu.VMEM((8, 128), F32),
            pltpu.VMEM((2 * NM, 256), F32),
            pltpu.VMEM((low_n, 8, 128), F32),
            pltpu.VMEM((high_n, 8, 128), F32),
            pltpu.VMEM((2, 9 * PPL + 8, 128), F32),
            pltpu.VMEM((2, 9 * PPL + 8, 128), F32),
            pltpu.VMEM((2, 9 * PPL + 8, 128), F32),
            pltpu.VMEM((2, PPL + 8, 128), F32),
            pltpu.VMEM((1440, 256), BF16),
            pltpu.VMEM((1440, 64), BF16),
            pltpu.VMEM((640, 1440), BF16),
            pltpu.VMEM((640, 1440), BF16),
            pltpu.VMEM((2, 4, NM, 256), F32),
            pltpu.VMEM((4, NM, 256), F32),
            pltpu.VMEM((4, 128, 128), F32),
            pltpu.VMEM((4, 128, 128), F32),
            pltpu.SemaphoreType.DMA((8,)),
            pltpu.SemaphoreType.DMA((8,)),
            pltpu.SemaphoreType.DMA((low_n,)),
            pltpu.SemaphoreType.DMA((low_n,)),
            pltpu.SemaphoreType.DMA((high_n,)),
            pltpu.SemaphoreType.DMA((high_n,)),
        ],
        compiler_params=pltpu.CompilerParams(
            collective_id=0, has_side_effects=True, vmem_limit_bytes=63 * 2**20
        ),
        name="fields",
    )(*operands)
    return out.reshape(128, 4, 128).transpose(1, 0, 2).reshape(4, LSIDE * LSIDE * PPL)


def solution(mesh):
    in_specs = (P(None, ("grp", "dev")), P(("grp", "dev")), P(("grp", "dev")))
    out_specs = P(None, ("grp", "dev"))
    return jax.shard_map(
        on_device, mesh=mesh, in_specs=in_specs, out_specs=out_specs, check_vma=False
    )
```

```python
import functools

import jax
import jax.numpy as jnp
import numpy as np
from jax import lax
from jax.experimental import pallas as pl
from jax.experimental.pallas import tpu as pltpu
from jax.sharding import PartitionSpec as P

NODES = 6
PPL = 64
LSIDE = 16
SOFTEN = 0.01
NM = 40
HIGHEST = lax.Precision.HIGHEST
F32 = jnp.float32
BF16 = jnp.bfloat16

DIRS = ((-1, 0), (1, 0), (0, -1), (0, 1), (-1, -1), (1, -1), (-1, 1), (1, 1))
ROW_OF = (0, 16, 32, 48, 64, 72, 80, 88)
ROWS_IN = (16, 16, 16, 16, 8, 8, 8, 8)
HROWS = 128
LANES_OUT = 512
OFFS = tuple((ox, oy) for ox in (-1, 0, 1) for oy in (-1, 0, 1) if (ox, oy) != (0, 0)) + ((0, 0),)
NEIGHBOURS = 8
FILL_LANES = 256


def gp_col(gx, gy):
    return (gx & 1) + 2 * (gy & 1) + 4 * (gx >> 1) + 8 * (gy >> 1)


def par_col(px, py):
    return (px & 1) * 32 + (py & 1) * 16 + gp_col(px >> 1, py >> 1)


def leaf_col(x, y):
    return (x & 1) * 128 + (y & 1) * 64 + par_col(x >> 1, y >> 1)


def halo_cells(side):
    cells = []
    for dx, dy in DIRS:
        ex = -1 if dx < 0 else side
        ey = -1 if dy < 0 else side
        if dy == 0:
            cells.append([(ex, j) for j in range(side)])
        elif dx == 0:
            cells.append([(j, ey) for j in range(side)])
        else:
            cells.append([(ex, ey)])
    return cells


def pick_rows(side, col, base, lanes):
    out = np.zeros((HROWS, lanes), np.float32)
    for d, cells in enumerate(halo_cells(side)):
        for j, (cx, cy) in enumerate(cells):
            out[ROW_OF[d] + base[d] + j, col(cx % side, cy % side)] = 1.0
    return out


PAR_BASE = (0,) * 8
GP_BASE = (8,) * 4 + (1,) * 4


def shift_index(side, col, base, own_at, halo_at):
    where = {}
    for x in range(side):
        for y in range(side):
            where[x, y] = own_at + col(x, y)
    for d, cells in enumerate(halo_cells(side)):
        for j, cell in enumerate(cells):
            where[cell] = halo_at + ROW_OF[d] + base[d] + j
    out = np.zeros((9, side * side), np.int32)
    for o, (ox, oy) in enumerate(OFFS):
        for x in range(side):
            for y in range(side):
                out[o, col(x, y)] = where[x + ox, y + oy]
    return out


def cheb(u):
    terms = [u * 0 + 1.0, u]
    for _ in range(NODES - 2):
        terms.append(2.0 * u * terms[-1] - terms[-2])
    return terms


ANGLES = (2.0 * np.arange(NODES) + 1.0) * np.pi / (2.0 * NODES)
POINTS = np.cos(ANGLES)
S_COEF = 2.0 / NODES * np.cos(np.arange(NODES)[:, None] * ANGLES[None, :])
S_COEF[0] = 1.0 / NODES


def basis(u):
    terms = cheb(u)
    out = []
    for k in range(NODES):
        total = S_COEF[0, k] + float(S_COEF[1, k]) * terms[1]
        for n in range(2, NODES):
            total = total + float(S_COEF[n, k]) * terms[n]
        out.append(total)
    return out


def child_table():
    side = []
    for s in (0, 1):
        side.append(np.stack(basis(s - 0.5 + POINTS / 2), axis=1))
    out = np.zeros((4, NM, NM), np.float32)
    for sx in (0, 1):
        for sy in (0, 1):
            prod = side[sx][:, None, :, None] * side[sy][None, :, None, :]
            out[2 * sx + sy, :36, :36] = prod.reshape(36, 36)
    return out


def cell_vectors():
    coord = np.zeros((2, 4, NM), np.float32)
    cell = np.zeros((2, 4, NM), np.float32)
    for sx in (0, 1):
        for sy in (0, 1):
            ch = 2 * sx + sy
            node = np.arange(36)
            coord[0, ch] = sx - 0.5
            coord[1, ch] = sy - 0.5
            coord[0, ch, :36] += 0.5 * POINTS[node // 6]
            coord[1, ch, :36] += 0.5 * POINTS[node % 6]
            cell[0, ch] = sx
            cell[1, ch] = sy
    return coord.reshape(2, 4 * NM), cell.reshape(2, 4 * NM)


def constants():
    c = {}
    c["sel_leaf"] = pick_rows(LSIDE, leaf_col, PAR_BASE, 256).astype(BF16)
    sel_par = pick_rows(LSIDE // 2, par_col, PAR_BASE, 64)
    sel_gp = pick_rows(LSIDE // 4, gp_col, GP_BASE, 64)
    c["sel_mom"] = np.concatenate([sel_par, sel_gp], axis=1).astype(BF16)
    table = child_table()
    c["up"] = np.transpose(table, (2, 0, 1)).reshape(NM, 4 * NM)
    c["down"] = table.reshape(4 * NM, NM)
    src = np.zeros((16, 256), np.int32)
    src[:9] = shift_index(LSIDE, leaf_col, PAR_BASE, 0, 256)
    for x in range(LSIDE):
        for y in range(LSIDE):
            src[9, leaf_col(x, y)] = sum(
                (x >> k & 1) << 2 * k | (y >> k & 1) << 2 * k + 1 for k in range(4)
            )
    c["src_leaf"] = src
    msrc = np.full((16, 128), -1, np.int32)
    msrc[:9, :64] = shift_index(LSIDE // 2, par_col, PAR_BASE, 0, 128)
    msrc[:9, 64:80] = shift_index(LSIDE // 4, gp_col, GP_BASE, 64, 128)
    c["src_mom"] = msrc
    coord, cell = cell_vectors()
    rows = np.zeros((160, 128), np.float32)
    rows[:, 0:2] = coord.T
    rows[:, 2:4] = cell.T
    c["t_rows"] = rows
    cols = np.zeros((8, 9, 160), np.float32)
    for o, (ox, oy) in enumerate(OFFS):
        cols[0, o] = coord[0] + 2 * ox
        cols[1, o] = coord[1] + 2 * oy
        cols[2, o] = cell[0] + 2 * ox
        cols[3, o] = cell[1] + 2 * oy
    c["t_cols"] = cols.reshape(8, 1440)
    far_x = coord[0][:, None] - cols[0].reshape(1440)[None, :]
    far_y = coord[1][:, None] - cols[1].reshape(1440)[None, :]
    gap = np.maximum(
        np.abs(cell[0][:, None] - cols[2].reshape(1440)[None, :]),
        np.abs(cell[1][:, None] - cols[3].reshape(1440)[None, :]),
    )
    for name, scale in (("leaf", 1.0), ("par", 2.0)):
        sx, sy = far_x * scale, far_y * scale
        inv = np.where(gap > 1.5, 1.0 / (sx**2 + sy**2 + SOFTEN), 0.0)
        kx, ky = sx * inv, sy * inv
        full = np.concatenate([kx, ky, ky * ky - kx * kx, -2.0 * kx * ky]).astype(np.float32)
        c["hi_" + name] = full.astype(BF16)
        c["lo_" + name] = (full - c["hi_" + name].astype(np.float32)).astype(BF16)
    sides = np.zeros((8, HROWS), np.float32)
    for d, (dx, dy) in enumerate(DIRS):
        sides[0, ROW_OF[d] : ROW_OF[d] + ROWS_IN[d]] = dx
        sides[1, ROW_OF[d] : ROW_OF[d] + ROWS_IN[d]] = dy
    c["sides"] = sides
    return c


CONST = constants()


def split2(x):
    hi = x.astype(BF16)
    return hi, (x - hi.astype(F32)).astype(BF16)


def split3(x):
    hi = x.astype(BF16)
    rest = x - hi.astype(F32)
    mid = rest.astype(BF16)
    return hi, mid, (rest - mid.astype(F32)).astype(BF16)


def nt_dot(a, b):
    return lax.dot_general(a, b, (((1,), (1,)), ((), ())), preferred_element_type=F32)


def tn_none(a, b):
    return lax.dot_general(a, b, (((1,), (0,)), ((), ())), preferred_element_type=F32)


def morton_split(code, bits):
    cx, cy = 0, 0
    for level in range((bits + 1) // 2):
        cx = cx + code // 4**level % 2 * 2**level
        cy = cy + code // (2 * 4**level) % 2 * 2**level
    return cx, cy


def morton_join(cx, cy, bits):
    code = 0
    for level in range((bits + 1) // 2):
        code = code + cx // 2**level % 2 * 4**level
        code = code + cy // 2**level % 2 * 2 * 4**level
    return code


def whole_kernel(dev_count, bits, *refs):
    sources, refs = refs[:OPERANDS], refs[OPERANDS:]
    out, refs = refs[0], refs[1:]
    held, refs = refs[:OPERANDS], refs[OPERANDS:]
    (pos, mass, count, src_leaf, sel_leaf, sel_mom, up, t_rows, t_cols, sides, src_mom,
     down, hi_par, lo_par, hi_leaf, lo_leaf) = held
    arrive_sems = refs[0]
    arrivals = [
        pltpu.make_async_copy(src, dst, arrive_sems.at[i])
        for i, (src, dst) in enumerate(zip(sources, held))
    ]
    for i in (1, 2, 3, 0, *range(4, OPERANDS)):
        arrivals[i].start()
    run_kernel(dev_count, bits, arrivals, pos, mass, count, sel_leaf, sel_mom, up, down, sides,
               src_leaf, src_mom, t_rows, t_cols, hi_par, lo_par, hi_leaf, lo_leaf, out, *refs[1:])


def run_kernel(dev_count, bits, arrivals, pos, mass, count, sel_leaf, sel_mom, up, down, sides,
               src_leaf, src_mom, t_rows, t_cols, hi_par, lo_par, hi_leaf, lo_leaf, out, own, mom, send, recv, part, mid, leaf_mom, first,
                 second, su, sv, sw, lone, xs, xs_par, leaf_kind, leaf_local,
                 result, self_live, edge_s, edge_r, sum_s1, sum_r1, sum_s2, sum_r2):
    code = lax.axis_index("grp") * dev_count + lax.axis_index("dev")
    bx, by = morton_split(code, bits)
    nx, ny = 2 ** ((bits + 1) // 2), 2 ** (bits // 2)
    low_n = 2 ** (bits // 2)
    high_n = 2**bits // low_n
    low, high = code % low_n, code // low_n

    def device(c):
        return {"grp": c // dev_count, "dev": c % dev_count}

    def beside(dx, dy):
        return device(morton_join((bx + dx + nx) % nx, (by + dy + ny) % ny, bits))

    def in_low(k):
        return device(high * low_n + (low + k) % low_n)

    def in_high(k):
        return device((high + k) % high_n * low_n + low)

    barrier = pltpu.get_barrier_semaphore()

    def greet(who):
        pl.semaphore_signal(barrier, inc=1, device_id=who, device_id_type=pl.DeviceIdType.MESH)

    def greet_low(k, carry):
        greet(in_low(k))
        return carry

    def greet_high(k, carry):
        greet(in_high(k))
        return carry

    lax.fori_loop(1, low_n, greet_low, 0)
    for dx, dy in DIRS:
        greet(beside(dx, dy))
    lax.fori_loop(1, high_n, greet_high, 0)

    starts = [qx * 2 + qy * 4 + sy for sy in (0, 1) for qx in (0, 1) for qy in (0, 1)]

    def turned(ref, lead, step):
        rows = jnp.concatenate(
            [ref[pl.ds(lead + step * s, 16, stride=8 * step), :] for s in starts], axis=0
        )
        return rows.T

    for arrival in arrivals[1:4]:
        arrival.wait()
    row256 = lax.broadcasted_iota(jnp.int32, (256, 256), 0)
    pick = jnp.where(row256 == src_leaf[9:10, :], 1.0, 0.0).astype(BF16)
    linear = count[...].astype(F32).astype(BF16)
    counts = tn_none(linear[0:1], pick[0:128]) + tn_none(linear[1:2], pick[128:256])
    m_turned = turned(mass, 0, 1)
    slot = lax.broadcasted_iota(jnp.int32, (PPL, 128), 0).astype(F32)
    totals = []
    for tile in (0, 1):
        lanes = slice(tile * 128, tile * 128 + 128)
        live = slot < counts[:, lanes]
        vals = jnp.where(live, m_turned[tile * PPL : tile * PPL + PPL], 0.0)
        own[128:192, lanes] = vals
        totals.append(jnp.sum(vals, axis=0, keepdims=True))
    near_mean = jnp.sum(totals[0] + totals[1], axis=1, keepdims=True) / jnp.sum(
        counts, axis=1, keepdims=True
    )
    row = lax.broadcasted_iota(jnp.int32, (8, 128), 0)
    part[...] = jnp.where(
        row == 0,
        totals[0] + totals[1],
        jnp.where(row == 1, counts[:, 0:128] + counts[:, 128:256], 0.0),
    )

    def low_copy(k):
        return pltpu.make_async_remote_copy(
            src_ref=part, dst_ref=first.at[k], send_sem=sum_s1.at[k], recv_sem=sum_r1.at[k],
            device_id=in_low(k), device_id_type=pl.DeviceIdType.MESH,
        )

    def high_copy(k):
        return pltpu.make_async_remote_copy(
            src_ref=mid, dst_ref=second.at[k], send_sem=sum_s2.at[k], recv_sem=sum_r2.at[k],
            device_id=in_high(k), device_id_type=pl.DeviceIdType.MESH,
        )

    def start_low(k, carry):
        low_copy(k).start()
        return carry

    def start_high(k, carry):
        high_copy(k).start()
        return carry

    def add_low(k, acc):
        low_copy(k).wait()
        return acc + first[k]

    def add_high(k, acc):
        high_copy(k).wait()
        return acc + second[k]

    pl.semaphore_wait(barrier, 8 + low_n - 1 + high_n - 1)
    lax.fori_loop(1, low_n, start_low, 0)
    arrivals[0].wait()
    for k in (0, 1):
        vals = turned(pos, k, 2)
        own[k * PPL : (k + 1) * PPL, 0:128] = vals[:PPL]
        own[k * PPL : (k + 1) * PPL, 128:256] = vals[PPL:]

    for arrival in arrivals[4:12]:
        arrival.wait()
    leaf_mom[...] = jnp.zeros_like(leaf_mom)
    for tile in (0, 1):
        lanes = slice(tile * 128, tile * 128 + 128)
        bu = basis(own[0:64, lanes])
        bv = basis(own[64:128, lanes])
        m_t = own[128:192, lanes]
        live_t = jnp.where(m_t > 0.0, 1.0, 0.0)
        for kind, weight in enumerate((m_t, live_t)):
            for a in range(NODES):
                wa = bu[a] * weight
                for b in range(NODES):
                    leaf_mom[pl.ds(kind * NM + a * 6 + b, 1), lanes] = jnp.sum(
                        wa * bv[b], axis=0, keepdims=True
                    )
    mom[...] = jnp.zeros_like(mom)
    stacked = []
    for kind in (0, 1):
        block = jnp.concatenate(
            [
                leaf_mom[kind * NM : (kind + 1) * NM, ch * 64 : ch * 64 + 64]
                for ch in range(4)
            ],
            axis=0,
        )
        mom[kind * 160 : kind * 160 + 160, 0:64] = block
        stacked.append(block)
    par = jnp.dot(
        up[...], jnp.concatenate(stacked, axis=1), precision=HIGHEST, preferred_element_type=F32
    )
    for kind in (0, 1):
        for q in range(4):
            at = kind * 64 + q * 16
            mom[pl.ds(kind * 160 + q * NM, NM), 64:80] = par[:, at : at + 16]
    own_cut = split3(own[...])
    send[:, 0:192] = nt_dot(
        jnp.concatenate([sel_leaf[...]] * 3, axis=1), jnp.concatenate(own_cut, axis=1)
    )
    send[:, 192:512] = nt_dot(
        jnp.concatenate([sel_mom[...]] * 3, axis=1),
        jnp.concatenate(split3(mom[...]), axis=1),
    )
    edges = []
    for d, (dx, dy) in enumerate(DIRS):
        rows = pl.ds(ROW_OF[d], ROWS_IN[d])
        copy = pltpu.make_async_remote_copy(
            src_ref=send.at[rows], dst_ref=recv.at[rows], send_sem=edge_s.at[d],
            recv_sem=edge_r.at[d], device_id=beside(-dx, -dy),
            device_id_type=pl.DeviceIdType.MESH,
        )
        copy.start()
        edges.append(copy)
    recv[96:HROWS, :] = jnp.zeros((HROWS - 96, LANES_OUT), F32)

    def at_offset(o):
        return slice(o * PPL, o * PPL + PPL)

    own_parts = jnp.concatenate(own_cut, axis=1)

    def shift_own(o):
        hot = jnp.where(row256 == src_leaf[o : o + 1, :], 1.0, 0.0).astype(BF16)
        moved = tn_none(own_parts, jnp.concatenate([hot] * 3, axis=0))
        for tile in (0, 1):
            lanes = slice(tile * 128, tile * 128 + 128)
            su[tile, at_offset(o), :] = moved[0:64, lanes]
            sv[tile, at_offset(o), :] = moved[64:128, lanes]
            sw[tile, at_offset(o), :] = moved[128:192, lanes]

    for o in range(NEIGHBOURS):
        shift_own(o)
    self_at = NEIGHBOURS * PPL
    for tile in (0, 1):
        lanes = slice(tile * 128, tile * 128 + 128)
        su[tile, self_at : self_at + PPL, :] = own[0:64, lanes] * 0.5
        sv[tile, self_at : self_at + PPL, :] = own[64:128, lanes] * 0.5
        m = own[128:192, lanes]
        sw[tile, self_at : self_at + PPL, :] = jnp.where(m > 0.0, m - near_mean, 0.0)
        lone[tile, 0:PPL, :] = jnp.where(m > 0.0, 1.0, 0.0)

    def near_field(first_row, row_count):
        width, unroll = 4, 16
        for tile in (0, 1):
            for piece in range(PPL // (8 * width)):
                base = piece * 8 * width
                tx, ty = targets(tile, base, width)

                def pairs(step, acc, tile=tile, tx=tx, ty=ty):
                    acc = list(acc)
                    for i in range(unroll):
                        at = pl.ds(first_row + step * unroll + i, 8, stride=0)
                        sx, sy, w = su[tile, at, :], sv[tile, at, :], sw[tile, at, :]
                        for t in range(width):
                            dx = tx[t] - sx
                            dy = ty[t] - sy
                            inv = 1.0 / (dy * dy + (dx * dx + SOFTEN))
                            kx = dx * inv
                            ky = dy * inv
                            wx = w * kx
                            wy = w * ky
                            acc[4 * t] = acc[4 * t] + wx
                            acc[4 * t + 1] = acc[4 * t + 1] + wy
                            acc[4 * t + 2] = (acc[4 * t + 2] + wy * ky) - wx * kx
                            acc[4 * t + 3] = acc[4 * t + 3] + wx * ky
                    return tuple(acc)

                acc = lax.fori_loop(0, row_count // unroll, pairs, (zero,) * (4 * width))
                for t in range(width):
                    rows = slice(tile * PPL + base + 8 * t, tile * PPL + base + 8 * t + 8)
                    for c in range(4):
                        near = acc[4 * t + c]
                        if c == 3:
                            near = near * -2.0
                        result[c, rows, :] = result[c, rows, :] + near

    mid[...] = lax.fori_loop(1, low_n, add_low, part[...])
    lax.fori_loop(1, high_n, start_high, 0)

    zero = jnp.zeros((8, 128), F32)

    def targets(tile, base, width):
        lanes = slice(tile * 128, tile * 128 + 128)
        tx = [own[base + 8 * i : base + 8 * i + 8, lanes] * 0.5 for i in range(width)]
        ty = [own[64 + base + 8 * i : 72 + base + 8 * i, lanes] * 0.5 for i in range(width)]
        return tx, ty

    self_width = 2
    for tile in (0, 1):
        for piece in range(PPL // (8 * self_width)):
            base = piece * 8 * self_width
            tx, ty = targets(tile, base, self_width)

            def self_pairs(step, acc, tile=tile, tx=tx, ty=ty):
                acc = list(acc)
                for i in range(4):
                    k = step * 4 + i
                    at = pl.ds(self_at + k, 8, stride=0)
                    sx, sy, m = su[tile, at, :], sv[tile, at, :], sw[tile, at, :]
                    one = lone[tile, pl.ds(k, 8, stride=0), :]
                    for t in range(self_width):
                        dx = tx[t] - sx
                        dy = ty[t] - sy
                        x2 = dx * dx
                        y2 = dy * dy
                        inv = 1.0 / (x2 + y2 + SOFTEN)
                        gap = y2 - x2
                        cross = dx * dy
                        for kind, w in enumerate((m, one)):
                            at_acc = 8 * t + 4 * kind
                            w1 = w * inv
                            w2 = w1 * inv
                            acc[at_acc] = acc[at_acc] + w1 * dx
                            acc[at_acc + 1] = acc[at_acc + 1] + w1 * dy
                            acc[at_acc + 2] = acc[at_acc + 2] + w2 * gap
                            acc[at_acc + 3] = acc[at_acc + 3] + w2 * cross
                return tuple(acc)

            acc = lax.fori_loop(0, PPL // 4, self_pairs, (zero,) * (8 * self_width))
            for t in range(self_width):
                rows = slice(tile * PPL + base + 8 * t, tile * PPL + base + 8 * t + 8)
                for c in range(4):
                    scale = -2.0 if c == 3 else 1.0
                    result[c, rows, :] = acc[8 * t + c] * scale
                    self_live[c, rows, :] = acc[8 * t + 4 + c] * scale

    for copy in edges:
        copy.wait()
    cell_x = sides[0:1] + jnp.full((1, 128), bx, jnp.int32).astype(F32)
    cell_y = sides[1:2] + jnp.full((1, 128), by, jnp.int32).astype(F32)
    inside = jnp.where(
        (cell_x >= 0.0) & (cell_x < float(nx)) & (cell_y >= 0.0) & (cell_y < float(ny)), 1.0, 0.0
    )
    halo = recv[...].T * inside
    halo_parts = jnp.concatenate(split3(halo[0:192]), axis=1)
    row128 = lax.broadcasted_iota(jnp.int32, (128, 256), 0) + 256

    def shift_halo(o):
        hot = jnp.where(row128 == src_leaf[o : o + 1, :], 1.0, 0.0).astype(BF16)
        moved = tn_none(halo_parts, jnp.concatenate([hot] * 3, axis=0))
        off_x, off_y = OFFS[o]
        for tile in (0, 1):
            lanes = slice(tile * 128, tile * 128 + 128)
            at = at_offset(o)
            su[tile, at, :] = (su[tile, at, :] + moved[0:64, lanes]) * 0.5 + off_x
            sv[tile, at, :] = (sv[tile, at, :] + moved[64:128, lanes]) * 0.5 + off_y
            sw[tile, at, :] = sw[tile, at, :] + moved[128:192, lanes]

    for o in range(NEIGHBOURS):
        shift_halo(o)

    all_mom = jnp.concatenate([mom[...], halo[192:512]], axis=1)
    all_mom = jnp.concatenate(
        [all_mom[0:160] - near_mean * all_mom[160:320], all_mom[160:320]], axis=0
    )
    cut_mom = jnp.concatenate(split2(all_mom), axis=0)

    def shift_moments(o):
        hot = jnp.where(row256[:, 0:128] == src_mom[o : o + 1, :], 1.0, 0.0).astype(BF16)
        moved = tn_none(cut_mom, hot)
        at = slice(o * 160, o * 160 + 160)
        pieces = [moved[160 * i : 160 * i + 160] for i in range(4)]
        xs[at, :] = jnp.concatenate([p[:, 0:64] for p in pieces], axis=1).astype(BF16)
        xs_par[at, :] = jnp.concatenate([p[:, 64:80] for p in pieces], axis=1).astype(BF16)

    for o in range(9):
        shift_moments(o)

    for arrival in arrivals[12:]:
        arrival.wait()
    wide = tn_none(hi_par[...], xs_par[...])
    par = wide[:, 0:32] + wide[:, 32:64] + tn_none(lo_par[...], xs_par[:, 0:32])
    par_cols = jnp.concatenate(
        [
            par[c * 160 + q * NM : c * 160 + q * NM + NM, kind * 16 : kind * 16 + 16]
            for kind in (0, 1)
            for c in range(4)
            for q in range(4)
        ],
        axis=1,
    )
    from_par = jnp.dot(
        down[...], par_cols, precision=HIGHEST, preferred_element_type=F32
    )
    wide = tn_none(hi_leaf[...], xs[...])
    leaf = wide[:, 0:128] + wide[:, 128:256] + tn_none(lo_leaf[...], xs[:, 0:128])
    for kind in (0, 1):
        for c in range(4):
            at = kind * 256 + c * 64
            leaf_kind[kind, c] = jnp.concatenate(
                [
                    leaf[c * 160 + ch * NM : c * 160 + ch * NM + NM, kind * 64 : kind * 64 + 64]
                    + from_par[ch * NM : ch * NM + NM, at : at + 64]
                    for ch in range(4)
                ],
                axis=1,
            )

    sums = lax.fori_loop(1, high_n, add_high, mid[...])
    mass_sum = jnp.sum(sums[0:1], axis=1, keepdims=True)
    live_sum = jnp.sum(sums[1:2], axis=1, keepdims=True)
    mean = mass_sum / live_sum
    for tile in (0, 1):
        m = sw[tile, 0:self_at, :]
        sw[tile, 0:self_at, :] = jnp.where(m > 0.0, m - mean, 0.0)
    for c in range(4):
        leaf_local[c] = leaf_kind[0, c] - (mean - near_mean) * leaf_kind[1, c]

    for tile in (0, 1):
        lanes = slice(tile * 128, tile * 128 + 128)
        bu = basis(own[0:64, lanes])
        bv = basis(own[64:128, lanes])
        for c in range(4):
            rows = slice(tile * PPL, tile * PPL + PPL)
            acc = result[c, rows, :] - (mean - near_mean) * self_live[c, rows, :]
            for a in range(NODES):
                half = leaf_local[c, pl.ds(a * 6, 1), lanes] * bv[0]
                for b in range(1, NODES):
                    half = half + leaf_local[c, pl.ds(a * 6 + b, 1), lanes] * bv[b]
                acc = acc + half * bu[a]
            result[c, rows, :] = acc

    near_field(0, self_at)

    for c in range(4):
        back = result[c].T
        for i, s in enumerate(starts):
            out[pl.ds(s * 4 + c, 16, stride=32), :] = back[16 * i : 16 * i + 16]


def vmem():
    return pl.BlockSpec(memory_space=pltpu.VMEM)


NAMES = ("src_leaf", "sel_leaf", "sel_mom", "up", "t_rows", "t_cols", "sides", "src_mom", "down",
         "hi_par", "lo_par", "hi_leaf", "lo_leaf")
OPERANDS = 3 + len(NAMES)


def on_device(particle_pos, particle_mass, leaf_counts):
    dev_count = lax.axis_size("dev")
    bits = (lax.axis_size("grp") * dev_count).bit_length() - 1
    low_n = 2 ** (bits // 2)
    high_n = 2**bits // low_n
    pos = particle_pos.reshape(2, 128, 128).transpose(1, 0, 2).reshape(256, 128)
    mass = particle_mass.reshape(128, 128)
    count = leaf_counts.reshape(2, 128)
    operands = (pos, mass, count, *[jnp.asarray(CONST[k]) for k in NAMES])
    out = pl.pallas_call(
        functools.partial(whole_kernel, dev_count, bits),
        out_shape=jax.ShapeDtypeStruct((512, 128), F32),
        in_specs=[pl.BlockSpec(memory_space=pltpu.HBM)] * OPERANDS,
        out_specs=vmem(),
        scratch_shapes=[pltpu.VMEM(x.shape, x.dtype) for x in operands]
        + [
            pltpu.SemaphoreType.DMA((OPERANDS,)),
            pltpu.VMEM((192, 256), F32),
            pltpu.VMEM((320, 128), F32),
            pltpu.VMEM((HROWS, LANES_OUT), F32),
            pltpu.VMEM((HROWS, LANES_OUT), F32),
            pltpu.VMEM((8, 128), F32),
            pltpu.VMEM((8, 128), F32),
            pltpu.VMEM((2 * NM, 256), F32),
            pltpu.VMEM((low_n, 8, 128), F32),
            pltpu.VMEM((high_n, 8, 128), F32),
            pltpu.VMEM((2, 9 * PPL + 8, 128), F32),
            pltpu.VMEM((2, 9 * PPL + 8, 128), F32),
            pltpu.VMEM((2, 9 * PPL + 8, 128), F32),
            pltpu.VMEM((2, PPL + 8, 128), F32),
            pltpu.VMEM((1440, 256), BF16),
            pltpu.VMEM((1440, 64), BF16),
            pltpu.VMEM((2, 4, NM, 256), F32),
            pltpu.VMEM((4, NM, 256), F32),
            pltpu.VMEM((4, 128, 128), F32),
            pltpu.VMEM((4, 128, 128), F32),
            pltpu.SemaphoreType.DMA((8,)),
            pltpu.SemaphoreType.DMA((8,)),
            pltpu.SemaphoreType.DMA((low_n,)),
            pltpu.SemaphoreType.DMA((low_n,)),
            pltpu.SemaphoreType.DMA((high_n,)),
            pltpu.SemaphoreType.DMA((high_n,)),
        ],
        compiler_params=pltpu.CompilerParams(
            collective_id=0, has_side_effects=True, vmem_limit_bytes=63 * 2**20
        ),
        name="fields",
    )(*operands)
    return out.reshape(128, 4, 128).transpose(1, 0, 2).reshape(4, LSIDE * LSIDE * PPL)


def solution(mesh):
    in_specs = (P(None, ("grp", "dev")), P(("grp", "dev")), P(("grp", "dev")))
    out_specs = P(None, ("grp", "dev"))
    return jax.shard_map(
        on_device, mesh=mesh, in_specs=in_specs, out_specs=out_specs, check_vma=False
    )
```

```python
import functools

import jax
import jax.numpy as jnp
import numpy as np
from jax import lax
from jax.experimental import pallas as pl
from jax.experimental.pallas import tpu as pltpu
from jax.sharding import PartitionSpec as P

NODES = 6
PPL = 64
LSIDE = 16
SOFTEN = 0.01
NM = 40
HIGHEST = lax.Precision.HIGHEST
F32 = jnp.float32
BF16 = jnp.bfloat16

DIRS = ((-1, 0), (1, 0), (0, -1), (0, 1), (-1, -1), (1, -1), (-1, 1), (1, 1))
ROW_OF = (0, 16, 32, 48, 64, 72, 80, 88)
ROWS_IN = (16, 16, 16, 16, 8, 8, 8, 8)
HROWS = 128
LANES_OUT = 512
OFFS = tuple((ox, oy) for ox in (-1, 0, 1) for oy in (-1, 0, 1) if (ox, oy) != (0, 0)) + ((0, 0),)
NEIGHBOURS = 8
FILL_LANES = 256


def gp_col(gx, gy):
    return (gx & 1) + 2 * (gy & 1) + 4 * (gx >> 1) + 8 * (gy >> 1)


def par_col(px, py):
    return (px & 1) * 32 + (py & 1) * 16 + gp_col(px >> 1, py >> 1)


def leaf_col(x, y):
    return (x & 1) * 128 + (y & 1) * 64 + par_col(x >> 1, y >> 1)


def halo_cells(side):
    cells = []
    for dx, dy in DIRS:
        ex = -1 if dx < 0 else side
        ey = -1 if dy < 0 else side
        if dy == 0:
            cells.append([(ex, j) for j in range(side)])
        elif dx == 0:
            cells.append([(j, ey) for j in range(side)])
        else:
            cells.append([(ex, ey)])
    return cells


def pick_rows(side, col, base, lanes):
    out = np.zeros((HROWS, lanes), np.float32)
    for d, cells in enumerate(halo_cells(side)):
        for j, (cx, cy) in enumerate(cells):
            out[ROW_OF[d] + base[d] + j, col(cx % side, cy % side)] = 1.0
    return out


PAR_BASE = (0,) * 8
GP_BASE = (8,) * 4 + (1,) * 4


def shift_index(side, col, base, own_at, halo_at):
    where = {}
    for x in range(side):
        for y in range(side):
            where[x, y] = own_at + col(x, y)
    for d, cells in enumerate(halo_cells(side)):
        for j, cell in enumerate(cells):
            where[cell] = halo_at + ROW_OF[d] + base[d] + j
    out = np.zeros((9, side * side), np.int32)
    for o, (ox, oy) in enumerate(OFFS):
        for x in range(side):
            for y in range(side):
                out[o, col(x, y)] = where[x + ox, y + oy]
    return out


def cheb(u):
    terms = [u * 0 + 1.0, u]
    for _ in range(NODES - 2):
        terms.append(2.0 * u * terms[-1] - terms[-2])
    return terms


ANGLES = (2.0 * np.arange(NODES) + 1.0) * np.pi / (2.0 * NODES)
POINTS = np.cos(ANGLES)
S_COEF = 2.0 / NODES * np.cos(np.arange(NODES)[:, None] * ANGLES[None, :])
S_COEF[0] = 1.0 / NODES


def basis(u):
    terms = cheb(u)
    out = []
    for k in range(NODES):
        total = S_COEF[0, k] + float(S_COEF[1, k]) * terms[1]
        for n in range(2, NODES):
            total = total + float(S_COEF[n, k]) * terms[n]
        out.append(total)
    return out


def child_table():
    side = []
    for s in (0, 1):
        side.append(np.stack(basis(s - 0.5 + POINTS / 2), axis=1))
    out = np.zeros((4, NM, NM), np.float32)
    for sx in (0, 1):
        for sy in (0, 1):
            prod = side[sx][:, None, :, None] * side[sy][None, :, None, :]
            out[2 * sx + sy, :36, :36] = prod.reshape(36, 36)
    return out


def cell_vectors():
    coord = np.zeros((2, 4, NM), np.float32)
    cell = np.zeros((2, 4, NM), np.float32)
    for sx in (0, 1):
        for sy in (0, 1):
            ch = 2 * sx + sy
            node = np.arange(36)
            coord[0, ch] = sx - 0.5
            coord[1, ch] = sy - 0.5
            coord[0, ch, :36] += 0.5 * POINTS[node // 6]
            coord[1, ch, :36] += 0.5 * POINTS[node % 6]
            cell[0, ch] = sx
            cell[1, ch] = sy
    return coord.reshape(2, 4 * NM), cell.reshape(2, 4 * NM)


def constants():
    c = {}
    c["sel_leaf"] = pick_rows(LSIDE, leaf_col, PAR_BASE, 256).astype(BF16)
    sel_par = pick_rows(LSIDE // 2, par_col, PAR_BASE, 64)
    sel_gp = pick_rows(LSIDE // 4, gp_col, GP_BASE, 64)
    c["sel_mom"] = np.concatenate([sel_par, sel_gp], axis=1).astype(BF16)
    table = child_table()
    c["up"] = np.transpose(table, (2, 0, 1)).reshape(NM, 4 * NM)
    c["down"] = table.reshape(4 * NM, NM)
    src = np.zeros((16, 256), np.int32)
    src[:9] = shift_index(LSIDE, leaf_col, PAR_BASE, 0, 256)
    for x in range(LSIDE):
        for y in range(LSIDE):
            src[9, leaf_col(x, y)] = sum(
                (x >> k & 1) << 2 * k | (y >> k & 1) << 2 * k + 1 for k in range(4)
            )
    c["src_leaf"] = src
    msrc = np.full((16, 128), -1, np.int32)
    msrc[:9, :64] = shift_index(LSIDE // 2, par_col, PAR_BASE, 0, 128)
    msrc[:9, 64:80] = shift_index(LSIDE // 4, gp_col, GP_BASE, 64, 128)
    c["src_mom"] = msrc
    coord, cell = cell_vectors()
    rows = np.zeros((160, 128), np.float32)
    rows[:, 0:2] = coord.T
    rows[:, 2:4] = cell.T
    c["t_rows"] = rows
    cols = np.zeros((8, 9, 160), np.float32)
    for o, (ox, oy) in enumerate(OFFS):
        cols[0, o] = coord[0] + 2 * ox
        cols[1, o] = coord[1] + 2 * oy
        cols[2, o] = cell[0] + 2 * ox
        cols[3, o] = cell[1] + 2 * oy
    c["t_cols"] = cols.reshape(8, 1440)
    far_x = coord[0][:, None] - cols[0].reshape(1440)[None, :]
    far_y = coord[1][:, None] - cols[1].reshape(1440)[None, :]
    gap = np.maximum(
        np.abs(cell[0][:, None] - cols[2].reshape(1440)[None, :]),
        np.abs(cell[1][:, None] - cols[3].reshape(1440)[None, :]),
    )
    for name, scale in (("leaf", 1.0), ("par", 2.0)):
        sx, sy = far_x * scale, far_y * scale
        inv = np.where(gap > 1.5, 1.0 / (sx**2 + sy**2 + SOFTEN), 0.0)
        kx, ky = sx * inv, sy * inv
        full = np.concatenate([kx, ky, ky * ky - kx * kx, -2.0 * kx * ky]).astype(np.float32)
        c["hi_" + name] = full.astype(BF16)
        c["lo_" + name] = (full - c["hi_" + name].astype(np.float32)).astype(BF16)
    sides = np.zeros((8, HROWS), np.float32)
    for d, (dx, dy) in enumerate(DIRS):
        sides[0, ROW_OF[d] : ROW_OF[d] + ROWS_IN[d]] = dx
        sides[1, ROW_OF[d] : ROW_OF[d] + ROWS_IN[d]] = dy
    c["sides"] = sides
    return c


CONST = constants()


def split2(x):
    hi = x.astype(BF16)
    return hi, (x - hi.astype(F32)).astype(BF16)


def split3(x):
    hi = x.astype(BF16)
    rest = x - hi.astype(F32)
    mid = rest.astype(BF16)
    return hi, mid, (rest - mid.astype(F32)).astype(BF16)


def nt_dot(a, b):
    return lax.dot_general(a, b, (((1,), (1,)), ((), ())), preferred_element_type=F32)


def tn_none(a, b):
    return lax.dot_general(a, b, (((1,), (0,)), ((), ())), preferred_element_type=F32)


def morton_split(code, bits):
    cx, cy = 0, 0
    for level in range((bits + 1) // 2):
        cx = cx + code // 4**level % 2 * 2**level
        cy = cy + code // (2 * 4**level) % 2 * 2**level
    return cx, cy


def morton_join(cx, cy, bits):
    code = 0
    for level in range((bits + 1) // 2):
        code = code + cx // 2**level % 2 * 4**level
        code = code + cy // 2**level % 2 * 2 * 4**level
    return code


def whole_kernel(dev_count, bits, *refs):
    sources, refs = refs[:OPERANDS], refs[OPERANDS:]
    out, refs = refs[0], refs[1:]
    held, refs = refs[:OPERANDS], refs[OPERANDS:]
    (pos, mass, count, src_leaf, sel_leaf, sel_mom, up, t_rows, t_cols, sides, src_mom,
     down, hi_par, lo_par, hi_leaf, lo_leaf) = held
    arrive_sems = refs[0]
    arrivals = [
        pltpu.make_async_copy(src, dst, arrive_sems.at[i])
        for i, (src, dst) in enumerate(zip(sources, held))
    ]
    for i in (1, 2, 3, 0, *range(4, OPERANDS)):
        arrivals[i].start()
    run_kernel(dev_count, bits, arrivals, pos, mass, count, sel_leaf, sel_mom, up, down, sides,
               src_leaf, src_mom, t_rows, t_cols, hi_par, lo_par, hi_leaf, lo_leaf, out, *refs[1:])


def run_kernel(dev_count, bits, arrivals, pos, mass, count, sel_leaf, sel_mom, up, down, sides,
               src_leaf, src_mom, t_rows, t_cols, hi_par, lo_par, hi_leaf, lo_leaf, out, own, mom, send, recv, part, mid, leaf_mom, first,
                 second, su, sv, sw, lone, xs, xs_par, leaf_kind, leaf_local,
                 result, self_live, edge_s, edge_r, sum_s1, sum_r1, sum_s2, sum_r2):
    code = lax.axis_index("grp") * dev_count + lax.axis_index("dev")
    bx, by = morton_split(code, bits)
    nx, ny = 2 ** ((bits + 1) // 2), 2 ** (bits // 2)
    low_n = 2 ** (bits // 2)
    high_n = 2**bits // low_n
    low, high = code % low_n, code // low_n

    def device(c):
        return {"grp": c // dev_count, "dev": c % dev_count}

    def beside(dx, dy):
        return device(morton_join((bx + dx + nx) % nx, (by + dy + ny) % ny, bits))

    def in_low(k):
        return device(high * low_n + (low + k) % low_n)

    def in_high(k):
        return device((high + k) % high_n * low_n + low)

    barrier = pltpu.get_barrier_semaphore()

    def greet(who):
        pl.semaphore_signal(barrier, inc=1, device_id=who, device_id_type=pl.DeviceIdType.MESH)

    def greet_low(k, carry):
        greet(in_low(k))
        return carry

    def greet_high(k, carry):
        greet(in_high(k))
        return carry

    lax.fori_loop(1, low_n, greet_low, 0)
    for dx, dy in DIRS:
        greet(beside(dx, dy))
    lax.fori_loop(1, high_n, greet_high, 0)

    starts = [qx * 2 + qy * 4 + sy for sy in (0, 1) for qx in (0, 1) for qy in (0, 1)]

    def turned(ref, lead, step):
        rows = jnp.concatenate(
            [ref[pl.ds(lead + step * s, 16, stride=8 * step), :] for s in starts], axis=0
        )
        return rows.T

    for arrival in arrivals[1:4]:
        arrival.wait()
    row256 = lax.broadcasted_iota(jnp.int32, (256, 256), 0)
    pick = jnp.where(row256 == src_leaf[9:10, :], 1.0, 0.0).astype(BF16)
    linear = count[...].astype(F32).astype(BF16)
    counts = tn_none(linear[0:1], pick[0:128]) + tn_none(linear[1:2], pick[128:256])
    m_turned = turned(mass, 0, 1)
    slot = lax.broadcasted_iota(jnp.int32, (PPL, 128), 0).astype(F32)
    totals = []
    for tile in (0, 1):
        lanes = slice(tile * 128, tile * 128 + 128)
        live = slot < counts[:, lanes]
        vals = jnp.where(live, m_turned[tile * PPL : tile * PPL + PPL], 0.0)
        own[128:192, lanes] = vals
        totals.append(jnp.sum(vals, axis=0, keepdims=True))
    near_mean = jnp.sum(totals[0] + totals[1], axis=1, keepdims=True) / jnp.sum(
        counts, axis=1, keepdims=True
    )
    row = lax.broadcasted_iota(jnp.int32, (8, 128), 0)
    part[...] = jnp.where(
        row == 0,
        totals[0] + totals[1],
        jnp.where(row == 1, counts[:, 0:128] + counts[:, 128:256], 0.0),
    )

    def low_copy(k):
        return pltpu.make_async_remote_copy(
            src_ref=part, dst_ref=first.at[k], send_sem=sum_s1.at[k], recv_sem=sum_r1.at[k],
            device_id=in_low(k), device_id_type=pl.DeviceIdType.MESH,
        )

    def high_copy(k):
        return pltpu.make_async_remote_copy(
            src_ref=mid, dst_ref=second.at[k], send_sem=sum_s2.at[k], recv_sem=sum_r2.at[k],
            device_id=in_high(k), device_id_type=pl.DeviceIdType.MESH,
        )

    def start_low(k, carry):
        low_copy(k).start()
        return carry

    def start_high(k, carry):
        high_copy(k).start()
        return carry

    def add_low(k, acc):
        low_copy(k).wait()
        return acc + first[k]

    def add_high(k, acc):
        high_copy(k).wait()
        return acc + second[k]

    pl.semaphore_wait(barrier, 8 + low_n - 1 + high_n - 1)
    lax.fori_loop(1, low_n, start_low, 0)
    arrivals[0].wait()
    for k in (0, 1):
        vals = turned(pos, k, 2)
        own[k * PPL : (k + 1) * PPL, 0:128] = vals[:PPL]
        own[k * PPL : (k + 1) * PPL, 128:256] = vals[PPL:]

    for arrival in arrivals[4:12]:
        arrival.wait()
    leaf_mom[...] = jnp.zeros_like(leaf_mom)
    for tile in (0, 1):
        lanes = slice(tile * 128, tile * 128 + 128)
        bu = basis(own[0:64, lanes])
        bv = basis(own[64:128, lanes])
        m_t = own[128:192, lanes]
        live_t = jnp.where(m_t > 0.0, 1.0, 0.0)
        for kind, weight in enumerate((m_t, live_t)):
            for a in range(NODES):
                wa = bu[a] * weight
                for b in range(NODES):
                    leaf_mom[pl.ds(kind * NM + a * 6 + b, 1), lanes] = jnp.sum(
                        wa * bv[b], axis=0, keepdims=True
                    )
    mom[...] = jnp.zeros_like(mom)
    stacked = []
    for kind in (0, 1):
        block = jnp.concatenate(
            [
                leaf_mom[kind * NM : (kind + 1) * NM, ch * 64 : ch * 64 + 64]
                for ch in range(4)
            ],
            axis=0,
        )
        mom[kind * 160 : kind * 160 + 160, 0:64] = block
        stacked.append(block)
    par = jnp.dot(
        up[...], jnp.concatenate(stacked, axis=1), precision=HIGHEST, preferred_element_type=F32
    )
    for kind in (0, 1):
        for q in range(4):
            at = kind * 64 + q * 16
            mom[pl.ds(kind * 160 + q * NM, NM), 64:80] = par[:, at : at + 16]
    own_cut = split3(own[...])
    send[:, 0:192] = nt_dot(
        jnp.concatenate([sel_leaf[...]] * 3, axis=1), jnp.concatenate(own_cut, axis=1)
    )
    send[:, 192:512] = nt_dot(
        jnp.concatenate([sel_mom[...]] * 3, axis=1),
        jnp.concatenate(split3(mom[...]), axis=1),
    )
    edges = []
    for d, (dx, dy) in enumerate(DIRS):
        rows = pl.ds(ROW_OF[d], ROWS_IN[d])
        copy = pltpu.make_async_remote_copy(
            src_ref=send.at[rows], dst_ref=recv.at[rows], send_sem=edge_s.at[d],
            recv_sem=edge_r.at[d], device_id=beside(-dx, -dy),
            device_id_type=pl.DeviceIdType.MESH,
        )
        copy.start()
        edges.append(copy)
    recv[96:HROWS, :] = jnp.zeros((HROWS - 96, LANES_OUT), F32)

    def at_offset(o):
        return slice(o * PPL, o * PPL + PPL)

    own_parts = jnp.concatenate(own_cut, axis=1)

    def shift_own(o):
        hot = jnp.where(row256 == src_leaf[o : o + 1, :], 1.0, 0.0).astype(BF16)
        moved = tn_none(own_parts, jnp.concatenate([hot] * 3, axis=0))
        for tile in (0, 1):
            lanes = slice(tile * 128, tile * 128 + 128)
            su[tile, at_offset(o), :] = moved[0:64, lanes]
            sv[tile, at_offset(o), :] = moved[64:128, lanes]
            sw[tile, at_offset(o), :] = moved[128:192, lanes]

    for o in range(NEIGHBOURS):
        shift_own(o)
    self_at = NEIGHBOURS * PPL
    for tile in (0, 1):
        lanes = slice(tile * 128, tile * 128 + 128)
        su[tile, self_at : self_at + PPL, :] = own[0:64, lanes] * 0.5
        sv[tile, self_at : self_at + PPL, :] = own[64:128, lanes] * 0.5
        m = own[128:192, lanes]
        sw[tile, self_at : self_at + PPL, :] = jnp.where(m > 0.0, m - near_mean, 0.0)
        lone[tile, 0:PPL, :] = jnp.where(m > 0.0, 1.0, 0.0)

    def near_field(first_row, row_count):
        width, unroll = 4, 16
        for tile in (0, 1):
            for piece in range(PPL // (8 * width)):
                base = piece * 8 * width
                tx, ty = targets(tile, base, width)

                def pairs(step, acc, tile=tile, tx=tx, ty=ty):
                    acc = list(acc)
                    for i in range(unroll):
                        at = pl.ds(first_row + step * unroll + i, 8, stride=0)
                        sx, sy, w = su[tile, at, :], sv[tile, at, :], sw[tile, at, :]
                        for t in range(width):
                            dx = tx[t] - sx
                            dy = ty[t] - sy
                            inv = 1.0 / (dy * dy + (dx * dx + SOFTEN))
                            kx = dx * inv
                            ky = dy * inv
                            wx = w * kx
                            wy = w * ky
                            acc[4 * t] = acc[4 * t] + wx
                            acc[4 * t + 1] = acc[4 * t + 1] + wy
                            acc[4 * t + 2] = (acc[4 * t + 2] + wy * ky) - wx * kx
                            acc[4 * t + 3] = acc[4 * t + 3] + wx * ky
                    return tuple(acc)

                acc = lax.fori_loop(0, row_count // unroll, pairs, (zero,) * (4 * width))
                for t in range(width):
                    rows = slice(tile * PPL + base + 8 * t, tile * PPL + base + 8 * t + 8)
                    for c in range(4):
                        near = acc[4 * t + c]
                        if c == 3:
                            near = near * -2.0
                        result[c, rows, :] = result[c, rows, :] + near

    zero = jnp.zeros((8, 128), F32)

    def targets(tile, base, width):
        lanes = slice(tile * 128, tile * 128 + 128)
        tx = [own[base + 8 * i : base + 8 * i + 8, lanes] * 0.5 for i in range(width)]
        ty = [own[64 + base + 8 * i : 72 + base + 8 * i, lanes] * 0.5 for i in range(width)]
        return tx, ty

    self_width = 2
    for tile in (0, 1):
        if tile == 1:
            mid[...] = lax.fori_loop(1, low_n, add_low, part[...])
            lax.fori_loop(1, high_n, start_high, 0)
        for piece in range(PPL // (8 * self_width)):
            base = piece * 8 * self_width
            tx, ty = targets(tile, base, self_width)

            def self_pairs(step, acc, tile=tile, tx=tx, ty=ty):
                acc = list(acc)
                for i in range(4):
                    k = step * 4 + i
                    at = pl.ds(self_at + k, 8, stride=0)
                    sx, sy, m = su[tile, at, :], sv[tile, at, :], sw[tile, at, :]
                    one = lone[tile, pl.ds(k, 8, stride=0), :]
                    for t in range(self_width):
                        dx = tx[t] - sx
                        dy = ty[t] - sy
                        x2 = dx * dx
                        y2 = dy * dy
                        inv = 1.0 / (x2 + y2 + SOFTEN)
                        gap = y2 - x2
                        cross = dx * dy
                        for kind, w in enumerate((m, one)):
                            at_acc = 8 * t + 4 * kind
                            w1 = w * inv
                            w2 = w1 * inv
                            acc[at_acc] = acc[at_acc] + w1 * dx
                            acc[at_acc + 1] = acc[at_acc + 1] + w1 * dy
                            acc[at_acc + 2] = acc[at_acc + 2] + w2 * gap
                            acc[at_acc + 3] = acc[at_acc + 3] + w2 * cross
                return tuple(acc)

            acc = lax.fori_loop(0, PPL // 4, self_pairs, (zero,) * (8 * self_width))
            for t in range(self_width):
                rows = slice(tile * PPL + base + 8 * t, tile * PPL + base + 8 * t + 8)
                for c in range(4):
                    scale = -2.0 if c == 3 else 1.0
                    result[c, rows, :] = acc[8 * t + c] * scale
                    self_live[c, rows, :] = acc[8 * t + 4 + c] * scale

    for copy in edges:
        copy.wait()
    cell_x = sides[0:1] + jnp.full((1, 128), bx, jnp.int32).astype(F32)
    cell_y = sides[1:2] + jnp.full((1, 128), by, jnp.int32).astype(F32)
    inside = jnp.where(
        (cell_x >= 0.0) & (cell_x < float(nx)) & (cell_y >= 0.0) & (cell_y < float(ny)), 1.0, 0.0
    )
    halo = recv[...].T * inside
    halo_parts = jnp.concatenate(split3(halo[0:192]), axis=1)
    row128 = lax.broadcasted_iota(jnp.int32, (128, 256), 0) + 256

    def shift_halo(o):
        hot = jnp.where(row128 == src_leaf[o : o + 1, :], 1.0, 0.0).astype(BF16)
        moved = tn_none(halo_parts, jnp.concatenate([hot] * 3, axis=0))
        off_x, off_y = OFFS[o]
        for tile in (0, 1):
            lanes = slice(tile * 128, tile * 128 + 128)
            at = at_offset(o)
            su[tile, at, :] = (su[tile, at, :] + moved[0:64, lanes]) * 0.5 + off_x
            sv[tile, at, :] = (sv[tile, at, :] + moved[64:128, lanes]) * 0.5 + off_y
            sw[tile, at, :] = sw[tile, at, :] + moved[128:192, lanes]

    for o in range(NEIGHBOURS):
        shift_halo(o)

    all_mom = jnp.concatenate([mom[...], halo[192:512]], axis=1)
    all_mom = jnp.concatenate(
        [all_mom[0:160] - near_mean * all_mom[160:320], all_mom[160:320]], axis=0
    )
    cut_mom = jnp.concatenate(split2(all_mom), axis=0)

    def shift_moments(o):
        hot = jnp.where(row256[:, 0:128] == src_mom[o : o + 1, :], 1.0, 0.0).astype(BF16)
        moved = tn_none(cut_mom, hot)
        at = slice(o * 160, o * 160 + 160)
        pieces = [moved[160 * i : 160 * i + 160] for i in range(4)]
        xs[at, :] = jnp.concatenate([p[:, 0:64] for p in pieces], axis=1).astype(BF16)
        xs_par[at, :] = jnp.concatenate([p[:, 64:80] for p in pieces], axis=1).astype(BF16)

    for o in range(9):
        shift_moments(o)

    for arrival in arrivals[12:]:
        arrival.wait()
    wide = tn_none(hi_par[...], xs_par[...])
    par = wide[:, 0:32] + wide[:, 32:64] + tn_none(lo_par[...], xs_par[:, 0:32])
    par_cols = jnp.concatenate(
        [
            par[c * 160 + q * NM : c * 160 + q * NM + NM, kind * 16 : kind * 16 + 16]
            for kind in (0, 1)
            for c in range(4)
            for q in range(4)
        ],
        axis=1,
    )
    from_par = jnp.dot(
        down[...], par_cols, precision=HIGHEST, preferred_element_type=F32
    )
    wide = tn_none(hi_leaf[...], xs[...])
    leaf = wide[:, 0:128] + wide[:, 128:256] + tn_none(lo_leaf[...], xs[:, 0:128])
    for kind in (0, 1):
        for c in range(4):
            at = kind * 256 + c * 64
            leaf_kind[kind, c] = jnp.concatenate(
                [
                    leaf[c * 160 + ch * NM : c * 160 + ch * NM + NM, kind * 64 : kind * 64 + 64]
                    + from_par[ch * NM : ch * NM + NM, at : at + 64]
                    for ch in range(4)
                ],
                axis=1,
            )

    sums = lax.fori_loop(1, high_n, add_high, mid[...])
    mass_sum = jnp.sum(sums[0:1], axis=1, keepdims=True)
    live_sum = jnp.sum(sums[1:2], axis=1, keepdims=True)
    mean = mass_sum / live_sum
    for tile in (0, 1):
        m = sw[tile, 0:self_at, :]
        sw[tile, 0:self_at, :] = jnp.where(m > 0.0, m - mean, 0.0)
    for c in range(4):
        leaf_local[c] = leaf_kind[0, c] - (mean - near_mean) * leaf_kind[1, c]

    for tile in (0, 1):
        lanes = slice(tile * 128, tile * 128 + 128)
        bu = basis(own[0:64, lanes])
        bv = basis(own[64:128, lanes])
        for c in range(4):
            rows = slice(tile * PPL, tile * PPL + PPL)
            acc = result[c, rows, :] - (mean - near_mean) * self_live[c, rows, :]
            for a in range(NODES):
                half = leaf_local[c, pl.ds(a * 6, 1), lanes] * bv[0]
                for b in range(1, NODES):
                    half = half + leaf_local[c, pl.ds(a * 6 + b, 1), lanes] * bv[b]
                acc = acc + half * bu[a]
            result[c, rows, :] = acc

    near_field(0, self_at)

    for c in range(4):
        back = result[c].T
        for i, s in enumerate(starts):
            out[pl.ds(s * 4 + c, 16, stride=32), :] = back[16 * i : 16 * i + 16]


def vmem():
    return pl.BlockSpec(memory_space=pltpu.VMEM)


NAMES = ("src_leaf", "sel_leaf", "sel_mom", "up", "t_rows", "t_cols", "sides", "src_mom", "down",
         "hi_par", "lo_par", "hi_leaf", "lo_leaf")
OPERANDS = 3 + len(NAMES)


def on_device(particle_pos, particle_mass, leaf_counts):
    dev_count = lax.axis_size("dev")
    bits = (lax.axis_size("grp") * dev_count).bit_length() - 1
    low_n = 2 ** (bits // 2)
    high_n = 2**bits // low_n
    pos = particle_pos.reshape(2, 128, 128).transpose(1, 0, 2).reshape(256, 128)
    mass = particle_mass.reshape(128, 128)
    count = leaf_counts.reshape(2, 128)
    operands = (pos, mass, count, *[jnp.asarray(CONST[k]) for k in NAMES])
    out = pl.pallas_call(
        functools.partial(whole_kernel, dev_count, bits),
        out_shape=jax.ShapeDtypeStruct((512, 128), F32),
        in_specs=[pl.BlockSpec(memory_space=pltpu.HBM)] * OPERANDS,
        out_specs=vmem(),
        scratch_shapes=[pltpu.VMEM(x.shape, x.dtype) for x in operands]
        + [
            pltpu.SemaphoreType.DMA((OPERANDS,)),
            pltpu.VMEM((192, 256), F32),
            pltpu.VMEM((320, 128), F32),
            pltpu.VMEM((HROWS, LANES_OUT), F32),
            pltpu.VMEM((HROWS, LANES_OUT), F32),
            pltpu.VMEM((8, 128), F32),
            pltpu.VMEM((8, 128), F32),
            pltpu.VMEM((2 * NM, 256), F32),
            pltpu.VMEM((low_n, 8, 128), F32),
            pltpu.VMEM((high_n, 8, 128), F32),
            pltpu.VMEM((2, 9 * PPL + 8, 128), F32),
            pltpu.VMEM((2, 9 * PPL + 8, 128), F32),
            pltpu.VMEM((2, 9 * PPL + 8, 128), F32),
            pltpu.VMEM((2, PPL + 8, 128), F32),
            pltpu.VMEM((1440, 256), BF16),
            pltpu.VMEM((1440, 64), BF16),
            pltpu.VMEM((2, 4, NM, 256), F32),
            pltpu.VMEM((4, NM, 256), F32),
            pltpu.VMEM((4, 128, 128), F32),
            pltpu.VMEM((4, 128, 128), F32),
            pltpu.SemaphoreType.DMA((8,)),
            pltpu.SemaphoreType.DMA((8,)),
            pltpu.SemaphoreType.DMA((low_n,)),
            pltpu.SemaphoreType.DMA((low_n,)),
            pltpu.SemaphoreType.DMA((high_n,)),
            pltpu.SemaphoreType.DMA((high_n,)),
        ],
        compiler_params=pltpu.CompilerParams(
            collective_id=0, has_side_effects=True, vmem_limit_bytes=63 * 2**20
        ),
        name="fields",
    )(*operands)
    return out.reshape(128, 4, 128).transpose(1, 0, 2).reshape(4, LSIDE * LSIDE * PPL)


def solution(mesh):
    in_specs = (P(None, ("grp", "dev")), P(("grp", "dev")), P(("grp", "dev")))
    out_specs = P(None, ("grp", "dev"))
    return jax.shard_map(
        on_device, mesh=mesh, in_specs=in_specs, out_specs=out_specs, check_vma=False
    )
```

```python
import functools

import jax
import jax.numpy as jnp
import numpy as np
from jax import lax
from jax.experimental import pallas as pl
from jax.experimental.pallas import tpu as pltpu
from jax.sharding import PartitionSpec as P

NODES = 6
PPL = 64
LSIDE = 16
SOFTEN = 0.01
NM = 40
HIGHEST = lax.Precision.HIGHEST
F32 = jnp.float32
BF16 = jnp.bfloat16

DIRS = ((-1, 0), (1, 0), (0, -1), (0, 1), (-1, -1), (1, -1), (-1, 1), (1, 1))
ROW_OF = (0, 16, 32, 48, 64, 72, 80, 88)
ROWS_IN = (16, 16, 16, 16, 8, 8, 8, 8)
ROWS_SENT = (16, 16, 16, 16, 2, 2, 2, 2)
HROWS = 128
LANES_OUT = 512
OFFS = tuple((ox, oy) for ox in (-1, 0, 1) for oy in (-1, 0, 1) if (ox, oy) != (0, 0)) + ((0, 0),)
NEIGHBOURS = 8
FILL_LANES = 256


def gp_col(gx, gy):
    return (gx & 1) + 2 * (gy & 1) + 4 * (gx >> 1) + 8 * (gy >> 1)


def par_col(px, py):
    return (px & 1) * 32 + (py & 1) * 16 + gp_col(px >> 1, py >> 1)


def leaf_col(x, y):
    return (x & 1) * 128 + (y & 1) * 64 + par_col(x >> 1, y >> 1)


def halo_cells(side):
    cells = []
    for dx, dy in DIRS:
        ex = -1 if dx < 0 else side
        ey = -1 if dy < 0 else side
        if dy == 0:
            cells.append([(ex, j) for j in range(side)])
        elif dx == 0:
            cells.append([(j, ey) for j in range(side)])
        else:
            cells.append([(ex, ey)])
    return cells


def pick_rows(side, col, base, lanes):
    out = np.zeros((HROWS, lanes), np.float32)
    for d, cells in enumerate(halo_cells(side)):
        for j, (cx, cy) in enumerate(cells):
            out[ROW_OF[d] + base[d] + j, col(cx % side, cy % side)] = 1.0
    return out


PAR_BASE = (0,) * 8
GP_BASE = (8,) * 4 + (1,) * 4


def shift_index(side, col, base, own_at, halo_at):
    where = {}
    for x in range(side):
        for y in range(side):
            where[x, y] = own_at + col(x, y)
    for d, cells in enumerate(halo_cells(side)):
        for j, cell in enumerate(cells):
            where[cell] = halo_at + ROW_OF[d] + base[d] + j
    out = np.zeros((9, side * side), np.int32)
    for o, (ox, oy) in enumerate(OFFS):
        for x in range(side):
            for y in range(side):
                out[o, col(x, y)] = where[x + ox, y + oy]
    return out


def cheb(u):
    terms = [u * 0 + 1.0, u]
    for _ in range(NODES - 2):
        terms.append(2.0 * u * terms[-1] - terms[-2])
    return terms


ANGLES = (2.0 * np.arange(NODES) + 1.0) * np.pi / (2.0 * NODES)
POINTS = np.cos(ANGLES)
S_COEF = 2.0 / NODES * np.cos(np.arange(NODES)[:, None] * ANGLES[None, :])
S_COEF[0] = 1.0 / NODES


def basis(u):
    terms = cheb(u)
    out = []
    for k in range(NODES):
        total = S_COEF[0, k] + float(S_COEF[1, k]) * terms[1]
        for n in range(2, NODES):
            total = total + float(S_COEF[n, k]) * terms[n]
        out.append(total)
    return out


def child_table():
    side = []
    for s in (0, 1):
        side.append(np.stack(basis(s - 0.5 + POINTS / 2), axis=1))
    out = np.zeros((4, NM, NM), np.float32)
    for sx in (0, 1):
        for sy in (0, 1):
            prod = side[sx][:, None, :, None] * side[sy][None, :, None, :]
            out[2 * sx + sy, :36, :36] = prod.reshape(36, 36)
    return out


def cell_vectors():
    coord = np.zeros((2, 4, NM), np.float32)
    cell = np.zeros((2, 4, NM), np.float32)
    for sx in (0, 1):
        for sy in (0, 1):
            ch = 2 * sx + sy
            node = np.arange(36)
            coord[0, ch] = sx - 0.5
            coord[1, ch] = sy - 0.5
            coord[0, ch, :36] += 0.5 * POINTS[node // 6]
            coord[1, ch, :36] += 0.5 * POINTS[node % 6]
            cell[0, ch] = sx
            cell[1, ch] = sy
    return coord.reshape(2, 4 * NM), cell.reshape(2, 4 * NM)


def constants():
    c = {}
    c["sel_leaf"] = pick_rows(LSIDE, leaf_col, PAR_BASE, 256).astype(BF16)
    sel_par = pick_rows(LSIDE // 2, par_col, PAR_BASE, 64)
    sel_gp = pick_rows(LSIDE // 4, gp_col, GP_BASE, 64)
    c["sel_mom"] = np.concatenate([sel_par, sel_gp], axis=1).astype(BF16)
    table = child_table()
    c["up"] = np.transpose(table, (2, 0, 1)).reshape(NM, 4 * NM)
    c["down"] = table.reshape(4 * NM, NM)
    src = np.zeros((16, 256), np.int32)
    src[:9] = shift_index(LSIDE, leaf_col, PAR_BASE, 0, 256)
    for x in range(LSIDE):
        for y in range(LSIDE):
            src[9, leaf_col(x, y)] = sum(
                (x >> k & 1) << 2 * k | (y >> k & 1) << 2 * k + 1 for k in range(4)
            )
    c["src_leaf"] = src
    msrc = np.full((16, 128), -1, np.int32)
    msrc[:9, :64] = shift_index(LSIDE // 2, par_col, PAR_BASE, 0, 128)
    msrc[:9, 64:80] = shift_index(LSIDE // 4, gp_col, GP_BASE, 64, 128)
    c["src_mom"] = msrc
    coord, cell = cell_vectors()
    rows = np.zeros((160, 128), np.float32)
    rows[:, 0:2] = coord.T
    rows[:, 2:4] = cell.T
    c["t_rows"] = rows
    cols = np.zeros((8, 9, 160), np.float32)
    for o, (ox, oy) in enumerate(OFFS):
        cols[0, o] = coord[0] + 2 * ox
        cols[1, o] = coord[1] + 2 * oy
        cols[2, o] = cell[0] + 2 * ox
        cols[3, o] = cell[1] + 2 * oy
    c["t_cols"] = cols.reshape(8, 1440)
    far_x = coord[0][:, None] - cols[0].reshape(1440)[None, :]
    far_y = coord[1][:, None] - cols[1].reshape(1440)[None, :]
    gap = np.maximum(
        np.abs(cell[0][:, None] - cols[2].reshape(1440)[None, :]),
        np.abs(cell[1][:, None] - cols[3].reshape(1440)[None, :]),
    )
    for name, scale in (("leaf", 1.0), ("par", 2.0)):
        sx, sy = far_x * scale, far_y * scale
        inv = np.where(gap > 1.5, 1.0 / (sx**2 + sy**2 + SOFTEN), 0.0)
        kx, ky = sx * inv, sy * inv
        full = np.concatenate([kx, ky, ky * ky - kx * kx, -2.0 * kx * ky]).astype(np.float32)
        c["hi_" + name] = full.astype(BF16)
        c["lo_" + name] = (full - c["hi_" + name].astype(np.float32)).astype(BF16)
    sides = np.zeros((8, HROWS), np.float32)
    for d, (dx, dy) in enumerate(DIRS):
        sides[0, ROW_OF[d] : ROW_OF[d] + ROWS_IN[d]] = dx
        sides[1, ROW_OF[d] : ROW_OF[d] + ROWS_IN[d]] = dy
    c["sides"] = sides
    return c


CONST = constants()


def split2(x):
    hi = x.astype(BF16)
    return hi, (x - hi.astype(F32)).astype(BF16)


def split3(x):
    hi = x.astype(BF16)
    rest = x - hi.astype(F32)
    mid = rest.astype(BF16)
    return hi, mid, (rest - mid.astype(F32)).astype(BF16)


def nt_dot(a, b):
    return lax.dot_general(a, b, (((1,), (1,)), ((), ())), preferred_element_type=F32)


def tn_none(a, b):
    return lax.dot_general(a, b, (((1,), (0,)), ((), ())), preferred_element_type=F32)


def morton_split(code, bits):
    cx, cy = 0, 0
    for level in range((bits + 1) // 2):
        cx = cx + code // 4**level % 2 * 2**level
        cy = cy + code // (2 * 4**level) % 2 * 2**level
    return cx, cy


def morton_join(cx, cy, bits):
    code = 0
    for level in range((bits + 1) // 2):
        code = code + cx // 2**level % 2 * 4**level
        code = code + cy // 2**level % 2 * 2 * 4**level
    return code


def whole_kernel(dev_count, bits, *refs):
    sources, refs = refs[:OPERANDS], refs[OPERANDS:]
    out, refs = refs[0], refs[1:]
    held, refs = refs[:OPERANDS], refs[OPERANDS:]
    (pos, mass, count, src_leaf, sel_leaf, sel_mom, up, t_rows, t_cols, sides, src_mom,
     down, hi_par, lo_par, hi_leaf, lo_leaf) = held
    arrive_sems = refs[0]
    arrivals = [
        pltpu.make_async_copy(src, dst, arrive_sems.at[i])
        for i, (src, dst) in enumerate(zip(sources, held))
    ]
    for i in (1, 2, 3, 0, *range(4, OPERANDS)):
        arrivals[i].start()
    run_kernel(dev_count, bits, arrivals, pos, mass, count, sel_leaf, sel_mom, up, down, sides,
               src_leaf, src_mom, t_rows, t_cols, hi_par, lo_par, hi_leaf, lo_leaf, out, *refs[1:])


def run_kernel(dev_count, bits, arrivals, pos, mass, count, sel_leaf, sel_mom, up, down, sides,
               src_leaf, src_mom, t_rows, t_cols, hi_par, lo_par, hi_leaf, lo_leaf, out, own, mom, send, recv, part, mid, leaf_mom, first,
                 second, su, sv, sw, lone, xs, xs_par, leaf_kind, leaf_local,
                 result, self_live, edge_s, edge_r, sum_s1, sum_r1, sum_s2, sum_r2):
    code = lax.axis_index("grp") * dev_count + lax.axis_index("dev")
    bx, by = morton_split(code, bits)
    nx, ny = 2 ** ((bits + 1) // 2), 2 ** (bits // 2)
    low_n = 2 ** (bits // 2)
    high_n = 2**bits // low_n
    low, high = code % low_n, code // low_n

    def device(c):
        return {"grp": c // dev_count, "dev": c % dev_count}

    def beside(dx, dy):
        return device(morton_join((bx + dx + nx) % nx, (by + dy + ny) % ny, bits))

    def in_low(k):
        return device(high * low_n + (low + k) % low_n)

    def in_high(k):
        return device((high + k) % high_n * low_n + low)

    barrier = pltpu.get_barrier_semaphore()

    def greet(who):
        pl.semaphore_signal(barrier, inc=1, device_id=who, device_id_type=pl.DeviceIdType.MESH)

    def greet_low(k, carry):
        greet(in_low(k))
        return carry

    def greet_high(k, carry):
        greet(in_high(k))
        return carry

    recv[64:HROWS, :] = jnp.zeros((HROWS - 64, LANES_OUT), F32)
    lax.fori_loop(1, low_n, greet_low, 0)
    for dx, dy in DIRS:
        greet(beside(dx, dy))
    lax.fori_loop(1, high_n, greet_high, 0)

    starts = [qx * 2 + qy * 4 + sy for sy in (0, 1) for qx in (0, 1) for qy in (0, 1)]

    def turned(ref, lead, step):
        rows = jnp.concatenate(
            [ref[pl.ds(lead + step * s, 16, stride=8 * step), :] for s in starts], axis=0
        )
        return rows.T

    for arrival in arrivals[1:4]:
        arrival.wait()
    row256 = lax.broadcasted_iota(jnp.int32, (256, 256), 0)
    pick = jnp.where(row256 == src_leaf[9:10, :], 1.0, 0.0).astype(BF16)
    linear = count[...].astype(F32).astype(BF16)
    counts = tn_none(linear[0:1], pick[0:128]) + tn_none(linear[1:2], pick[128:256])
    m_turned = turned(mass, 0, 1)
    slot = lax.broadcasted_iota(jnp.int32, (PPL, 128), 0).astype(F32)
    totals = []
    for tile in (0, 1):
        lanes = slice(tile * 128, tile * 128 + 128)
        live = slot < counts[:, lanes]
        vals = jnp.where(live, m_turned[tile * PPL : tile * PPL + PPL], 0.0)
        own[128:192, lanes] = vals
        totals.append(jnp.sum(vals, axis=0, keepdims=True))
    near_mean = jnp.sum(totals[0] + totals[1], axis=1, keepdims=True) / jnp.sum(
        counts, axis=1, keepdims=True
    )
    row = lax.broadcasted_iota(jnp.int32, (8, 128), 0)
    part[...] = jnp.where(
        row == 0,
        totals[0] + totals[1],
        jnp.where(row == 1, counts[:, 0:128] + counts[:, 128:256], 0.0),
    )

    def low_copy(k):
        return pltpu.make_async_remote_copy(
            src_ref=part, dst_ref=first.at[k], send_sem=sum_s1.at[k], recv_sem=sum_r1.at[k],
            device_id=in_low(k), device_id_type=pl.DeviceIdType.MESH,
        )

    def high_copy(k):
        return pltpu.make_async_remote_copy(
            src_ref=mid, dst_ref=second.at[k], send_sem=sum_s2.at[k], recv_sem=sum_r2.at[k],
            device_id=in_high(k), device_id_type=pl.DeviceIdType.MESH,
        )

    def start_low(k, carry):
        low_copy(k).start()
        return carry

    def start_high(k, carry):
        high_copy(k).start()
        return carry

    def add_low(k, acc):
        low_copy(k).wait()
        return acc + first[k]

    def add_high(k, acc):
        high_copy(k).wait()
        return acc + second[k]

    pl.semaphore_wait(barrier, 8 + low_n - 1 + high_n - 1)
    lax.fori_loop(1, low_n, start_low, 0)
    arrivals[0].wait()
    for k in (0, 1):
        vals = turned(pos, k, 2)
        own[k * PPL : (k + 1) * PPL, 0:128] = vals[:PPL]
        own[k * PPL : (k + 1) * PPL, 128:256] = vals[PPL:]

    for arrival in arrivals[4:12]:
        arrival.wait()
    leaf_mom[...] = jnp.zeros_like(leaf_mom)
    for tile in (0, 1):
        lanes = slice(tile * 128, tile * 128 + 128)
        bu = basis(own[0:64, lanes])
        bv = basis(own[64:128, lanes])
        m_t = own[128:192, lanes]
        live_t = jnp.where(m_t > 0.0, 1.0, 0.0)
        for kind, weight in enumerate((m_t, live_t)):
            for a in range(NODES):
                wa = bu[a] * weight
                for b in range(NODES):
                    leaf_mom[pl.ds(kind * NM + a * 6 + b, 1), lanes] = jnp.sum(
                        wa * bv[b], axis=0, keepdims=True
                    )
    mom[...] = jnp.zeros_like(mom)
    stacked = []
    for kind in (0, 1):
        block = jnp.concatenate(
            [
                leaf_mom[kind * NM : (kind + 1) * NM, ch * 64 : ch * 64 + 64]
                for ch in range(4)
            ],
            axis=0,
        )
        mom[kind * 160 : kind * 160 + 160, 0:64] = block
        stacked.append(block)
    par = jnp.dot(
        up[...], jnp.concatenate(stacked, axis=1), precision=HIGHEST, preferred_element_type=F32
    )
    for kind in (0, 1):
        for q in range(4):
            at = kind * 64 + q * 16
            mom[pl.ds(kind * 160 + q * NM, NM), 64:80] = par[:, at : at + 16]
    own_cut = split3(own[...])
    send[:, 0:192] = nt_dot(
        jnp.concatenate([sel_leaf[...]] * 3, axis=1), jnp.concatenate(own_cut, axis=1)
    )
    send[:, 192:512] = nt_dot(
        jnp.concatenate([sel_mom[...]] * 3, axis=1),
        jnp.concatenate(split3(mom[...]), axis=1),
    )
    edges = []
    for d, (dx, dy) in enumerate(DIRS):
        rows = pl.ds(ROW_OF[d], ROWS_SENT[d])
        copy = pltpu.make_async_remote_copy(
            src_ref=send.at[rows], dst_ref=recv.at[rows], send_sem=edge_s.at[d],
            recv_sem=edge_r.at[d], device_id=beside(-dx, -dy),
            device_id_type=pl.DeviceIdType.MESH,
        )
        copy.start()
        edges.append(copy)

    def at_offset(o):
        return slice(o * PPL, o * PPL + PPL)

    own_parts = jnp.concatenate(own_cut, axis=1)

    def shift_own(o):
        hot = jnp.where(row256 == src_leaf[o : o + 1, :], 1.0, 0.0).astype(BF16)
        moved = tn_none(own_parts, jnp.concatenate([hot] * 3, axis=0))
        for tile in (0, 1):
            lanes = slice(tile * 128, tile * 128 + 128)
            su[tile, at_offset(o), :] = moved[0:64, lanes]
            sv[tile, at_offset(o), :] = moved[64:128, lanes]
            sw[tile, at_offset(o), :] = moved[128:192, lanes]

    for o in range(NEIGHBOURS):
        shift_own(o)
    self_at = NEIGHBOURS * PPL
    for tile in (0, 1):
        lanes = slice(tile * 128, tile * 128 + 128)
        su[tile, self_at : self_at + PPL, :] = own[0:64, lanes] * 0.5
        sv[tile, self_at : self_at + PPL, :] = own[64:128, lanes] * 0.5
        m = own[128:192, lanes]
        sw[tile, self_at : self_at + PPL, :] = jnp.where(m > 0.0, m - near_mean, 0.0)
        lone[tile, 0:PPL, :] = jnp.where(m > 0.0, 1.0, 0.0)

    def near_field(first_row, row_count):
        width, unroll = 4, 16
        for tile in (0, 1):
            for piece in range(PPL // (8 * width)):
                base = piece * 8 * width
                tx, ty = targets(tile, base, width)

                def pairs(step, acc, tile=tile, tx=tx, ty=ty):
                    acc = list(acc)
                    for i in range(unroll):
                        at = pl.ds(first_row + step * unroll + i, 8, stride=0)
                        sx, sy, w = su[tile, at, :], sv[tile, at, :], sw[tile, at, :]
                        for t in range(width):
                            dx = tx[t] - sx
                            dy = ty[t] - sy
                            inv = 1.0 / (dy * dy + (dx * dx + SOFTEN))
                            kx = dx * inv
                            ky = dy * inv
                            wx = w * kx
                            wy = w * ky
                            acc[4 * t] = acc[4 * t] + wx
                            acc[4 * t + 1] = acc[4 * t + 1] + wy
                            acc[4 * t + 2] = (acc[4 * t + 2] + wy * ky) - wx * kx
                            acc[4 * t + 3] = acc[4 * t + 3] + wx * ky
                    return tuple(acc)

                acc = lax.fori_loop(0, row_count // unroll, pairs, (zero,) * (4 * width))
                for t in range(width):
                    rows = slice(tile * PPL + base + 8 * t, tile * PPL + base + 8 * t + 8)
                    for c in range(4):
                        near = acc[4 * t + c]
                        if c == 3:
                            near = near * -2.0
                        result[c, rows, :] = result[c, rows, :] + near

    zero = jnp.zeros((8, 128), F32)

    def targets(tile, base, width):
        lanes = slice(tile * 128, tile * 128 + 128)
        tx = [own[base + 8 * i : base + 8 * i + 8, lanes] * 0.5 for i in range(width)]
        ty = [own[64 + base + 8 * i : 72 + base + 8 * i, lanes] * 0.5 for i in range(width)]
        return tx, ty

    self_width = 2
    for tile in (0, 1):
        if tile == 1:
            mid[...] = lax.fori_loop(1, low_n, add_low, part[...])
            lax.fori_loop(1, high_n, start_high, 0)
        for piece in range(PPL // (8 * self_width)):
            base = piece * 8 * self_width
            tx, ty = targets(tile, base, self_width)

            def self_pairs(step, acc, tile=tile, tx=tx, ty=ty):
                acc = list(acc)
                for i in range(4):
                    k = step * 4 + i
                    at = pl.ds(self_at + k, 8, stride=0)
                    sx, sy, m = su[tile, at, :], sv[tile, at, :], sw[tile, at, :]
                    one = lone[tile, pl.ds(k, 8, stride=0), :]
                    for t in range(self_width):
                        dx = tx[t] - sx
                        dy = ty[t] - sy
                        x2 = dx * dx
                        y2 = dy * dy
                        inv = 1.0 / (x2 + y2 + SOFTEN)
                        gap = y2 - x2
                        cross = dx * dy
                        for kind, w in enumerate((m, one)):
                            at_acc = 8 * t + 4 * kind
                            w1 = w * inv
                            w2 = w1 * inv
                            acc[at_acc] = acc[at_acc] + w1 * dx
                            acc[at_acc + 1] = acc[at_acc + 1] + w1 * dy
                            acc[at_acc + 2] = acc[at_acc + 2] + w2 * gap
                            acc[at_acc + 3] = acc[at_acc + 3] + w2 * cross
                return tuple(acc)

            acc = lax.fori_loop(0, PPL // 4, self_pairs, (zero,) * (8 * self_width))
            for t in range(self_width):
                rows = slice(tile * PPL + base + 8 * t, tile * PPL + base + 8 * t + 8)
                for c in range(4):
                    scale = -2.0 if c == 3 else 1.0
                    result[c, rows, :] = acc[8 * t + c] * scale
                    self_live[c, rows, :] = acc[8 * t + 4 + c] * scale

    for copy in edges:
        copy.wait()
    cell_x = sides[0:1] + jnp.full((1, 128), bx, jnp.int32).astype(F32)
    cell_y = sides[1:2] + jnp.full((1, 128), by, jnp.int32).astype(F32)
    inside = jnp.where(
        (cell_x >= 0.0) & (cell_x < float(nx)) & (cell_y >= 0.0) & (cell_y < float(ny)), 1.0, 0.0
    )
    halo = recv[...].T * inside
    halo_parts = jnp.concatenate(split3(halo[0:192]), axis=1)
    row128 = lax.broadcasted_iota(jnp.int32, (128, 256), 0) + 256

    def shift_halo(o):
        hot = jnp.where(row128 == src_leaf[o : o + 1, :], 1.0, 0.0).astype(BF16)
        moved = tn_none(halo_parts, jnp.concatenate([hot] * 3, axis=0))
        off_x, off_y = OFFS[o]
        for tile in (0, 1):
            lanes = slice(tile * 128, tile * 128 + 128)
            at = at_offset(o)
            su[tile, at, :] = (su[tile, at, :] + moved[0:64, lanes]) * 0.5 + off_x
            sv[tile, at, :] = (sv[tile, at, :] + moved[64:128, lanes]) * 0.5 + off_y
            sw[tile, at, :] = sw[tile, at, :] + moved[128:192, lanes]

    for o in range(NEIGHBOURS):
        shift_halo(o)

    all_mom = jnp.concatenate([mom[...], halo[192:512]], axis=1)
    all_mom = jnp.concatenate(
        [all_mom[0:160] - near_mean * all_mom[160:320], all_mom[160:320]], axis=0
    )
    cut_mom = jnp.concatenate(split2(all_mom), axis=0)

    def shift_moments(o):
        hot = jnp.where(row256[:, 0:128] == src_mom[o : o + 1, :], 1.0, 0.0).astype(BF16)
        moved = tn_none(cut_mom, hot)
        at = slice(o * 160, o * 160 + 160)
        pieces = [moved[160 * i : 160 * i + 160] for i in range(4)]
        xs[at, :] = jnp.concatenate([p[:, 0:64] for p in pieces], axis=1).astype(BF16)
        xs_par[at, :] = jnp.concatenate([p[:, 64:80] for p in pieces], axis=1).astype(BF16)

    for o in range(9):
        shift_moments(o)

    for arrival in arrivals[12:]:
        arrival.wait()
    wide = tn_none(hi_par[...], xs_par[...])
    par = wide[:, 0:32] + wide[:, 32:64] + tn_none(lo_par[...], xs_par[:, 0:32])
    par_cols = jnp.concatenate(
        [
            par[c * 160 + q * NM : c * 160 + q * NM + NM, kind * 16 : kind * 16 + 16]
            for kind in (0, 1)
            for c in range(4)
            for q in range(4)
        ],
        axis=1,
    )
    from_par = jnp.dot(
        down[...], par_cols, precision=HIGHEST, preferred_element_type=F32
    )
    wide = tn_none(hi_leaf[...], xs[...])
    leaf = wide[:, 0:128] + wide[:, 128:256] + tn_none(lo_leaf[...], xs[:, 0:128])
    for kind in (0, 1):
        for c in range(4):
            at = kind * 256 + c * 64
            leaf_kind[kind, c] = jnp.concatenate(
                [
                    leaf[c * 160 + ch * NM : c * 160 + ch * NM + NM, kind * 64 : kind * 64 + 64]
                    + from_par[ch * NM : ch * NM + NM, at : at + 64]
                    for ch in range(4)
                ],
                axis=1,
            )

    sums = lax.fori_loop(1, high_n, add_high, mid[...])
    mass_sum = jnp.sum(sums[0:1], axis=1, keepdims=True)
    live_sum = jnp.sum(sums[1:2], axis=1, keepdims=True)
    mean = mass_sum / live_sum
    for tile in (0, 1):
        m = sw[tile, 0:self_at, :]
        sw[tile, 0:self_at, :] = jnp.where(m > 0.0, m - mean, 0.0)
    for c in range(4):
        leaf_local[c] = leaf_kind[0, c] - (mean - near_mean) * leaf_kind[1, c]

    for tile in (0, 1):
        lanes = slice(tile * 128, tile * 128 + 128)
        bu = basis(own[0:64, lanes])
        bv = basis(own[64:128, lanes])
        for c in range(4):
            rows = slice(tile * PPL, tile * PPL + PPL)
            acc = result[c, rows, :] - (mean - near_mean) * self_live[c, rows, :]
            for a in range(NODES):
                half = leaf_local[c, pl.ds(a * 6, 1), lanes] * bv[0]
                for b in range(1, NODES):
                    half = half + leaf_local[c, pl.ds(a * 6 + b, 1), lanes] * bv[b]
                acc = acc + half * bu[a]
            result[c, rows, :] = acc

    near_field(0, self_at)

    for c in range(4):
        back = result[c].T
        for i, s in enumerate(starts):
            out[pl.ds(s * 4 + c, 16, stride=32), :] = back[16 * i : 16 * i + 16]


def vmem():
    return pl.BlockSpec(memory_space=pltpu.VMEM)


NAMES = ("src_leaf", "sel_leaf", "sel_mom", "up", "t_rows", "t_cols", "sides", "src_mom", "down",
         "hi_par", "lo_par", "hi_leaf", "lo_leaf")
OPERANDS = 3 + len(NAMES)


def on_device(particle_pos, particle_mass, leaf_counts):
    dev_count = lax.axis_size("dev")
    bits = (lax.axis_size("grp") * dev_count).bit_length() - 1
    low_n = 2 ** (bits // 2)
    high_n = 2**bits // low_n
    pos = particle_pos.reshape(2, 128, 128).transpose(1, 0, 2).reshape(256, 128)
    mass = particle_mass.reshape(128, 128)
    count = leaf_counts.reshape(2, 128)
    operands = (pos, mass, count, *[jnp.asarray(CONST[k]) for k in NAMES])
    out = pl.pallas_call(
        functools.partial(whole_kernel, dev_count, bits),
        out_shape=jax.ShapeDtypeStruct((512, 128), F32),
        in_specs=[pl.BlockSpec(memory_space=pltpu.HBM)] * OPERANDS,
        out_specs=vmem(),
        scratch_shapes=[pltpu.VMEM(x.shape, x.dtype) for x in operands]
        + [
            pltpu.SemaphoreType.DMA((OPERANDS,)),
            pltpu.VMEM((192, 256), F32),
            pltpu.VMEM((320, 128), F32),
            pltpu.VMEM((HROWS, LANES_OUT), F32),
            pltpu.VMEM((HROWS, LANES_OUT), F32),
            pltpu.VMEM((8, 128), F32),
            pltpu.VMEM((8, 128), F32),
            pltpu.VMEM((2 * NM, 256), F32),
            pltpu.VMEM((low_n, 8, 128), F32),
            pltpu.VMEM((high_n, 8, 128), F32),
            pltpu.VMEM((2, 9 * PPL + 8, 128), F32),
            pltpu.VMEM((2, 9 * PPL + 8, 128), F32),
            pltpu.VMEM((2, 9 * PPL + 8, 128), F32),
            pltpu.VMEM((2, PPL + 8, 128), F32),
            pltpu.VMEM((1440, 256), BF16),
            pltpu.VMEM((1440, 64), BF16),
            pltpu.VMEM((2, 4, NM, 256), F32),
            pltpu.VMEM((4, NM, 256), F32),
            pltpu.VMEM((4, 128, 128), F32),
            pltpu.VMEM((4, 128, 128), F32),
            pltpu.SemaphoreType.DMA((8,)),
            pltpu.SemaphoreType.DMA((8,)),
            pltpu.SemaphoreType.DMA((low_n,)),
            pltpu.SemaphoreType.DMA((low_n,)),
            pltpu.SemaphoreType.DMA((high_n,)),
            pltpu.SemaphoreType.DMA((high_n,)),
        ],
        compiler_params=pltpu.CompilerParams(
            collective_id=0, has_side_effects=True, vmem_limit_bytes=63 * 2**20
        ),
        name="fields",
    )(*operands)
    return out.reshape(128, 4, 128).transpose(1, 0, 2).reshape(4, LSIDE * LSIDE * PPL)


def solution(mesh):
    in_specs = (P(None, ("grp", "dev")), P(("grp", "dev")), P(("grp", "dev")))
    out_specs = P(None, ("grp", "dev"))
    return jax.shard_map(
        on_device, mesh=mesh, in_specs=in_specs, out_specs=out_specs, check_vma=False
    )
```

```python
import functools

import jax
import jax.numpy as jnp
import numpy as np
from jax import lax
from jax.experimental import pallas as pl
from jax.experimental.pallas import tpu as pltpu
from jax.sharding import PartitionSpec as P

NODES = 6
PPL = 64
LSIDE = 16
SOFTEN = 0.01
NM = 40
HIGHEST = lax.Precision.HIGHEST
F32 = jnp.float32
BF16 = jnp.bfloat16

DIRS = ((-1, 0), (1, 0), (0, -1), (0, 1), (-1, -1), (1, -1), (-1, 1), (1, 1))
ROW_OF = (0, 16, 32, 48, 64, 72, 80, 88)
ROWS_IN = (16, 16, 16, 16, 8, 8, 8, 8)
ROWS_SENT = (16, 16, 16, 16, 2, 2, 2, 2)
HROWS = 128
LANES_OUT = 512
OFFS = tuple((ox, oy) for ox in (-1, 0, 1) for oy in (-1, 0, 1) if (ox, oy) != (0, 0)) + ((0, 0),)
NEIGHBOURS = 8
FILL_LANES = 256


def gp_col(gx, gy):
    return (gx & 1) + 2 * (gy & 1) + 4 * (gx >> 1) + 8 * (gy >> 1)


def par_col(px, py):
    return (px & 1) * 32 + (py & 1) * 16 + gp_col(px >> 1, py >> 1)


def leaf_col(x, y):
    return (x & 1) * 128 + (y & 1) * 64 + par_col(x >> 1, y >> 1)


def halo_cells(side):
    cells = []
    for dx, dy in DIRS:
        ex = -1 if dx < 0 else side
        ey = -1 if dy < 0 else side
        if dy == 0:
            cells.append([(ex, j) for j in range(side)])
        elif dx == 0:
            cells.append([(j, ey) for j in range(side)])
        else:
            cells.append([(ex, ey)])
    return cells


def pick_rows(side, col, base, lanes):
    out = np.zeros((HROWS, lanes), np.float32)
    for d, cells in enumerate(halo_cells(side)):
        for j, (cx, cy) in enumerate(cells):
            out[ROW_OF[d] + base[d] + j, col(cx % side, cy % side)] = 1.0
    return out


PAR_BASE = (0,) * 8
GP_BASE = (8,) * 4 + (1,) * 4


def shift_index(side, col, base, own_at, halo_at):
    where = {}
    for x in range(side):
        for y in range(side):
            where[x, y] = own_at + col(x, y)
    for d, cells in enumerate(halo_cells(side)):
        for j, cell in enumerate(cells):
            where[cell] = halo_at + ROW_OF[d] + base[d] + j
    out = np.zeros((9, side * side), np.int32)
    for o, (ox, oy) in enumerate(OFFS):
        for x in range(side):
            for y in range(side):
                out[o, col(x, y)] = where[x + ox, y + oy]
    return out


def cheb(u):
    terms = [u * 0 + 1.0, u]
    for _ in range(NODES - 2):
        terms.append(2.0 * u * terms[-1] - terms[-2])
    return terms


ANGLES = (2.0 * np.arange(NODES) + 1.0) * np.pi / (2.0 * NODES)
POINTS = np.cos(ANGLES)
S_COEF = 2.0 / NODES * np.cos(np.arange(NODES)[:, None] * ANGLES[None, :])
S_COEF[0] = 1.0 / NODES


def basis(u):
    terms = cheb(u)
    out = []
    for k in range(NODES):
        total = S_COEF[0, k] + float(S_COEF[1, k]) * terms[1]
        for n in range(2, NODES):
            total = total + float(S_COEF[n, k]) * terms[n]
        out.append(total)
    return out


def child_table():
    side = []
    for s in (0, 1):
        side.append(np.stack(basis(s - 0.5 + POINTS / 2), axis=1))
    out = np.zeros((4, NM, NM), np.float32)
    for sx in (0, 1):
        for sy in (0, 1):
            prod = side[sx][:, None, :, None] * side[sy][None, :, None, :]
            out[2 * sx + sy, :36, :36] = prod.reshape(36, 36)
    return out


def cell_vectors():
    coord = np.zeros((2, 4, NM), np.float32)
    cell = np.zeros((2, 4, NM), np.float32)
    for sx in (0, 1):
        for sy in (0, 1):
            ch = 2 * sx + sy
            node = np.arange(36)
            coord[0, ch] = sx - 0.5
            coord[1, ch] = sy - 0.5
            coord[0, ch, :36] += 0.5 * POINTS[node // 6]
            coord[1, ch, :36] += 0.5 * POINTS[node % 6]
            cell[0, ch] = sx
            cell[1, ch] = sy
    return coord.reshape(2, 4 * NM), cell.reshape(2, 4 * NM)


def constants():
    c = {}
    c["sel_leaf"] = pick_rows(LSIDE, leaf_col, PAR_BASE, 256).astype(BF16)
    sel_par = pick_rows(LSIDE // 2, par_col, PAR_BASE, 64)
    sel_gp = pick_rows(LSIDE // 4, gp_col, GP_BASE, 64)
    c["sel_mom"] = np.concatenate([sel_par, sel_gp], axis=1).astype(BF16)
    table = child_table()
    c["up"] = np.transpose(table, (2, 0, 1)).reshape(NM, 4 * NM)
    c["down"] = table.reshape(4 * NM, NM)
    src = np.zeros((16, 256), np.int32)
    src[:9] = shift_index(LSIDE, leaf_col, PAR_BASE, 0, 256)
    for x in range(LSIDE):
        for y in range(LSIDE):
            src[9, leaf_col(x, y)] = sum(
                (x >> k & 1) << 2 * k | (y >> k & 1) << 2 * k + 1 for k in range(4)
            )
    c["src_leaf"] = src
    msrc = np.full((16, 128), -1, np.int32)
    msrc[:9, :64] = shift_index(LSIDE // 2, par_col, PAR_BASE, 0, 128)
    msrc[:9, 64:80] = shift_index(LSIDE // 4, gp_col, GP_BASE, 64, 128)
    c["src_mom"] = msrc
    coord, cell = cell_vectors()
    rows = np.zeros((160, 128), np.float32)
    rows[:, 0:2] = coord.T
    rows[:, 2:4] = cell.T
    c["t_rows"] = rows
    cols = np.zeros((8, 9, 160), np.float32)
    for o, (ox, oy) in enumerate(OFFS):
        cols[0, o] = coord[0] + 2 * ox
        cols[1, o] = coord[1] + 2 * oy
        cols[2, o] = cell[0] + 2 * ox
        cols[3, o] = cell[1] + 2 * oy
    c["t_cols"] = cols.reshape(8, 1440)
    far_x = coord[0][:, None] - cols[0].reshape(1440)[None, :]
    far_y = coord[1][:, None] - cols[1].reshape(1440)[None, :]
    gap = np.maximum(
        np.abs(cell[0][:, None] - cols[2].reshape(1440)[None, :]),
        np.abs(cell[1][:, None] - cols[3].reshape(1440)[None, :]),
    )
    for name, scale in (("leaf", 1.0), ("par", 2.0)):
        sx, sy = far_x * scale, far_y * scale
        inv = np.where(gap > 1.5, 1.0 / (sx**2 + sy**2 + SOFTEN), 0.0)
        kx, ky = sx * inv, sy * inv
        full = np.concatenate([kx, ky, ky * ky - kx * kx, -2.0 * kx * ky]).astype(np.float32)
        c["hi_" + name] = full.astype(BF16)
        c["lo_" + name] = (full - c["hi_" + name].astype(np.float32)).astype(BF16)
    sides = np.zeros((8, HROWS), np.float32)
    for d, (dx, dy) in enumerate(DIRS):
        sides[0, ROW_OF[d] : ROW_OF[d] + ROWS_IN[d]] = dx
        sides[1, ROW_OF[d] : ROW_OF[d] + ROWS_IN[d]] = dy
    c["sides"] = sides
    return c


CONST = constants()


def split2(x):
    hi = x.astype(BF16)
    return hi, (x - hi.astype(F32)).astype(BF16)


def split3(x):
    hi = x.astype(BF16)
    rest = x - hi.astype(F32)
    mid = rest.astype(BF16)
    return hi, mid, (rest - mid.astype(F32)).astype(BF16)


def nt_dot(a, b):
    return lax.dot_general(a, b, (((1,), (1,)), ((), ())), preferred_element_type=F32)


def tn_none(a, b):
    return lax.dot_general(a, b, (((1,), (0,)), ((), ())), preferred_element_type=F32)


def morton_split(code, bits):
    cx, cy = 0, 0
    for level in range((bits + 1) // 2):
        cx = cx + code // 4**level % 2 * 2**level
        cy = cy + code // (2 * 4**level) % 2 * 2**level
    return cx, cy


def morton_join(cx, cy, bits):
    code = 0
    for level in range((bits + 1) // 2):
        code = code + cx // 2**level % 2 * 4**level
        code = code + cy // 2**level % 2 * 2 * 4**level
    return code


def whole_kernel(dev_count, bits, *refs):
    sources, refs = refs[:OPERANDS], refs[OPERANDS:]
    out, refs = refs[0], refs[1:]
    held, refs = refs[:OPERANDS], refs[OPERANDS:]
    (pos, mass, count, src_leaf, sel_leaf, sel_mom, up, t_rows, t_cols, sides, src_mom,
     down, hi_par, lo_par, hi_leaf, lo_leaf) = held
    arrive_sems = refs[0]
    arrivals = [
        pltpu.make_async_copy(src, dst, arrive_sems.at[i])
        for i, (src, dst) in enumerate(zip(sources, held))
    ]
    for i in (1, 2, 3, 0, *range(4, OPERANDS)):
        arrivals[i].start()
    run_kernel(dev_count, bits, arrivals, pos, mass, count, sel_leaf, sel_mom, up, down, sides,
               src_leaf, src_mom, t_rows, t_cols, hi_par, lo_par, hi_leaf, lo_leaf, out, *refs[1:])


def run_kernel(dev_count, bits, arrivals, pos, mass, count, sel_leaf, sel_mom, up, down, sides,
               src_leaf, src_mom, t_rows, t_cols, hi_par, lo_par, hi_leaf, lo_leaf, out, own, mom, send, recv, part, mid, leaf_mom, first,
                 second, su, sv, sw, lone, xs, xs_par, leaf_kind, leaf_local,
                 result, self_live, edge_s, edge_r, sum_s1, sum_r1, sum_s2, sum_r2):
    code = lax.axis_index("grp") * dev_count + lax.axis_index("dev")
    bx, by = morton_split(code, bits)
    nx, ny = 2 ** ((bits + 1) // 2), 2 ** (bits // 2)
    low_n = 2 ** (bits // 2)
    high_n = 2**bits // low_n
    low, high = code % low_n, code // low_n

    def device(c):
        return {"grp": c // dev_count, "dev": c % dev_count}

    def beside(dx, dy):
        return device(morton_join((bx + dx + nx) % nx, (by + dy + ny) % ny, bits))

    def in_low(k):
        return device(high * low_n + (low + k) % low_n)

    def in_high(k):
        return device((high + k) % high_n * low_n + low)

    barrier = pltpu.get_barrier_semaphore()

    def greet(who):
        pl.semaphore_signal(barrier, inc=1, device_id=who, device_id_type=pl.DeviceIdType.MESH)

    def greet_low(k, carry):
        greet(in_low(k))
        return carry

    def greet_high(k, carry):
        greet(in_high(k))
        return carry

    recv[64:HROWS, :] = jnp.zeros((HROWS - 64, LANES_OUT), F32)
    lax.fori_loop(1, low_n, greet_low, 0, unroll=True)
    for dx, dy in DIRS:
        greet(beside(dx, dy))
    lax.fori_loop(1, high_n, greet_high, 0, unroll=True)

    starts = [qx * 2 + qy * 4 + sy for sy in (0, 1) for qx in (0, 1) for qy in (0, 1)]

    def turned(ref, lead, step):
        rows = jnp.concatenate(
            [ref[pl.ds(lead + step * s, 16, stride=8 * step), :] for s in starts], axis=0
        )
        return rows.T

    for arrival in arrivals[1:4]:
        arrival.wait()
    row256 = lax.broadcasted_iota(jnp.int32, (256, 256), 0)
    pick = jnp.where(row256 == src_leaf[9:10, :], 1.0, 0.0).astype(BF16)
    linear = count[...].astype(F32).astype(BF16)
    counts = tn_none(linear[0:1], pick[0:128]) + tn_none(linear[1:2], pick[128:256])
    m_turned = turned(mass, 0, 1)
    slot = lax.broadcasted_iota(jnp.int32, (PPL, 128), 0).astype(F32)
    totals = []
    for tile in (0, 1):
        lanes = slice(tile * 128, tile * 128 + 128)
        live = slot < counts[:, lanes]
        vals = jnp.where(live, m_turned[tile * PPL : tile * PPL + PPL], 0.0)
        own[128:192, lanes] = vals
        totals.append(jnp.sum(vals, axis=0, keepdims=True))
    near_mean = jnp.sum(totals[0] + totals[1], axis=1, keepdims=True) / jnp.sum(
        counts, axis=1, keepdims=True
    )
    row = lax.broadcasted_iota(jnp.int32, (8, 128), 0)
    part[...] = jnp.where(
        row == 0,
        totals[0] + totals[1],
        jnp.where(row == 1, counts[:, 0:128] + counts[:, 128:256], 0.0),
    )

    def low_copy(k):
        return pltpu.make_async_remote_copy(
            src_ref=part, dst_ref=first.at[k], send_sem=sum_s1.at[k], recv_sem=sum_r1.at[k],
            device_id=in_low(k), device_id_type=pl.DeviceIdType.MESH,
        )

    def high_copy(k):
        return pltpu.make_async_remote_copy(
            src_ref=mid, dst_ref=second.at[k], send_sem=sum_s2.at[k], recv_sem=sum_r2.at[k],
            device_id=in_high(k), device_id_type=pl.DeviceIdType.MESH,
        )

    def start_low(k, carry):
        low_copy(k).start()
        return carry

    def start_high(k, carry):
        high_copy(k).start()
        return carry

    def add_low(k, acc):
        low_copy(k).wait()
        return acc + first[k]

    def add_high(k, acc):
        high_copy(k).wait()
        return acc + second[k]

    pl.semaphore_wait(barrier, 8 + low_n - 1 + high_n - 1)
    lax.fori_loop(1, low_n, start_low, 0, unroll=True)
    arrivals[0].wait()
    for k in (0, 1):
        vals = turned(pos, k, 2)
        own[k * PPL : (k + 1) * PPL, 0:128] = vals[:PPL]
        own[k * PPL : (k + 1) * PPL, 128:256] = vals[PPL:]

    for arrival in arrivals[4:12]:
        arrival.wait()
    leaf_mom[...] = jnp.zeros_like(leaf_mom)
    for tile in (0, 1):
        lanes = slice(tile * 128, tile * 128 + 128)
        bu = basis(own[0:64, lanes])
        bv = basis(own[64:128, lanes])
        m_t = own[128:192, lanes]
        live_t = jnp.where(m_t > 0.0, 1.0, 0.0)
        for kind, weight in enumerate((m_t, live_t)):
            for a in range(NODES):
                wa = bu[a] * weight
                for b in range(NODES):
                    leaf_mom[pl.ds(kind * NM + a * 6 + b, 1), lanes] = jnp.sum(
                        wa * bv[b], axis=0, keepdims=True
                    )
    mom[...] = jnp.zeros_like(mom)
    stacked = []
    for kind in (0, 1):
        block = jnp.concatenate(
            [
                leaf_mom[kind * NM : (kind + 1) * NM, ch * 64 : ch * 64 + 64]
                for ch in range(4)
            ],
            axis=0,
        )
        mom[kind * 160 : kind * 160 + 160, 0:64] = block
        stacked.append(block)
    par = jnp.dot(
        up[...], jnp.concatenate(stacked, axis=1), precision=HIGHEST, preferred_element_type=F32
    )
    for kind in (0, 1):
        for q in range(4):
            at = kind * 64 + q * 16
            mom[pl.ds(kind * 160 + q * NM, NM), 64:80] = par[:, at : at + 16]
    own_cut = split3(own[...])
    send[:, 0:192] = nt_dot(
        jnp.concatenate([sel_leaf[...]] * 3, axis=1), jnp.concatenate(own_cut, axis=1)
    )
    send[:, 192:512] = nt_dot(
        jnp.concatenate([sel_mom[...]] * 3, axis=1),
        jnp.concatenate(split3(mom[...]), axis=1),
    )
    edges = []
    for d, (dx, dy) in enumerate(DIRS):
        rows = pl.ds(ROW_OF[d], ROWS_SENT[d])
        copy = pltpu.make_async_remote_copy(
            src_ref=send.at[rows], dst_ref=recv.at[rows], send_sem=edge_s.at[d],
            recv_sem=edge_r.at[d], device_id=beside(-dx, -dy),
            device_id_type=pl.DeviceIdType.MESH,
        )
        copy.start()
        edges.append(copy)

    def at_offset(o):
        return slice(o * PPL, o * PPL + PPL)

    own_parts = jnp.concatenate(own_cut, axis=1)

    def shift_own(o):
        hot = jnp.where(row256 == src_leaf[o : o + 1, :], 1.0, 0.0).astype(BF16)
        moved = tn_none(own_parts, jnp.concatenate([hot] * 3, axis=0))
        for tile in (0, 1):
            lanes = slice(tile * 128, tile * 128 + 128)
            su[tile, at_offset(o), :] = moved[0:64, lanes]
            sv[tile, at_offset(o), :] = moved[64:128, lanes]
            sw[tile, at_offset(o), :] = moved[128:192, lanes]

    for o in range(NEIGHBOURS):
        shift_own(o)
    self_at = NEIGHBOURS * PPL
    for tile in (0, 1):
        lanes = slice(tile * 128, tile * 128 + 128)
        su[tile, self_at : self_at + PPL, :] = own[0:64, lanes] * 0.5
        sv[tile, self_at : self_at + PPL, :] = own[64:128, lanes] * 0.5
        m = own[128:192, lanes]
        sw[tile, self_at : self_at + PPL, :] = jnp.where(m > 0.0, m - near_mean, 0.0)
        lone[tile, 0:PPL, :] = jnp.where(m > 0.0, 1.0, 0.0)

    def near_field(first_row, row_count):
        width, unroll = 4, 16
        for tile in (0, 1):
            for piece in range(PPL // (8 * width)):
                base = piece * 8 * width
                tx, ty = targets(tile, base, width)

                def pairs(step, acc, tile=tile, tx=tx, ty=ty):
                    acc = list(acc)
                    for i in range(unroll):
                        at = pl.ds(first_row + step * unroll + i, 8, stride=0)
                        sx, sy, w = su[tile, at, :], sv[tile, at, :], sw[tile, at, :]
                        for t in range(width):
                            dx = tx[t] - sx
                            dy = ty[t] - sy
                            inv = 1.0 / (dy * dy + (dx * dx + SOFTEN))
                            kx = dx * inv
                            ky = dy * inv
                            wx = w * kx
                            wy = w * ky
                            acc[4 * t] = acc[4 * t] + wx
                            acc[4 * t + 1] = acc[4 * t + 1] + wy
                            acc[4 * t + 2] = (acc[4 * t + 2] + wy * ky) - wx * kx
                            acc[4 * t + 3] = acc[4 * t + 3] + wx * ky
                    return tuple(acc)

                acc = lax.fori_loop(0, row_count // unroll, pairs, (zero,) * (4 * width))
                for t in range(width):
                    rows = slice(tile * PPL + base + 8 * t, tile * PPL + base + 8 * t + 8)
                    for c in range(4):
                        near = acc[4 * t + c]
                        if c == 3:
                            near = near * -2.0
                        result[c, rows, :] = result[c, rows, :] + near

    zero = jnp.zeros((8, 128), F32)

    def targets(tile, base, width):
        lanes = slice(tile * 128, tile * 128 + 128)
        tx = [own[base + 8 * i : base + 8 * i + 8, lanes] * 0.5 for i in range(width)]
        ty = [own[64 + base + 8 * i : 72 + base + 8 * i, lanes] * 0.5 for i in range(width)]
        return tx, ty

    self_width = 2
    for tile in (0, 1):
        if tile == 1:
            mid[...] = lax.fori_loop(1, low_n, add_low, part[...], unroll=True)
            lax.fori_loop(1, high_n, start_high, 0, unroll=True)
        for piece in range(PPL // (8 * self_width)):
            base = piece * 8 * self_width
            tx, ty = targets(tile, base, self_width)

            def self_pairs(step, acc, tile=tile, tx=tx, ty=ty):
                acc = list(acc)
                for i in range(4):
                    k = step * 4 + i
                    at = pl.ds(self_at + k, 8, stride=0)
                    sx, sy, m = su[tile, at, :], sv[tile, at, :], sw[tile, at, :]
                    one = lone[tile, pl.ds(k, 8, stride=0), :]
                    for t in range(self_width):
                        dx = tx[t] - sx
                        dy = ty[t] - sy
                        x2 = dx * dx
                        y2 = dy * dy
                        inv = 1.0 / (x2 + y2 + SOFTEN)
                        gap = y2 - x2
                        cross = dx * dy
                        for kind, w in enumerate((m, one)):
                            at_acc = 8 * t + 4 * kind
                            w1 = w * inv
                            w2 = w1 * inv
                            acc[at_acc] = acc[at_acc] + w1 * dx
                            acc[at_acc + 1] = acc[at_acc + 1] + w1 * dy
                            acc[at_acc + 2] = acc[at_acc + 2] + w2 * gap
                            acc[at_acc + 3] = acc[at_acc + 3] + w2 * cross
                return tuple(acc)

            acc = lax.fori_loop(0, PPL // 4, self_pairs, (zero,) * (8 * self_width))
            for t in range(self_width):
                rows = slice(tile * PPL + base + 8 * t, tile * PPL + base + 8 * t + 8)
                for c in range(4):
                    scale = -2.0 if c == 3 else 1.0
                    result[c, rows, :] = acc[8 * t + c] * scale
                    self_live[c, rows, :] = acc[8 * t + 4 + c] * scale

    for copy in edges:
        copy.wait()
    cell_x = sides[0:1] + jnp.full((1, 128), bx, jnp.int32).astype(F32)
    cell_y = sides[1:2] + jnp.full((1, 128), by, jnp.int32).astype(F32)
    inside = jnp.where(
        (cell_x >= 0.0) & (cell_x < float(nx)) & (cell_y >= 0.0) & (cell_y < float(ny)), 1.0, 0.0
    )
    halo = recv[...].T * inside
    halo_parts = jnp.concatenate(split3(halo[0:192]), axis=1)
    row128 = lax.broadcasted_iota(jnp.int32, (128, 256), 0) + 256

    def shift_halo(o):
        hot = jnp.where(row128 == src_leaf[o : o + 1, :], 1.0, 0.0).astype(BF16)
        moved = tn_none(halo_parts, jnp.concatenate([hot] * 3, axis=0))
        off_x, off_y = OFFS[o]
        for tile in (0, 1):
            lanes = slice(tile * 128, tile * 128 + 128)
            at = at_offset(o)
            su[tile, at, :] = (su[tile, at, :] + moved[0:64, lanes]) * 0.5 + off_x
            sv[tile, at, :] = (sv[tile, at, :] + moved[64:128, lanes]) * 0.5 + off_y
            sw[tile, at, :] = sw[tile, at, :] + moved[128:192, lanes]

    for o in range(NEIGHBOURS):
        shift_halo(o)

    all_mom = jnp.concatenate([mom[...], halo[192:512]], axis=1)
    all_mom = jnp.concatenate(
        [all_mom[0:160] - near_mean * all_mom[160:320], all_mom[160:320]], axis=0
    )
    cut_mom = jnp.concatenate(split2(all_mom), axis=0)

    def shift_moments(o):
        hot = jnp.where(row256[:, 0:128] == src_mom[o : o + 1, :], 1.0, 0.0).astype(BF16)
        moved = tn_none(cut_mom, hot)
        at = slice(o * 160, o * 160 + 160)
        pieces = [moved[160 * i : 160 * i + 160] for i in range(4)]
        xs[at, :] = jnp.concatenate([p[:, 0:64] for p in pieces], axis=1).astype(BF16)
        xs_par[at, :] = jnp.concatenate([p[:, 64:80] for p in pieces], axis=1).astype(BF16)

    for o in range(9):
        shift_moments(o)

    for arrival in arrivals[12:]:
        arrival.wait()
    wide = tn_none(hi_par[...], xs_par[...])
    par = wide[:, 0:32] + wide[:, 32:64] + tn_none(lo_par[...], xs_par[:, 0:32])
    par_cols = jnp.concatenate(
        [
            par[c * 160 + q * NM : c * 160 + q * NM + NM, kind * 16 : kind * 16 + 16]
            for kind in (0, 1)
            for c in range(4)
            for q in range(4)
        ],
        axis=1,
    )
    from_par = jnp.dot(
        down[...], par_cols, precision=HIGHEST, preferred_element_type=F32
    )
    wide = tn_none(hi_leaf[...], xs[...])
    leaf = wide[:, 0:128] + wide[:, 128:256] + tn_none(lo_leaf[...], xs[:, 0:128])
    for kind in (0, 1):
        for c in range(4):
            at = kind * 256 + c * 64
            leaf_kind[kind, c] = jnp.concatenate(
                [
                    leaf[c * 160 + ch * NM : c * 160 + ch * NM + NM, kind * 64 : kind * 64 + 64]
                    + from_par[ch * NM : ch * NM + NM, at : at + 64]
                    for ch in range(4)
                ],
                axis=1,
            )

    sums = lax.fori_loop(1, high_n, add_high, mid[...], unroll=True)
    mass_sum = jnp.sum(sums[0:1], axis=1, keepdims=True)
    live_sum = jnp.sum(sums[1:2], axis=1, keepdims=True)
    mean = mass_sum / live_sum
    for tile in (0, 1):
        m = sw[tile, 0:self_at, :]
        sw[tile, 0:self_at, :] = jnp.where(m > 0.0, m - mean, 0.0)
    for c in range(4):
        leaf_local[c] = leaf_kind[0, c] - (mean - near_mean) * leaf_kind[1, c]

    for tile in (0, 1):
        lanes = slice(tile * 128, tile * 128 + 128)
        bu = basis(own[0:64, lanes])
        bv = basis(own[64:128, lanes])
        for c in range(4):
            rows = slice(tile * PPL, tile * PPL + PPL)
            acc = result[c, rows, :] - (mean - near_mean) * self_live[c, rows, :]
            for a in range(NODES):
                half = leaf_local[c, pl.ds(a * 6, 1), lanes] * bv[0]
                for b in range(1, NODES):
                    half = half + leaf_local[c, pl.ds(a * 6 + b, 1), lanes] * bv[b]
                acc = acc + half * bu[a]
            result[c, rows, :] = acc

    near_field(0, self_at)

    for c in range(4):
        back = result[c].T
        for i, s in enumerate(starts):
            out[pl.ds(s * 4 + c, 16, stride=32), :] = back[16 * i : 16 * i + 16]


def vmem():
    return pl.BlockSpec(memory_space=pltpu.VMEM)


NAMES = ("src_leaf", "sel_leaf", "sel_mom", "up", "t_rows", "t_cols", "sides", "src_mom", "down",
         "hi_par", "lo_par", "hi_leaf", "lo_leaf")
OPERANDS = 3 + len(NAMES)


def on_device(particle_pos, particle_mass, leaf_counts):
    dev_count = lax.axis_size("dev")
    bits = (lax.axis_size("grp") * dev_count).bit_length() - 1
    low_n = 2 ** (bits // 2)
    high_n = 2**bits // low_n
    pos = particle_pos.reshape(2, 128, 128).transpose(1, 0, 2).reshape(256, 128)
    mass = particle_mass.reshape(128, 128)
    count = leaf_counts.reshape(2, 128)
    operands = (pos, mass, count, *[jnp.asarray(CONST[k]) for k in NAMES])
    out = pl.pallas_call(
        functools.partial(whole_kernel, dev_count, bits),
        out_shape=jax.ShapeDtypeStruct((512, 128), F32),
        in_specs=[pl.BlockSpec(memory_space=pltpu.HBM)] * OPERANDS,
        out_specs=vmem(),
        scratch_shapes=[pltpu.VMEM(x.shape, x.dtype) for x in operands]
        + [
            pltpu.SemaphoreType.DMA((OPERANDS,)),
            pltpu.VMEM((192, 256), F32),
            pltpu.VMEM((320, 128), F32),
            pltpu.VMEM((HROWS, LANES_OUT), F32),
            pltpu.VMEM((HROWS, LANES_OUT), F32),
            pltpu.VMEM((8, 128), F32),
            pltpu.VMEM((8, 128), F32),
            pltpu.VMEM((2 * NM, 256), F32),
            pltpu.VMEM((low_n, 8, 128), F32),
            pltpu.VMEM((high_n, 8, 128), F32),
            pltpu.VMEM((2, 9 * PPL + 8, 128), F32),
            pltpu.VMEM((2, 9 * PPL + 8, 128), F32),
            pltpu.VMEM((2, 9 * PPL + 8, 128), F32),
            pltpu.VMEM((2, PPL + 8, 128), F32),
            pltpu.VMEM((1440, 256), BF16),
            pltpu.VMEM((1440, 64), BF16),
            pltpu.VMEM((2, 4, NM, 256), F32),
            pltpu.VMEM((4, NM, 256), F32),
            pltpu.VMEM((4, 128, 128), F32),
            pltpu.VMEM((4, 128, 128), F32),
            pltpu.SemaphoreType.DMA((8,)),
            pltpu.SemaphoreType.DMA((8,)),
            pltpu.SemaphoreType.DMA((low_n,)),
            pltpu.SemaphoreType.DMA((low_n,)),
            pltpu.SemaphoreType.DMA((high_n,)),
            pltpu.SemaphoreType.DMA((high_n,)),
        ],
        compiler_params=pltpu.CompilerParams(
            collective_id=0, has_side_effects=True, vmem_limit_bytes=63 * 2**20
        ),
        name="fields",
    )(*operands)
    return out.reshape(128, 4, 128).transpose(1, 0, 2).reshape(4, LSIDE * LSIDE * PPL)


def solution(mesh):
    in_specs = (P(None, ("grp", "dev")), P(("grp", "dev")), P(("grp", "dev")))
    out_specs = P(None, ("grp", "dev"))
    return jax.shard_map(
        on_device, mesh=mesh, in_specs=in_specs, out_specs=out_specs, check_vma=False
    )
```
